32 devices in a mesh: wide: 16 (over z, y, x), narrow: 2 (over core).
Axes of the slice: x: 2, y: 2, z: 4, core: 2. Of those that a mesh axis runs over, the one named last changes fastest.
Arguments:
- tokens: bfloat16 [36864, 512], P('wide'), may hold values from -6 to 6
- attn_gain: float32 [512], replicated, may hold values from 0.25 to 1.75
- attn_shift: float32 [512], replicated, may hold values from -3 to 3
- qkv_weight: bfloat16 [512, 3, 512], P(None, None, 'narrow'), may hold values from -0.25 to 0.25
- query_value_bias: float32 [2, 512], P(None, 'narrow'), may hold values from -3 to 3
- proj_weight: bfloat16 [512, 512], P('narrow'), may hold values from -2 to 2
- proj_bias: float32 [512], replicated, may hold values from -3 to 3
- moe_gain: float32 [512], replicated, may hold values from 0.25 to 1.75
- moe_shift: float32 [512], replicated, may hold values from -3 to 3
- router_weight: bfloat16 [512, 16], replicated, may hold values from -0.25 to 0.25
- expert_up: bfloat16 [16, 512, 2048], P('wide', None, 'narrow'), may hold values from -0.25 to 0.25
- expert_up_bias: float32 [16, 2048], P('wide', 'narrow'), may hold values from -3 to 3
- expert_down: bfloat16 [16, 2048, 512], P('wide', 'narrow'), may hold values from -4 to 4
- expert_down_bias: float32 [16, 512], P('wide'), may hold values from -48 to 48
- routes: int32 [36864, 2], P('wide'), may hold values from 0 to 15, as said below
- slot_index: int32 [36864, 2], P('wide'), may hold values from 0 to 144, as said below
- cotangent: bfloat16 [36864, 512], P('wide'), may hold values from -6 to 6
Outputs:
- output: bfloat16 [36864, 512], P('wide')
- grad_tokens: float32 [36864, 512], P('wide')
- grad_attn_gain: float32 [512], replicated
- grad_attn_shift: float32 [512], replicated
- grad_qkv: float32 [512, 3, 512], P(None, None, 'narrow')
- grad_query_value_bias: float32 [2, 512], P(None, 'narrow')
- grad_proj: float32 [512, 512], P('narrow')
- grad_proj_bias: float32 [512], replicated
- grad_moe_gain: float32 [512], replicated
- grad_moe_shift: float32 [512], replicated
- grad_router: float32 [512, 16], replicated
- grad_expert_up: float32 [16, 512, 2048], P('wide', None, 'narrow')
- grad_expert_up_bias: float32 [16, 2048], P('wide', 'narrow')
- grad_expert_down: float32 [16, 2048, 512], P('wide', 'narrow')
- grad_expert_down_bias: float32 [16, 512], P('wide')
The draws below stay inside these ranges and needn't reach their ends.
Inputs may be any that keep to these rules, and one draw needn't show every extreme that they name: `routes`: each token names two different experts, its first and its second choice. `slot_index`: in each routing group of 2304 tokens the kept pairs of one expert hold slots 0, 1, 2, ... without gaps or repeats, all first choices before any second choice, each in one priority order of the group's tokens; the value 144 marks a dropped pair.
All inputs are finite; a program needn't handle non-finite values.
Results may differ from the reference program's by a relative error of at most 0.02.
Values may be sent and summed in bfloat16 or wider, within the bound.
A program may use at most 192 MiB of HBM per device.

```python
import jax
import jax.numpy as jnp
from jax import lax

D = 512
HEADS = 8
FF = 2048
PATCHES = 144
HEAD_DIM = 64
TOK_DEV = 2304
EXPERT_COUNT = 16
CAP = 144
TOKENS = 36864


def route_table(key):
    groups = TOKENS // TOK_DEV
    expert_choice_index = jnp.arange(EXPERT_COUNT, dtype=jnp.int32)
    priority_boost = jax.random.permutation(jax.random.fold_in(key, 11), EXPERT_COUNT).astype(jnp.int32) * (1 << 13)
    router_jitter = jax.random.randint(jax.random.fold_in(key, 12), (TOKENS, EXPERT_COUNT), 0, 1 << 19, dtype=jnp.int32)
    expert_score_matrix = (router_jitter + priority_boost[None, :]) * EXPERT_COUNT + expert_choice_index[None, :]
    highest_expert_scores, chosen = lax.top_k(expert_score_matrix, 2)
    routes = chosen.astype(jnp.int32)
    priority = jax.random.randint(jax.random.fold_in(key, 13), (groups, TOK_DEV), 0, 1 << 18, dtype=jnp.int32)
    priority = priority * TOK_DEV + jnp.arange(TOK_DEV, dtype=jnp.int32)[None, :]
    order = jnp.argsort(priority, axis=1).astype(jnp.int32)
    inverse_permutation = jnp.argsort(order, axis=1).astype(jnp.int32)
    grouped = routes.reshape(groups, TOK_DEV, 2)
    sorted_routes = jnp.take_along_axis(grouped, order[:, :, None], axis=1)
    first_hot = (sorted_routes[:, :, 0:1] == expert_choice_index[None, None, :]).astype(jnp.int32)
    second_hot = (sorted_routes[:, :, 1:2] == expert_choice_index[None, None, :]).astype(jnp.int32)
    first_before = jnp.cumsum(first_hot, axis=1) - first_hot
    second_before = jnp.cumsum(second_hot, axis=1) - second_hot
    first_total = jnp.sum(first_hot, axis=1)
    first_slot = jnp.sum(first_before * first_hot, axis=-1)
    second_slot = jnp.sum((second_before + first_total[:, None, :]) * second_hot, axis=-1)
    first_slot = jnp.take_along_axis(first_slot, inverse_permutation, axis=1)
    second_slot = jnp.take_along_axis(second_slot, inverse_permutation, axis=1)
    slot_table = jnp.minimum(jnp.stack([first_slot, second_slot], axis=-1), CAP).reshape(TOKENS, 2)
    return (routes, slot_table.astype(jnp.int32))


def draw_routes(key, part):
    return route_table(key)[0]


def draw_slot_index(key, part):
    return route_table(key)[1]


def shard_levels(rng, dims, split, least, largest):
    factor_of = 1.0
    for dim, parts in split:
        heights = jax.random.uniform(jax.random.fold_in(jax.random.fold_in(rng, 6), dim), (parts,), jnp.float32, least / len(split), largest / len(split))
        factor_of = factor_of * jnp.repeat(jnp.exp(heights), dims[dim] // parts).reshape((-1,) + (1,) * (len(dims) - 1 - dim))
    return factor_of


def centred(rng, dims, scale, reach, cuts=(), kind=jnp.bfloat16):
    loudness = shard_levels(rng, dims, cuts, -0.22, 0.18) if cuts else 1.0
    entries = jax.random.normal(rng, dims, jnp.float32) * scale * loudness
    return jnp.minimum(jnp.maximum(entries, -reach), reach).astype(kind)


def setup_inputs(seed: int = 0) -> dict:
    key_of = jax.random.split(jax.random.key(seed), 18)
    tokens = centred(key_of[0], (TOKENS, D), 1.0, 6.0, ((0, 16),))
    attn_gain = jnp.clip(1.0 + 0.15 * jax.random.normal(key_of[1], (D,), jnp.float32), 0.25, 1.75)
    attn_shift = centred(key_of[2], (D,), 0.5, 3.0, (), jnp.float32)
    qkv_weight = centred(key_of[3], (D, 3, D), D ** -0.5, 0.25, ((2, 2),))
    query_value_bias = centred(key_of[4], (2, D), 0.5, 3.0, ((1, 2),), jnp.float32)
    proj_weight = centred(key_of[5], (D, D), (max(D // 64, 1)) ** -0.5, 2.0, ((0, 2),))
    proj_bias = centred(key_of[6], (D,), 0.5, 3.0, (), jnp.float32)
    moe_gain = jnp.clip(1.0 + 0.15 * jax.random.normal(key_of[7], (D,), jnp.float32), 0.25, 1.75)
    moe_shift = centred(key_of[8], (D,), 0.5, 3.0, (), jnp.float32)
    router_weight = centred(key_of[9], (D, EXPERT_COUNT), D ** -0.5, 0.25)
    expert_up = centred(key_of[10], (EXPERT_COUNT, D, FF), D ** -0.5, 0.25, ((0, 16), (2, 2)))
    expert_up_bias = centred(key_of[11], (EXPERT_COUNT, FF), 0.5, 3.0, ((0, 16), (1, 2)), jnp.float32)
    expert_down = centred(key_of[12], (EXPERT_COUNT, FF, D), (max(FF // 1024, 1)) ** -0.5, 4.0, ((0, 16), (1, 2)))
    expert_down_bias = centred(key_of[13], (EXPERT_COUNT, D), 8.0, 48.0, ((0, 16),), jnp.float32)
    routes = draw_routes(jax.random.fold_in(key_of[17], 71), 0)
    slot_index = draw_slot_index(jax.random.fold_in(key_of[17], 71), 0)
    cotangent = centred(key_of[16], (TOKENS, D), 1.0, 6.0, ((0, 16),))
    return dict(tokens=tokens, attn_gain=attn_gain, attn_shift=attn_shift, qkv_weight=qkv_weight, query_value_bias=query_value_bias, proj_weight=proj_weight, proj_bias=proj_bias, moe_gain=moe_gain, moe_shift=moe_shift, router_weight=router_weight, expert_up=expert_up, expert_up_bias=expert_up_bias, expert_down=expert_down, expert_down_bias=expert_down_bias, routes=routes, slot_index=slot_index, cotangent=cotangent)


EPSILON = 1e-06
HIGH = lax.Precision.HIGHEST

@jax.custom_vjp
def low(v):
    return lax.optimization_barrier(v.astype(jnp.bfloat16)).astype(jnp.float32)

@jax.custom_vjp
def low_back(v):
    return v

def low_keep(v):
    return (low(v), None)

def low_pass(kept, grad):
    return (grad,)

def back_keep(v):
    return (v, None)

def back_low(kept, grad):
    return (low(grad),)
low.defvjp(low_keep, low_pass)
low_back.defvjp(back_keep, back_low)

def layer_norm(values, norm_gain, norm_shift):
    center = values - lax.optimization_barrier(jnp.mean(values, axis=-1, keepdims=True))
    inv_root = lax.rsqrt(lax.optimization_barrier(jnp.mean(center * center, axis=-1, keepdims=True)) + EPSILON)
    return center * inv_root * norm_gain + norm_shift

def forward(tokens, attn_gain, attn_shift, qkv_weight, query_value_bias, proj_weight, proj_bias, moe_gain, moe_shift, router_weight, expert_up, expert_up_bias, expert_down, expert_down_bias, routes, slot_index):
    groups = TOKENS // TOK_DEV
    images = TOKENS // PATCHES
    scale_factor = HEAD_DIM ** (-0.5)
    attn_in = low(layer_norm(tokens, attn_gain, attn_shift))
    projected = jnp.einsum('td,dcf->tcf', attn_in, qkv_weight, precision=HIGH)
    queries = low(low_back(projected[:, 0] + query_value_bias[0]))
    key_rows = low(low_back(projected[:, 1]))
    value_rows = low(low_back(projected[:, 2] + query_value_bias[1]))

    def by_heads(matrix):
        return matrix.reshape(images, PATCHES, HEADS, HEAD_DIM)
    scores = low_back(jnp.einsum('iphe,iqhe->ihpq', by_heads(queries), by_heads(key_rows), precision=HIGH) * scale_factor)
    probs_low = low(jax.nn.softmax(scores, axis=-1))
    attended = jnp.einsum('ihpq,iqhe->iphe', probs_low, by_heads(value_rows), precision=HIGH).reshape(TOKENS, D)
    attended = low(low_back(attended))
    attn_out = low_back(jnp.dot(attended, proj_weight, precision=HIGH) + proj_bias)
    residual = tokens + attn_out
    moe_in = low(layer_norm(residual, moe_gain, moe_shift))
    logits = low_back(jnp.dot(moe_in, router_weight, precision=HIGH))
    router_probs = jax.nn.softmax(logits, axis=-1)
    kept_pair = slot_index < CAP
    chosen = jnp.take_along_axis(router_probs, routes, axis=1)
    gate_values = jnp.where(kept_pair, chosen, 0.0)
    slot_place = routes * CAP + slot_index
    place_hot = ((slot_place[:, :, None] == jnp.arange(TOK_DEV, dtype=jnp.int32)[None, None, :]) & kept_pair[:, :, None]).astype(jnp.float32)
    place_hot = place_hot.reshape(groups, TOK_DEV, 2, TOK_DEV)
    gathered = jnp.einsum('gtks,gtd->gsd', place_hot, moe_in.reshape(groups, TOK_DEV, D), precision=HIGH)
    expert_rows = gathered.reshape(groups, EXPERT_COUNT, CAP, D).transpose(1, 0, 2, 3).reshape(EXPERT_COUNT, groups * CAP, D)
    expert_rows = low_back(expert_rows)
    pre_act = low_back(jnp.einsum('erd,edf->erf', expert_rows, expert_up, precision=HIGH) + expert_up_bias[:, None, :])
    hidden = low(jax.nn.gelu(pre_act))
    expert_out = jnp.einsum('erf,efd->erd', hidden, expert_down, precision=HIGH) + expert_down_bias[:, None, :]
    expert_out = low(low_back(expert_out))
    back_rows = expert_out.reshape(EXPERT_COUNT, groups, CAP, D).transpose(1, 0, 2, 3).reshape(groups, TOK_DEV, D)
    picked = jnp.einsum('gtks,gsd->gtkd', place_hot, back_rows, precision=HIGH).reshape(TOKENS, 2, D)
    mixture = lax.optimization_barrier(jnp.sum(gate_values[:, :, None] * picked, axis=1))
    return residual + mixture

def reference(tokens, attn_gain, attn_shift, qkv_weight, query_value_bias, proj_weight, proj_bias, moe_gain, moe_shift, router_weight, expert_up, expert_up_bias, expert_down, expert_down_bias, routes, slot_index, cotangent):

    def run(*params):
        return forward(*params, routes, slot_index)
    floats = (tokens.astype(jnp.float32), attn_gain, attn_shift, qkv_weight.astype(jnp.float32), query_value_bias, proj_weight.astype(jnp.float32), proj_bias, moe_gain, moe_shift, router_weight.astype(jnp.float32), expert_up.astype(jnp.float32), expert_up_bias, expert_down.astype(jnp.float32), expert_down_bias)
    result, pull = jax.vjp(run, *floats)
    grads = pull(cotangent.astype(jnp.float32))
    return (result.astype(jnp.bfloat16), grads[0], grads[1], grads[2], grads[3], grads[4], grads[5], grads[6], grads[7], grads[8], grads[9], grads[10], grads[11], grads[12], grads[13])
```

```python
import functools

import jax
import jax.numpy as jnp
from jax import lax
from jax.experimental import pallas as pl
from jax.experimental.pallas import tpu as pltpu
from jax.sharding import PartitionSpec as P

PATCHES = 144
HEAD_DIM = 64
EPSILON = 1e-06
MESH = pl.DeviceIdType.MESH
BF = jnp.bfloat16
F32 = jnp.float32
GELU_C = 0.7978845608028654
GELU_A = 0.044715


def dot(a, b):
    return jnp.dot(a, b, preferred_element_type=F32)


def dot_nt(a, b):
    return lax.dot_general(a, b, (((1,), (1,)), ((), ())), preferred_element_type=F32)


def dot_tn(a, b):
    return lax.dot_general(a, b, (((0,), (0,)), ((), ())), preferred_element_type=F32)


def norm_parts(values):
    center = values - jnp.mean(values, axis=-1, keepdims=True)
    inv_root = lax.rsqrt(jnp.mean(center * center, axis=-1, keepdims=True) + EPSILON)
    return center * inv_root, inv_root


def norm_pull(upstream, normed, inv_root, norm_gain):
    scaled = upstream * norm_gain
    bracket = (
        scaled
        - jnp.mean(scaled, axis=-1, keepdims=True)
        - normed * jnp.mean(scaled * normed, axis=-1, keepdims=True)
    )
    return inv_root * bracket


class Sizes:
    def __init__(self, wide, narrow, tokens, width, experts, local_ff):
        self.W, self.N = wide, narrow
        self.T, self.D, self.E = tokens, width, experts
        self.TL = tokens // narrow
        self.cap = tokens // experts
        self.PW = wide // narrow
        self.Rb = -(-self.cap // 16) * 16
        self.L = width // narrow
        self.FL = local_ff
        self.CH = 2 * PATCHES
        self.NCH = self.TL // self.CH
        self.IMG = self.CH // PATCHES
        self.HP = width // (2 * HEAD_DIM)
        self.EC = 2
        self.ROWS = self.PW * self.Rb
        self.RC = self.ROWS // 4 if self.ROWS % 64 == 0 and self.ROWS >= 1024 else self.ROWS
        self.FC = min(512, local_ff)
        self.GR = 4 * width
        self.PR = self.GR // wide
        self.RP = -(-(experts + 7) // 8) * 8


def place():
    return lax.axis_index("wide"), lax.axis_index("narrow")


def signal(sem, wide, narrow):
    pl.semaphore_signal(sem, 1, device_id=(wide, narrow), device_id_type=MESH)


def remote(src, dst, send, recv, wide, narrow):
    return pltpu.make_async_remote_copy(
        src, dst, send, recv, device_id=(wide, narrow), device_id_type=MESH
    )


class Swap:
    def __init__(self, s, src, dst, send, recv, local, half=False):
        self.s, self.src = s, src
        self.send, self.recv, self.local = send, recv, local
        w, h = place()
        self.w, self.h = w, h
        self.far = w // s.PW
        self.slot = lax.rem(w, s.PW)
        self.dst = dst.at[self.far] if half else dst
        self.land = dst.at[h] if half else dst

    def own(self, i):
        return jnp.logical_and(self.far == self.h, self.h * self.s.PW + i == self.w)

    def copy(self, i, slot):
        return remote(
            self.src.at[i],
            self.dst.at[self.slot],
            self.send.at[i],
            self.recv.at[slot],
            self.h * self.s.PW + i,
            self.far,
        )

    def start(self, i):
        @pl.when(jnp.logical_not(self.own(i)))
        def _():
            self.copy(i, self.slot).start()

        @pl.when(self.own(i))
        def _():
            pltpu.make_async_copy(self.src.at[i], self.dst.at[self.slot], self.local).start()

    def wait_send(self, i):
        @pl.when(jnp.logical_not(self.own(i)))
        def _():
            self.copy(i, self.slot).wait_send()

    def wait_recv(self, i):
        @pl.when(jnp.logical_not(self.own(i)))
        def _():
            remote(
                self.src.at[i],
                self.land.at[i],
                self.send.at[i],
                self.recv.at[i],
                self.h * self.s.PW + i,
                self.far,
            ).wait_recv()

        @pl.when(self.own(i))
        def _():
            pltpu.make_async_copy(self.src.at[i], self.land.at[i], self.local).wait()


def greet_swap(s, barrier):
    w, h = place()
    far = w // s.PW

    @pl.loop(0, s.PW)
    def _(i):
        @pl.when(jnp.logical_or(far != h, h * s.PW + i != w))
        def _():
            signal(barrier, h * s.PW + i, far)

    for j in range(1, s.N):
        signal(barrier, w, lax.rem(h + j, s.N))


def await_swap(s, barrier):
    w, h = place()
    pl.semaphore_wait(barrier, s.PW + s.N - 1 - (w // s.PW == h).astype(jnp.int32))


def front_kernel(s, *refs):
    (
        tok, dy, g1, b1, wq_loc, qvb_loc, wp_loc, pb, g2, b2, prow, up_loc, dn_loc, ub_loc,
        x_out, dy_out, wq_out, wp_out, up_all, dn_all, ub_all, q_out, k_out, v_out, p_out, att_out,
        ain_out, res_out,
        tokv, wq, wp, qvb, hot, moe, qs, ks, vs, ps, atts, ains, ress, snd_x, snd_dy,
        w_send, w_recv, own_sem, m_send, m_recv, x_send, x_recv, d_send, d_recv, l_sem, out_sem, tok_sem,
    ) = refs
    w, h = place()
    N, TL, CH, L = s.N, s.TL, s.CH, s.L
    barrier = pltpu.get_barrier_semaphore()
    greet_swap(s, barrier)
    load_tok = pltpu.make_async_copy(tok.at[pl.ds(pl.multiple_of(h * TL, 16), TL)], tokv, tok_sem)
    load_tok.start()
    pairs = ((wq_loc, wq), (wp_loc, wp), (qvb_loc, qvb), (up_loc, up_all), (dn_loc, dn_all), (ub_loc, ub_all))
    owns = [pltpu.make_async_copy(a, b.at[h], own_sem.at[i]) for i, (a, b) in enumerate(pairs)]
    for copy in owns:
        copy.start()
    await_swap(s, barrier)

    def weight_copy(i, j):
        a, b = pairs[i]
        return remote(a, b.at[h], w_send.at[i, j], w_recv.at[i, j], w, lax.rem(h + j, N))

    for i in range(len(pairs)):
        for j in range(1, N):
            weight_copy(i, j).start()

    swap_d = Swap(s, snd_dy, dy_out, d_send, d_recv, l_sem.at[0])
    swap_x = Swap(s, snd_x, x_out, x_send, x_recv, l_sem.at[1])

    @pl.loop(0, s.PW // s.EC)
    def _(c):
        for k in range(s.EC):
            i = c * s.EC + k
            row = lax.broadcasted_iota(jnp.int32, (s.Rb, 1), 0)
            value = jnp.where(row < s.cap, (h * s.PW + i) * s.cap + row, -2)
            hit = jnp.logical_or(prow[0:1, :] == value, prow[1:2, :] == value)
            hot[pl.ds(pl.multiple_of(i * s.Rb, 16), s.Rb), :] = jnp.where(hit, 1.0, 0.0).astype(BF)
        rows = pl.ds(pl.multiple_of(c * s.EC * s.Rb, 16), s.EC * s.Rb)
        got = dot(hot[rows, :], dy[...]).astype(BF)
        for k in range(s.EC):
            snd_dy[c * s.EC + k] = got[k * s.Rb : (k + 1) * s.Rb]
            swap_d.start(c * s.EC + k)

    load_tok.wait()
    for copy in owns[:3]:
        copy.wait()
    for i in range(3):
        for j in range(1, N):
            weight_copy(i, j).wait_recv()

    def moe_copy(c, j):
        part = moe.at[pl.ds(pl.multiple_of(h * TL + c * CH, 16), CH)]
        return remote(part, part, m_send.at[c, j], m_recv.at[c, j], w, lax.rem(h + j, N))

    lane = lax.broadcasted_iota(jnp.int32, (PATCHES, 2 * HEAD_DIM), 1)
    first = lane < HEAD_DIM

    @pl.loop(0, s.NCH)
    def _(c):
        rows = pl.ds(pl.multiple_of(c * CH, 16), CH)
        t = tokv[rows, :].astype(F32)
        normed, _r = norm_parts(t)
        ain = (normed * g1[...] + b1[...]).astype(BF)
        ains[rows, :] = ain
        for j in range(N):
            cols = slice(j * L, (j + 1) * L)
            q = (dot(ain, wq[j, 0]) + qvb[j, 0:1, :]).astype(BF)
            qs[rows, cols] = q * BF(HEAD_DIM ** (-0.5))
            ks[rows, cols] = dot(ain, wq[j, 1]).astype(BF)
            vs[rows, cols] = (dot(ain, wq[j, 2]) + qvb[j, 1:2, :]).astype(BF)
        for m in range(s.IMG):
            image = pl.ds(pl.multiple_of(c * CH + m * PATCHES, 16), PATCHES)
            for p in range(s.HP):
                cols = slice(2 * HEAD_DIM * p, 2 * HEAD_DIM * (p + 1))
                q = qs[image, cols]
                zero = jnp.zeros_like(q)
                both = jnp.concatenate([jnp.where(first, q, zero), jnp.where(first, zero, q)], axis=0)
                scores = dot_nt(both, ks[image, cols])
                top = jnp.max(scores, axis=-1, keepdims=True)
                grown = jnp.exp(scores - top)
                probs = (grown * (1.0 / jnp.sum(grown, axis=-1, keepdims=True))).astype(BF)
                ps[(c * s.IMG + m) * s.HP + p] = probs
                mixed = dot(probs, vs[image, cols])
                atts[image, cols] = jnp.where(first, mixed[:PATCHES], mixed[PATCHES:]).astype(BF)
        wpf = wp[...].reshape(s.D, s.D)
        residual = t + (dot(atts[rows, :], wpf) + pb[...])
        ress[rows, :] = residual
        normed, _r = norm_parts(residual)
        moe[pl.ds(pl.multiple_of(h * TL + c * CH, 16), CH), :] = (normed * g2[...] + b2[...]).astype(BF)
        for j in range(1, N):
            moe_copy(c, j).start()

    saves = (
        (wq, wq_out), (wp, wp_out), (qs, q_out), (ks, k_out), (vs, v_out), (ps, p_out), (atts, att_out),
        (ains, ain_out), (ress, res_out),
    )
    outs = [pltpu.make_async_copy(a, b, out_sem.at[i]) for i, (a, b) in enumerate(saves)]
    for copy in outs:
        copy.start()

    @pl.loop(0, s.NCH)
    def _(c):
        for j in range(1, N):
            moe_copy(c, j).wait_recv()

    @pl.loop(0, s.PW // s.EC)
    def _(c):
        rows = pl.ds(pl.multiple_of(c * s.EC * s.Rb, 16), s.EC * s.Rb)
        got = dot(hot[rows, :], moe[...]).astype(BF)
        for k in range(s.EC):
            snd_x[c * s.EC + k] = got[k * s.Rb : (k + 1) * s.Rb]
            swap_x.start(c * s.EC + k)

    for copy in owns[3:]:
        copy.wait()
    for i in range(len(pairs)):
        for j in range(1, N):
            if i >= 3:
                weight_copy(i, j).wait_recv()
            weight_copy(i, j).wait_send()

    @pl.loop(0, s.NCH)
    def _(c):
        for j in range(1, N):
            moe_copy(c, j).wait_send()

    for copy in outs:
        copy.wait()

    @pl.loop(0, s.PW)
    def _(i):
        swap_d.wait_send(i)
        swap_d.wait_recv(i)

    @pl.loop(0, s.PW)
    def _(i):
        swap_x.wait_send(i)
        swap_x.wait_recv(i)


def expert_kernel(s, *refs):
    (
        x, dyr, up, dn, ub, db, wr,
        rg_all, z_out, gu_out, gd_out, gub_out, gdb_out, grt_out,
        og, hid, pg, ysum, rsum, rg_snd, us, ds_, ur, dr, bs, br,
        r_send, r_recv, l_sem, f_send, f_recv, n_send, n_recv,
    ) = refs
    w, h = place()
    N, RC, FC, FL, D = s.N, s.RC, s.FC, s.FL, s.D
    barrier = pltpu.get_barrier_semaphore()
    greet_swap(s, barrier)
    lane = lax.broadcasted_iota(jnp.int32, (RC, 128), 1)

    def router(rows):
        logits = dot(x[rows, :], wr[...])
        logits = jnp.where(lane < s.E, logits, -jnp.inf)
        top = jnp.max(logits, axis=-1, keepdims=True)
        grown = jnp.exp(logits - top)
        probs = grown * (1.0 / jnp.sum(grown, axis=-1, keepdims=True))
        gate = jnp.sum(jnp.where(lane == w, probs, 0.0), axis=-1, keepdims=True)
        return probs, gate

    def row_chunk(r):
        return pl.ds(pl.multiple_of(r * RC, 16), RC)

    @pl.loop(0, s.ROWS // RC)
    def _(r):
        rows = row_chunk(r)
        _p, gate = router(rows)
        og[rows, :] = (gate * dyr[rows, :].astype(F32)).astype(BF)
        ysum[rows, :] = jnp.broadcast_to(db[...], (RC, D))
        rsum[rows, :] = jnp.zeros((RC, D), F32)

    per = FL // FC

    @pl.loop(0, N * per)
    def _(f):
        j = f // per
        off = pl.ds(pl.multiple_of(lax.rem(f, per) * FC, 128), FC)

        @pl.loop(0, s.ROWS // RC)
        def _(r):
            rows = row_chunk(r)
            pre = dot(x[rows, :], up[j, :, off]) + ub[j, :, off]
            square = pre * pre
            t = jnp.tanh(GELU_C * (pre + GELU_A * (square * pre)))
            half = 0.5 * (1.0 + t)
            hidden = (pre * half).astype(BF)
            slope = half + (0.5 * GELU_C) * pre * (1.0 - t * t) * (1.0 + (3.0 * GELU_A) * square)
            grad = (dot_nt(og[rows, :], dn[j, off, :]) * slope).astype(BF)
            hid[f, rows, :] = hidden
            pg[f, rows, :] = grad
            ysum[rows, :] += dot(hidden, dn[j, off, :])
            rsum[rows, :] += dot_nt(grad, up[j, :, off])

    await_swap(s, barrier)
    swap_r = Swap(s, rg_snd, rg_all, r_send, r_recv, l_sem, True)
    per_block = RC // s.Rb if RC % s.Rb == 0 else 1
    grt_out[...] = jnp.zeros(grt_out.shape, F32)

    @pl.loop(0, s.ROWS // RC)
    def _(r):
        rows = row_chunk(r)
        probs, gate = router(rows)
        y = ysum[rows, :].astype(BF).astype(F32)
        gate_grad = jnp.sum(dyr[rows, :].astype(F32) * y, axis=-1, keepdims=True)
        z_out[rows, :] = (gate * y).astype(BF)
        logit = (gate_grad * probs * (jnp.where(lane == w, 1.0, 0.0) - gate)).astype(BF)
        back = (rsum[rows, :] + dot_nt(logit, wr[...])).astype(BF)
        grt_out[...] += dot_tn(logit, x[rows, :])
        for k in range(per_block):
            rg_snd[r * per_block + k] = back[k * s.Rb : (k + 1) * s.Rb]
            swap_r.start(r * per_block + k)

    def n_copy(i, j):
        a, b = ((us, ur), (ds_, dr), (bs, br))[i]
        return remote(a.at[j], b.at[h], n_send.at[i, j], n_recv.at[i, j], w, lax.rem(h + j, N))

    def up_part(owner, c):
        return dot_tn(x[...], pg[owner * per + c])

    def down_part(owner, c):
        return dot_tn(hid[owner * per + c], og[...])

    og_sum = jnp.sum(og[...].astype(F32), axis=0, keepdims=True)
    for j in range(1, N):
        owner = lax.rem(h + j, N)
        for c in range(per):
            us[j, :, c * FC : (c + 1) * FC] = up_part(owner, c).astype(BF)
            ds_[j, c * FC : (c + 1) * FC, :] = down_part(owner, c).astype(BF)
            bs[j, 0:1, c * FC : (c + 1) * FC] = jnp.sum(
                pg[owner * per + c].astype(F32), axis=0, keepdims=True
            )
        bs[j, 1:2, :] = jnp.concatenate([og_sum] * max(1, FL // D), axis=1)[:, :FL]
        if FL < D:
            for b in range(1, D // FL):
                bs[j, 1 + b : 2 + b, :] = og_sum[:, b * FL : (b + 1) * FL]
        for i in range(3):
            n_copy(i, j).start()
    for c in range(per):
        gu_out[:, c * FC : (c + 1) * FC] = up_part(h, c)
        gd_out[c * FC : (c + 1) * FC, :] = down_part(h, c)
        gub_out[:, c * FC : (c + 1) * FC] = jnp.sum(pg[h * per + c].astype(F32), axis=0, keepdims=True)
    br[h, 1:2, :] = jnp.concatenate([og_sum] * max(1, FL // D), axis=1)[:, :FL]
    if FL < D:
        for b in range(1, D // FL):
            br[h, 1 + b : 2 + b, :] = og_sum[:, b * FL : (b + 1) * FL]

    for j in range(1, N):
        for i in range(3):
            n_copy(i, j).wait_send()
    for j in range(1, N):
        src = lax.rem(h + N - j, N)
        for i in range(3):
            a, b = ((us, ur), (ds_, dr), (bs, br))[i]
            remote(a.at[j], b.at[src], n_send.at[i, j], n_recv.at[i, j], w, src).wait_recv()
        gu_out[...] += ur[src].astype(F32)
        gd_out[...] += dr[src].astype(F32)
        gub_out[...] += br[src, 0:1, :]
    if FL >= D:
        gdb_out[...] = sum(br[j, 1:2, :D] for j in range(N))
    else:
        for b in range(D // FL):
            gdb_out[:, b * FL : (b + 1) * FL] = sum(br[j, 1 + b : 2 + b, :] for j in range(N))

    def forward(i, j):
        part = rg_all.at[h, i]
        return remote(part, part, f_send.at[i, j], f_recv.at[i, j], w, lax.rem(h + j, N))

    @pl.loop(0, s.PW)
    def _(i):
        swap_r.wait_recv(i)
        for j in range(1, N):
            forward(i, j).start()

    @pl.loop(0, s.PW)
    def _(i):
        swap_r.wait_send(i)
        for j in range(1, N):
            forward(i, j).wait_send()
            src = lax.rem(h + N - j, N)
            part = rg_all.at[src, i]
            remote(part, part, f_send.at[i, j], f_recv.at[i, j], w, src).wait_recv()


def back_kernel(s, *refs):
    (
        z, rg_all, pcol, svals, res, tok, dy, wq, wp, g1, g2, q, k, v, ps, att, ain, grt,
        out, gtok, gbig, gsmall,
        zall, outv, gtokv, dqs, dks, dvs, ags, rgrad, gsend, gnar, gown, gsum, gpiece, rs_in,
        small, snar, ssum, srs, spiece,
        z_send, z_recv, l_sem, f_send, f_recv, o_send, o_recv, g_send, g_recv, o_loc, g_loc,
        n_send, n_recv, sn_send, sn_recv, rs_send, rs_recv, ag_send, ag_recv,
        srs_send, srs_recv, sag_send, sag_recv,
    ) = refs
    w, h = place()
    N, W, TL, CH, L, D, HP = s.N, s.W, s.TL, s.CH, s.L, s.D, s.HP
    far = w // s.PW
    barrier = pltpu.get_barrier_semaphore()

    @pl.loop(0, W)
    def _(i):
        @pl.when(i != w)
        def _():
            signal(barrier, i, h)

    for j in range(1, N):
        signal(barrier, w, lax.rem(h + j, N))

    @pl.when(far != h)
    def _():
        @pl.loop(0, s.PW)
        def _(i):
            signal(barrier, h * s.PW + i, far)

    pl.semaphore_wait(barrier, W - 1 + N - 1 + s.PW * (far != h).astype(jnp.int32))

    swap_z = Swap(s, z, zall, z_send, z_recv, l_sem, True)

    @pl.loop(0, s.PW)
    def _(i):
        swap_z.start(i)

    def hot(c):
        rows = pl.ds(pl.multiple_of(c * CH, 16), CH)
        one, two = pcol[rows, 0:1], pcol[rows, 1:2]
        hit = jnp.logical_or(one == svals[...], two == svals[...])
        return jnp.where(hit, 1.0, 0.0).astype(BF)

    lane = lax.broadcasted_iota(jnp.int32, (PATCHES, 2 * HEAD_DIM), 1)
    first = lane < HEAD_DIM
    wpf = wp[...].reshape(D, D)
    small[...] = jnp.zeros(small.shape, F32)
    small[0 : s.E, :] = grt[0 : s.E, :]
    E = s.E

    def add_row(r, value):
        small[r : r + 1, :] += jnp.sum(value, axis=0, keepdims=True)

    @pl.loop(0, s.NCH)
    def _(c):
        rows = pl.ds(pl.multiple_of(c * CH, 16), CH)
        moe_grad = dot(hot(c), rg_all[...])
        normed, inv = norm_parts(res[rows, :])
        add_row(E + 2, moe_grad * normed)
        add_row(E + 3, moe_grad)
        total = dy[rows, :].astype(F32) + norm_pull(moe_grad, normed, inv, g2[...])
        rgrad[rows, :] = total
        ag = total.astype(BF)
        ags[rows, :] = ag
        add_row(E + 4, ag.astype(F32))
        da = dot_nt(ag, wpf).astype(BF)
        for m in range(s.IMG):
            image = pl.ds(pl.multiple_of(c * CH + m * PATCHES, 16), PATCHES)
            for p in range(HP):
                cols = slice(2 * HEAD_DIM * p, 2 * HEAD_DIM * (p + 1))
                part = da[m * PATCHES : (m + 1) * PATCHES, cols]
                zero = jnp.zeros_like(part)
                both = jnp.concatenate([jnp.where(first, part, zero), jnp.where(first, zero, part)], axis=0)
                low = ps[(c * s.IMG + m) * HP + p]
                probs = low.astype(F32)
                pgrad = dot_nt(both, v[image, cols])
                sgrad = (probs * (pgrad - jnp.sum(pgrad * probs, axis=-1, keepdims=True))).astype(BF)
                qg = dot(sgrad, k[image, cols]) * (HEAD_DIM ** (-0.5))
                dqs[image, cols] = jnp.where(first, qg[:PATCHES], qg[PATCHES:]).astype(BF)
                qq = q[image, cols]
                qboth = jnp.concatenate([jnp.where(first, qq, zero), jnp.where(first, zero, qq)], axis=0)
                dks[image, cols] = dot_tn(sgrad, qboth).astype(BF)
                dvs[image, cols] = dot_tn(low, both).astype(BF)

    for j in range(N):
        cols = slice(j * L, (j + 1) * L)
        parts = [dot_tn(ain[...], dd[:, cols]) for dd in (dqs, dks, dvs)]
        lower = dot_tn(att[:, cols], ags[...])

        def put(ref, cast):
            for i in range(3):
                ref[i * D : (i + 1) * D, :] = parts[i].astype(cast)
            for b in range(N):
                ref[3 * D + b * L : 3 * D + (b + 1) * L, :] = lower[:, b * L : (b + 1) * L].astype(cast)

        @pl.when(h == j)
        def _():
            put(gown, F32)

        @pl.when(h != j)
        def _():
            put(gsend.at[j], BF)
            remote(gsend.at[j], gnar.at[h], n_send.at[j], n_recv.at[h], w, j).start()

    small[E + 5 : E + 6, :] = jnp.sum(dqs[...].astype(F32), axis=0, keepdims=True)
    small[E + 6 : E + 7, :] = jnp.sum(dvs[...].astype(F32), axis=0, keepdims=True)

    for j in range(N):

        @pl.when(h != j)
        def _():
            remote(gsend.at[j], gnar.at[j], n_send.at[j], n_recv.at[j], w, j).wait_recv()
            gown[...] += gnar[j].astype(F32)

    gsum[...] = gown[...].astype(BF).reshape(W, s.PR, L)

    def rs_copy(i):
        return remote(gsum.at[i], rs_in.at[w], rs_send.at[i], rs_recv.at[w], i, h)

    @pl.loop(1, W)
    def _(d):
        rs_copy(lax.rem(w + d, W)).start()

    def tok_copy(src, dst, send, recv, c, j):
        mine = pl.ds(pl.multiple_of(c * CH, 16), CH)
        there = pl.ds(pl.multiple_of(h * TL + c * CH, 16), CH)
        return remote(src.at[mine], dst.at[there], send.at[c, j], recv.at[c, j], w, lax.rem(h + j, N))

    def tok_local(src, dst, sem, c):
        mine = pl.ds(pl.multiple_of(c * CH, 16), CH)
        there = pl.ds(pl.multiple_of(h * TL + c * CH, 16), CH)
        return pltpu.make_async_copy(src.at[mine], dst.at[there], sem.at[c])

    @pl.loop(0, s.NCH)
    def _(c):
        rows = pl.ds(pl.multiple_of(c * CH, 16), CH)
        back = jnp.zeros((CH, D), F32)
        for j in range(N):
            cols = slice(j * L, (j + 1) * L)
            for i, dd in enumerate((dqs, dks, dvs)):
                back += dot_nt(dd[rows, cols], wq[j, i])
        normed, inv = norm_parts(tok[rows, :].astype(F32))
        add_row(E, back * normed)
        add_row(E + 1, back)
        gtokv[rows, :] = (rgrad[rows, :] + norm_pull(back, normed, inv, g1[...])).astype(BF)
        for j in range(1, N):
            tok_copy(gtokv, gtok, g_send, g_recv, c, j).start()
        tok_local(gtokv, gtok, g_loc, c).start()

    for b in range(D // 128):
        snar[h, b * s.RP : (b + 1) * s.RP, :] = small[:, b * 128 : (b + 1) * 128]
    if 4 * s.RP < W * 8:
        snar[h, 4 * s.RP :, :] = jnp.zeros((W * 8 - 4 * s.RP, 128), F32)
    for j in range(1, N):
        remote(snar.at[h], snar.at[h], sn_send.at[j], sn_recv.at[j], w, lax.rem(h + j, N)).start()

    def forward(i, j):
        part = zall.at[h, i]
        return remote(part, part, f_send.at[i, j], f_recv.at[i, j], w, lax.rem(h + j, N))

    @pl.loop(0, s.PW)
    def _(i):
        swap_z.wait_recv(i)
        for j in range(1, N):
            forward(i, j).start()

    for j in range(1, N):
        src = lax.rem(h + N - j, N)
        remote(snar.at[h], snar.at[h], sn_send.at[j], sn_recv.at[j], w, src).wait_send()
        remote(snar.at[src], snar.at[src], sn_send.at[j], sn_recv.at[j], w, src).wait_recv()
    ssum[...] = sum(snar[j] for j in range(N)).reshape(W, 8, 128)

    def srs_copy(i):
        return remote(ssum.at[i], srs.at[w], srs_send.at[i], srs_recv.at[w], i, h)

    @pl.loop(1, W)
    def _(d):
        srs_copy(lax.rem(w + d, W)).start()

    @pl.loop(0, s.PW)
    def _(i):
        for j in range(1, N):
            src = lax.rem(h + N - j, N)
            part = zall.at[src, i]
            remote(part, part, f_send.at[i, j], f_recv.at[i, j], w, src).wait_recv()

    @pl.loop(0, s.NCH)
    def _(c):
        rows = pl.ds(pl.multiple_of(c * CH, 16), CH)
        mix = dot(hot(c), zall[...].reshape(s.E * s.Rb, D))
        outv[rows, :] = (res[rows, :] + mix).astype(BF)
        for j in range(1, N):
            tok_copy(outv, out, o_send, o_recv, c, j).start()
        tok_local(outv, out, o_loc, c).start()

    rs_in[w] = gsum[w]
    srs[w] = ssum[w]

    @pl.loop(1, W)
    def _(d):
        i = lax.rem(w + d, W)
        remote(gsum.at[i], rs_in.at[i], rs_send.at[i], rs_recv.at[i], i, h).wait_recv()
        remote(ssum.at[i], srs.at[i], srs_send.at[i], srs_recv.at[i], i, h).wait_recv()

    gpiece[...] = sum(rs_in[i].astype(F32) for i in range(W)).astype(BF)
    spiece[...] = sum(srs[i] for i in range(W))

    def ag_copy(i, slot):
        return remote(gpiece, gbig.at[slot], ag_send.at[i], ag_recv.at[slot], i, h)

    def sag_copy(i, slot):
        return remote(spiece, gsmall.at[slot], sag_send.at[i], sag_recv.at[slot], i, h)

    @pl.loop(1, W)
    def _(d):
        i = lax.rem(w + d, W)
        ag_copy(i, w).start()
        sag_copy(i, w).start()

    own_big = pltpu.make_async_copy(gpiece, gbig.at[w], l_sem)
    own_big.start()
    own_big.wait()
    own_small = pltpu.make_async_copy(spiece, gsmall.at[w], l_sem)
    own_small.start()
    own_small.wait()

    for j in range(N):

        @pl.when(h != j)
        def _():
            remote(gsend.at[j], gnar.at[j], n_send.at[j], n_recv.at[j], w, j).wait_send()

    @pl.loop(0, s.NCH)
    def _(c):
        tok_local(gtokv, gtok, g_loc, c).wait()
        tok_local(outv, out, o_loc, c).wait()
        for j in range(1, N):
            src = lax.rem(h + N - j, N)
            there = pl.ds(pl.multiple_of(src * TL + c * CH, 16), CH)
            mine = pl.ds(pl.multiple_of(c * CH, 16), CH)
            tok_copy(gtokv, gtok, g_send, g_recv, c, j).wait_send()
            tok_copy(outv, out, o_send, o_recv, c, j).wait_send()
            remote(gtokv.at[mine], gtok.at[there], g_send.at[c, j], g_recv.at[c, j], w, src).wait_recv()
            remote(outv.at[mine], out.at[there], o_send.at[c, j], o_recv.at[c, j], w, src).wait_recv()

    @pl.loop(0, s.PW)
    def _(i):
        swap_z.wait_send(i)
        for j in range(1, N):
            forward(i, j).wait_send()

    @pl.loop(1, W)
    def _(d):
        i = lax.rem(w + d, W)
        rs_copy(i).wait_send()
        srs_copy(i).wait_send()
        ag_copy(i, i).wait_send()
        sag_copy(i, i).wait_send()
        ag_copy(i, i).wait_recv()
        sag_copy(i, i).wait_recv()


VM = pl.BlockSpec(memory_space=pltpu.VMEM)
ANY = pl.BlockSpec(memory_space=pl.ANY)
DMA = pltpu.SemaphoreType.DMA


def call(kernel, s, ins, outs, scratch, collective_id, limit, name):
    return pl.pallas_call(
        functools.partial(kernel, s),
        in_specs=[spec for spec, _ in ins],
        out_specs=[spec for spec, _, _ in outs],
        out_shape=[jax.ShapeDtypeStruct(shape, dtype) for _, shape, dtype in outs],
        scratch_shapes=scratch,
        compiler_params=pltpu.CompilerParams(
            collective_id=collective_id, has_side_effects=True, vmem_limit_bytes=limit << 20
        ),
        name=name,
    )(*[a for _, a in ins])


def shards(
    wide,
    narrow,
    tokens,
    attn_gain,
    attn_shift,
    qkv_weight,
    query_value_bias,
    proj_weight,
    proj_bias,
    moe_gain,
    moe_shift,
    router_weight,
    expert_up,
    expert_up_bias,
    expert_down,
    expert_down_bias,
    routes,
    slot_index,
    cotangent,
):
    s = Sizes(wide, narrow, tokens.shape[0], tokens.shape[1], router_weight.shape[1], expert_up.shape[2])
    T, D, E, N, W, L, TL = s.T, s.D, s.E, s.N, s.W, s.L, s.TL
    PW, Rb, FL, ROWS, CH = s.PW, s.Rb, s.FL, s.ROWS, s.CH
    places = jnp.where(slot_index < s.cap, routes * s.cap + slot_index, -1)
    prow = places.T
    slot = jnp.arange(E * Rb, dtype=jnp.int32)
    inner = slot % Rb
    svals = jnp.where(inner < s.cap, (slot // Rb) * s.cap + inner, -2)[None, :]
    h = lax.axis_index("narrow")
    half = lambda a: lax.dynamic_slice_in_dim(a, h * TL, TL, 0)
    row = lambda a: a.reshape(1, -1)
    wq_loc = qkv_weight.transpose(1, 0, 2)
    blk = (PW, Rb, D)
    heads = (TL // PATCHES) * s.HP

    (
        x_in, dy_in, wq, wp, up_all, dn_all, ub_all, q, k, v, ps, att, ain, res,
    ) = call(
        front_kernel,
        s,
        [
            (ANY, tokens), (VM, cotangent), (VM, row(attn_gain)), (VM, row(attn_shift)), (ANY, wq_loc),
            (ANY, query_value_bias), (ANY, proj_weight), (VM, row(proj_bias)), (VM, row(moe_gain)),
            (VM, row(moe_shift)), (VM, prow), (ANY, expert_up[0]), (ANY, expert_down[0]), (ANY, expert_up_bias),
        ],
        [
            (ANY, blk, BF), (ANY, blk, BF), (ANY, (N, 3, D, L), BF), (ANY, (N, L, D), BF),
            (ANY, (N, D, FL), BF), (ANY, (N, FL, D), BF), (ANY, (N, 1, FL), F32),
            (ANY, (TL, D), BF), (ANY, (TL, D), BF), (ANY, (TL, D), BF),
            (ANY, (heads, 2 * PATCHES, PATCHES), BF), (ANY, (TL, D), BF), (ANY, (TL, D), BF), (ANY, (TL, D), F32),
        ],
        [
            pltpu.VMEM((TL, D), BF), pltpu.VMEM((N, 3, D, L), BF), pltpu.VMEM((N, L, D), BF),
            pltpu.VMEM((N, 2, L), F32), pltpu.VMEM((ROWS, T), BF), pltpu.VMEM((T, D), BF),
            pltpu.VMEM((TL, D), BF), pltpu.VMEM((TL, D), BF), pltpu.VMEM((TL, D), BF),
            pltpu.VMEM((heads, 2 * PATCHES, PATCHES), BF), pltpu.VMEM((TL, D), BF), pltpu.VMEM((TL, D), BF),
            pltpu.VMEM((TL, D), F32), pltpu.VMEM(blk, BF), pltpu.VMEM(blk, BF),
            DMA((6, N)), DMA((6, N)), DMA((6,)), DMA((s.NCH, N)), DMA((s.NCH, N)), DMA((PW,)), DMA((PW,)),
            DMA((PW,)), DMA((PW,)), DMA((2,)), DMA((9,)), DMA,
        ],
        1,
        56,
        "front",
    )

    wr = jnp.pad(router_weight, ((0, 0), (0, 128 - E)))
    rg_all, z, gu, gd, gub, gdb, grt = call(
        expert_kernel,
        s,
        [
            (VM, x_in.reshape(ROWS, D)), (VM, dy_in.reshape(ROWS, D)), (VM, up_all), (VM, dn_all), (VM, ub_all),
            (VM, expert_down_bias), (VM, wr),
        ],
        [
            (ANY, (N, PW, Rb, D), BF), (VM, (ROWS, D), BF), (VM, (D, FL), F32), (VM, (FL, D), F32),
            (VM, (1, FL), F32), (VM, (1, D), F32), (VM, (128, D), F32),
        ],
        [
            pltpu.VMEM((ROWS, D), BF), pltpu.VMEM((N * FL // s.FC, ROWS, s.FC), BF),
            pltpu.VMEM((N * FL // s.FC, ROWS, s.FC), BF), pltpu.VMEM((ROWS, D), F32), pltpu.VMEM((ROWS, D), F32),
            pltpu.VMEM(blk, BF),
            pltpu.VMEM((N, D, FL), BF), pltpu.VMEM((N, FL, D), BF), pltpu.VMEM((N, D, FL), BF),
            pltpu.VMEM((N, FL, D), BF), pltpu.VMEM((N, 8, FL), F32), pltpu.VMEM((N, 8, FL), F32),
            DMA((PW,)), DMA((PW,)), DMA, DMA((PW, N)), DMA((PW, N)), DMA((3, N)), DMA((3, N)),
        ],
        2,
        58,
        "expert",
    )

    out, gtok, gbig, gsmall = call(
        back_kernel,
        s,
        [
            (VM, z.reshape(blk)), (VM, rg_all.reshape(E * Rb, D)), (VM, half(places)), (VM, svals), (VM, res),
            (VM, half(tokens)), (VM, half(cotangent)), (VM, wq), (VM, wp), (VM, row(attn_gain)),
            (VM, row(moe_gain)), (VM, q), (VM, k), (VM, v), (VM, ps), (VM, att), (VM, ain), (VM, grt),
        ],
        [(ANY, (T, D), BF), (ANY, (T, D), BF), (ANY, (W, s.PR, L), BF), (ANY, (W, 8, 128), F32)],
        [
            pltpu.VMEM((N, PW, Rb, D), BF), pltpu.VMEM((TL, D), BF), pltpu.VMEM((TL, D), BF),
            pltpu.VMEM((TL, D), BF), pltpu.VMEM((TL, D), BF), pltpu.VMEM((TL, D), BF), pltpu.VMEM((TL, D), BF),
            pltpu.VMEM((TL, D), F32), pltpu.VMEM((N, s.GR, L), BF), pltpu.VMEM((N, s.GR, L), BF),
            pltpu.VMEM((s.GR, L), F32), pltpu.VMEM((W, s.PR, L), BF), pltpu.VMEM((s.PR, L), BF),
            pltpu.VMEM((W, s.PR, L), BF),
            pltpu.VMEM((s.RP, D), F32), pltpu.VMEM((N, W * 8, 128), F32), pltpu.VMEM((W, 8, 128), F32),
            pltpu.VMEM((W, 8, 128), F32), pltpu.VMEM((8, 128), F32),
            DMA((PW,)), DMA((PW,)), DMA, DMA((PW, N)), DMA((PW, N)), DMA((s.NCH, N)), DMA((s.NCH, N)),
            DMA((s.NCH, N)), DMA((s.NCH, N)), DMA((s.NCH,)), DMA((s.NCH,)),
            DMA((N,)), DMA((N,)), DMA((N,)), DMA((N,)), DMA((W,)), DMA((W,)), DMA((W,)), DMA((W,)),
            DMA((W,)), DMA((W,)), DMA((W,)), DMA((W,)),
        ],
        3,
        62,
        "back",
    )

    big = gbig.reshape(s.GR, L).astype(F32)
    grad_qkv = big[: 3 * D].reshape(3, D, L).transpose(1, 0, 2)
    grad_proj = big[3 * D :].reshape(N, L, L).transpose(1, 0, 2).reshape(L, D)
    flat = gsmall.reshape(W * 8, 128)[: 4 * s.RP].reshape(4, s.RP, 128).transpose(1, 0, 2).reshape(s.RP, D)
    qv = lax.dynamic_slice_in_dim(flat[E + 5 : E + 7], h * L, L, 1)
    return (
        out,
        gtok.astype(F32),
        flat[E],
        flat[E + 1],
        grad_qkv,
        qv,
        grad_proj,
        flat[E + 4],
        flat[E + 2],
        flat[E + 3],
        flat[:E].T,
        gu[None],
        gub,
        gd[None],
        gdb,
    )


def solution(mesh):
    in_specs = (
        P("wide", None),
        P(),
        P(),
        P(None, None, "narrow"),
        P(None, "narrow"),
        P("narrow", None),
        P(),
        P(),
        P(),
        P(),
        P("wide", None, "narrow"),
        P("wide", "narrow"),
        P("wide", "narrow", None),
        P("wide", None),
        P("wide", None),
        P("wide", None),
        P("wide", None),
    )
    out_specs = (
        P("wide", None),
        P("wide", None),
        P(),
        P(),
        P(None, None, "narrow"),
        P(None, "narrow"),
        P("narrow", None),
        P(),
        P(),
        P(),
        P(),
        P("wide", None, "narrow"),
        P("wide", "narrow"),
        P("wide", "narrow", None),
        P("wide", None),
    )
    body = functools.partial(shards, mesh.shape["wide"], mesh.shape["narrow"])
    return jax.shard_map(body, mesh=mesh, in_specs=in_specs, out_specs=out_specs, check_vma=False)
```

```python
import functools

import jax
import jax.numpy as jnp
import numpy as np
from jax import lax
from jax.experimental import pallas as pl
from jax.experimental.pallas import tpu as pltpu
from jax.sharding import PartitionSpec as P

PATCHES = 144
HEAD_DIM = 64
EPSILON = 1e-06
MESH = pl.DeviceIdType.MESH
BF = jnp.bfloat16
F32 = jnp.float32
GELU_C = 0.7978845608028654
GELU_A = 0.044715
VMEM_MB = 63


def dot(a, b):
    return jnp.dot(a, b, preferred_element_type=F32)


def dot_nt(a, b):
    return lax.dot_general(a, b, (((1,), (1,)), ((), ())), preferred_element_type=F32)


def dot_tn(a, b):
    return lax.dot_general(a, b, (((0,), (0,)), ((), ())), preferred_element_type=F32)


def norm_parts(values):
    center = values - jnp.mean(values, axis=-1, keepdims=True)
    inv_root = lax.rsqrt(jnp.mean(center * center, axis=-1, keepdims=True) + EPSILON)
    return center * inv_root, inv_root


def norm_pull(upstream, normed, inv_root, norm_gain):
    scaled = upstream * norm_gain
    bracket = (
        scaled
        - jnp.mean(scaled, axis=-1, keepdims=True)
        - normed * jnp.mean(scaled * normed, axis=-1, keepdims=True)
    )
    return inv_root * bracket


class Sizes:
    def __init__(self, wide, narrow, tokens, width, experts, local_ff):
        self.W, self.N = wide, narrow
        self.T, self.D, self.E = tokens, width, experts
        self.TL = tokens // narrow
        self.cap = tokens // experts
        self.PW = wide // narrow
        self.Rb = -(-self.cap // 16) * 16
        self.L = width // narrow
        self.FL = local_ff
        self.CH = 2 * PATCHES
        self.NCH = self.TL // self.CH
        self.IMG = self.CH // PATCHES
        self.HP = width // (2 * HEAD_DIM)
        self.ROWS = self.PW * self.Rb
        self.RC = 2 * self.Rb
        self.NR = self.PW // 2
        self.FC = min(512, local_ff)
        self.NF = narrow * local_ff // self.FC
        self.GR = 4 * width
        self.RP = -(-(experts + 7) // 8) * 8
        self.RPS = self.RP * (width // 128)
        self.bits = wide.bit_length() - 1
        unit = 16 * wide
        units = self.GR // unit
        sizes = [-(-units // 3), -(-(units - -(-units // 3)) // 2)]
        sizes.append(units - sum(sizes))
        self.streams, start = [], 0
        for t, size in enumerate(sizes):
            if size:
                low = list(range(min(3, self.bits)))
                order = low[t:] + low[:t] + list(range(len(low), self.bits))
                self.streams.append((start * unit, size * unit, order))
                start += size


def place():
    return lax.axis_index("wide"), lax.axis_index("narrow")


def signal(sem, wide, narrow):
    pl.semaphore_signal(sem, 1, device_id=(wide, narrow), device_id_type=MESH)


def remote(src, dst, send, recv, wide, narrow):
    return pltpu.make_async_remote_copy(
        src, dst, send, recv, device_id=(wide, narrow), device_id_type=MESH
    )


class Swap:
    def __init__(self, s, src, dst, send, recv, local, half=False):
        self.s, self.src = s, src
        self.send, self.recv, self.local = send, recv, local
        w, h = place()
        self.w, self.h = w, h
        self.far = lax.rem(w, s.N)
        self.slot = w // s.N
        self.dst = dst.at[self.far] if half else dst
        self.land = dst.at[h] if half else dst

    def own(self, i):
        return jnp.logical_and(self.far == self.h, i == self.slot)

    def start(self, i):
        @pl.when(jnp.logical_not(self.own(i)))
        def _():
            remote(
                self.src.at[i],
                self.dst.at[self.slot],
                self.send.at[i],
                self.recv.at[self.slot],
                i * self.s.N + self.h,
                self.far,
            ).start()

        @pl.when(self.own(i))
        def _():
            pltpu.make_async_copy(self.src.at[i], self.dst.at[self.slot], self.local).start()

    def there(self, i):
        return remote(
            self.src.at[i],
            self.land.at[i],
            self.send.at[i],
            self.recv.at[i],
            i * self.s.N + self.h,
            self.far,
        )

    def wait_send(self, i):
        @pl.when(jnp.logical_not(self.own(i)))
        def _():
            self.there(i).wait_send()

    def wait_recv(self, i):
        @pl.when(jnp.logical_not(self.own(i)))
        def _():
            self.there(i).wait_recv()

        @pl.when(self.own(i))
        def _():
            pltpu.make_async_copy(self.src.at[i], self.land.at[i], self.local).wait()


def flip(value, bit):
    return value + bit * (1 - 2 * lax.rem(value // bit, 2))


def mix_bits(value, other, count):
    total = 0
    for b in range(count):
        p, q = lax.rem(value // (1 << b), 2), lax.rem(other // (1 << b), 2)
        total = total + (p + q - 2 * p * q) * (1 << b)
    return total


def align(x, m):
    return pl.multiple_of(x, m)


def block_kernel(s, *refs):
    (
        tok, cot, g1, b1, wq_loc, qvb_loc, wp_loc, pb, g2, b2, wr, up_loc, ub_loc, dn_loc, db,
        routes, slots, svals,
        out, gtok, gbig, gsmall, gu_out, gd_out, gub_out, gdb_out,
        tokv, wq, wp, qvb, pcol, hot, quad, qs, ks, vs, ps, atts, ains, ress, snd_x, snd_dy,
        x, dyr, up, dn, ub, og, ysum, rsum, us, ds_, ur, dr, bs, br, stage, grt,
        rg_all, zall, ags, rgrad, gsend, gnar, gown, rbuf, gfin, small, snar, sacc, srec,
        ld_sem, own_sem, w_send, w_recv, m_send, m_recv, x_send, x_recv, d_send, d_recv, r_send, r_recv,
        z_send, z_recv, l_sem, rf_send, rf_recv, zf_send, zf_recv, wn_send, wn_recv, go_sem,
        n_send, n_recv, sn_send, sn_recv, h_send, h_recv, a_send, a_recv, s_send, s_recv,
        o_send, o_recv, g_send, g_recv, o_loc, g_loc, fin_sem,
    ) = refs
    w, h = place()
    N, W, T, TL, CH, L, D, E = s.N, s.W, s.T, s.TL, s.CH, s.L, s.D, s.E
    RC, FC, FL, HP, Rb, NF = s.RC, s.FC, s.FL, s.HP, s.Rb, s.NF
    far = lax.rem(w, N)
    slot = w // N
    prime = slot // 2
    pair_bits = s.NR.bit_length() - 1

    barrier = pltpu.get_barrier_semaphore()

    @pl.loop(0, s.PW)
    def _(i):
        @pl.when(jnp.logical_or(far != h, i != slot))
        def _():
            signal(barrier, i * N + h, far)

    for j in range(1, N):
        signal(barrier, w, lax.rem(h + j, N))
    low_bits = [b for b in range(s.bits) if (1 << b) < N]
    for b in range(s.bits):
        if b in low_bits:
            signal(barrier, flip(w, 1 << b), h)
        else:

            @pl.when(far != h)
            def _():
                signal(barrier, flip(w, 1 << b), h)

    mine = pl.ds(align(h * TL, 16), TL)
    load_dy = pltpu.make_async_copy(cot, quad.at[pl.ds(0, T)], ld_sem.at[0])
    load_tok = pltpu.make_async_copy(tok.at[mine], tokv, ld_sem.at[1])
    load_dy.start()
    load_tok.start()
    pairs = ((wq_loc, wq), (wp_loc, wp), (qvb_loc, qvb), (up_loc, up), (dn_loc, dn), (ub_loc, ub))
    owns = [pltpu.make_async_copy(a, b.at[h], own_sem.at[i]) for i, (a, b) in enumerate(pairs)]
    for copy in owns:
        copy.start()

    slot_rows = slots[...]
    prow = jnp.where(slot_rows < s.cap, routes[...] * s.cap + slot_rows, -1)
    one_row, two_row = prow[0:1, :], prow[1:2, :]
    pcol[...] = jnp.transpose(jnp.concatenate([prow] * 4, axis=0))

    @pl.loop(0, s.PW)
    def _(i):
        row = lax.broadcasted_iota(jnp.int32, (Rb, 1), 0)
        value = jnp.where(row < s.cap, (i * N + h) * s.cap + row, -2)
        hit = jnp.logical_or(one_row == value, two_row == value)
        hot[pl.ds(align(i * Rb, 16), Rb), :] = jnp.where(hit, 1.0, 0.0).astype(BF)

    pl.semaphore_wait(
        barrier,
        s.PW + N - 1 + len(low_bits)
        + jnp.where(far == h, -1, s.bits - len(low_bits)).astype(jnp.int32),
    )

    def weight_copy(i, j):
        a, b = pairs[i]
        return remote(a, b.at[h], w_send.at[i, j], w_recv.at[i, j], w, lax.rem(h + j, N))

    for i in range(len(pairs)):
        for j in range(1, N):
            weight_copy(i, j).start()

    swap_d = Swap(s, snd_dy, dyr, d_send, d_recv, l_sem.at[0])
    swap_x = Swap(s, snd_x, x, x_send, x_recv, l_sem.at[1])
    swap_r = Swap(s, snd_dy, rg_all, r_send, r_recv, l_sem.at[2], True)
    swap_z = Swap(s, dyr, zall, z_send, z_recv, l_sem.at[3], True)

    def dispatch(first_row, buffer, swap):
        @pl.loop(0, s.NR)
        def _(c):
            pair = mix_bits(prime, s.NR - 1 - c, pair_bits)
            rows = pl.ds(align(pair * RC, 16), RC)
            got = dot(hot[rows, :], quad[pl.ds(first_row, T), :]).astype(BF)
            for k in range(2):
                buffer[pair * 2 + k] = got[k * Rb : (k + 1) * Rb]
                swap.start(pair * 2 + k)

    load_dy.wait()
    dispatch(0, snd_dy, swap_d)

    load_tok.wait()
    for copy in owns[:3]:
        copy.wait()
    for i in range(3):
        for j in range(1, N):
            weight_copy(i, j).wait_recv()

    def moe_copy(c, j):
        part = quad.at[pl.ds(align(T + h * TL + c * CH, 16), CH)]
        return remote(part, part, m_send.at[c, j], m_recv.at[c, j], w, lax.rem(h + j, N))

    def moe_from(c, j):
        src = lax.rem(h + N - j, N)
        part = quad.at[pl.ds(align(T + src * TL + c * CH, 16), CH)]
        return remote(part, part, m_send.at[c, j], m_recv.at[c, j], w, src)

    lane = lax.broadcasted_iota(jnp.int32, (PATCHES, 2 * HEAD_DIM), 1)
    first = lane < HEAD_DIM

    def split_heads(part):
        zero = jnp.zeros_like(part)
        return jnp.concatenate([jnp.where(first, part, zero), jnp.where(first, zero, part)], axis=0)

    def join_heads(both):
        return jnp.where(first, both[:PATCHES], both[PATCHES:])

    @pl.loop(0, s.NCH)
    def _(c):
        rows = pl.ds(align(c * CH, 16), CH)
        t = tokv[rows, :].astype(F32)
        normed, _r = norm_parts(t)
        ain = (normed * g1[...] + b1[...]).astype(BF)
        ains[rows, :] = ain
        for j in range(N):
            cols = slice(j * L, (j + 1) * L)
            q = (dot(ain, wq[j, 0]) + qvb[j, 0:1, :]).astype(BF)
            qs[rows, cols] = q * BF(HEAD_DIM ** (-0.5))
            ks[rows, cols] = dot(ain, wq[j, 1]).astype(BF)
            vs[rows, cols] = (dot(ain, wq[j, 2]) + qvb[j, 1:2, :]).astype(BF)
        for m in range(s.IMG):
            image = pl.ds(align(c * CH + m * PATCHES, 16), PATCHES)
            for p in range(HP):
                cols = slice(2 * HEAD_DIM * p, 2 * HEAD_DIM * (p + 1))
                scores = dot_nt(split_heads(qs[image, cols]), ks[image, cols])
                top = jnp.max(scores, axis=-1, keepdims=True)
                grown = jnp.exp(scores - top)
                probs = (grown * (1.0 / jnp.sum(grown, axis=-1, keepdims=True))).astype(BF)
                ps[(c * s.IMG + m) * HP + p] = probs
                atts[image, cols] = join_heads(dot(probs, vs[image, cols])).astype(BF)
        residual = t + (dot(atts[rows, :], wp[...].reshape(D, D)) + pb[...])
        ress[rows, :] = residual
        normed, _r = norm_parts(residual)
        quad[pl.ds(align(T + h * TL + c * CH, 16), CH), :] = (normed * g2[...] + b2[...]).astype(BF)
        for j in range(1, N):
            moe_copy(c, j).start()

    @pl.loop(0, s.NCH)
    def _(c):
        for j in range(1, N):
            moe_from(c, j).wait_recv()

    dispatch(T, snd_x, swap_x)

    @pl.loop(0, s.NCH)
    def _(c):
        for j in range(1, N):
            moe_copy(c, j).wait_send()

    for copy in owns[3:]:
        copy.wait()
    for i in range(len(pairs)):
        for j in range(1, N):
            if i >= 3:
                weight_copy(i, j).wait_recv()
            weight_copy(i, j).wait_send()

    @pl.loop(0, s.PW)
    def _(i):
        swap_d.wait_send(i)

    load_ags = pltpu.make_async_copy(cot.at[mine], ags, ld_sem.at[0])
    load_ags.start()
    per = FL // FC
    expert_lane = lax.broadcasted_iota(jnp.int32, (RC, E), 1)
    grt[...] = jnp.zeros(grt.shape, F32)

    def pg_rows(f):
        return pl.ds(align(f * s.ROWS, 16), s.ROWS)

    @pl.loop(0, s.NR)
    def _(c):
        pair = mix_bits(prime, c, pair_bits)
        rows = pl.ds(align(pair * RC, 16), RC)
        both = pl.ds(pair * 2, 2)
        for k in range(2):
            swap_d.wait_recv(pair * 2 + k)
            swap_x.wait_recv(pair * 2 + k)
        xr = x[both].reshape(RC, D)
        dyf = dyr[both].reshape(RC, D).astype(F32)
        logits = dot_nt(xr, wr[...])
        top = jnp.max(logits, axis=-1, keepdims=True)
        grown = jnp.exp(logits - top)
        probs = grown * (1.0 / jnp.sum(grown, axis=-1, keepdims=True))
        gate = jnp.sum(jnp.where(expert_lane == w, probs, 0.0), axis=-1, keepdims=True)
        og[rows, :] = (gate * dyf).astype(BF)
        ysum[...] = jnp.broadcast_to(db[...], (RC, D))
        rsum[...] = jnp.zeros((RC, D), F32)

        @pl.loop(0, NF)
        def _(f):
            j = f // per
            off = pl.ds(align(lax.rem(f, per) * FC, 128), FC)
            pre = dot(x[both].reshape(RC, D), up[j, :, off]) + ub[j, :, off]
            square = pre * pre
            t = jnp.tanh(GELU_C * (pre + GELU_A * (square * pre)))
            half = 0.5 * (1.0 + t)
            hidden = (pre * half).astype(BF)
            slope = half + (0.5 * GELU_C) * pre * (1.0 - t * t) * (1.0 + (3.0 * GELU_A) * square)
            grad = (dot_nt(og[rows, :], dn[j, off, :]) * slope).astype(BF)
            hot[rows, pl.ds(align(f * FC, 128), FC)] = hidden
            quad[pl.ds(align(f * s.ROWS + pair * RC, 16), RC), 0:FC] = grad
            ysum[...] += dot(hidden, dn[j, off, :])
            rsum[...] += dot_nt(grad, up[j, :, off])

        y = ysum[...].astype(BF).astype(F32)
        gate_grad = jnp.sum(dyf * y, axis=-1, keepdims=True)
        logit = (gate_grad * probs * (jnp.where(expert_lane == w, 1.0, 0.0) - gate)).astype(BF)
        back = (rsum[...] + dot(logit, wr[...])).astype(BF)
        for k in range(2):
            snd_dy[pair * 2 + k] = back[k * Rb : (k + 1) * Rb]
            swap_r.start(pair * 2 + k)
        zz = (gate * y).astype(BF)
        for k in range(2):
            dyr[pair * 2 + k] = zz[k * Rb : (k + 1) * Rb]
        grt[...] += dot_tn(logit, xr)

    def n_copy(i, j):
        a, b = ((us, ur), (ds_, dr))[i]
        return remote(a.at[j - 1], b.at[j - 1], wn_send.at[i, j], wn_recv.at[i, j], w, lax.rem(h + j, N))

    def b_copy(j, slab):
        return remote(bs.at[j - 1], br.at[slab], wn_send.at[2, j], wn_recv.at[2, j], w, lax.rem(h + j, N))

    def hid_cols(owner, c):
        return pl.ds(align((owner * per + c) * FC, 128), FC)

    def up_part(owner, c):
        return dot_tn(x[...].reshape(s.ROWS, D), quad[pg_rows(owner * per + c), 0:FC])

    def down_part(owner, c):
        return dot_tn(hot[:, hid_cols(owner, c)], og[...])

    def pg_sum(owner, c):
        return jnp.sum(quad[pg_rows(owner * per + c), 0:FC].astype(F32), axis=0, keepdims=True)

    og_sum = jnp.sum(og[...].astype(F32), axis=0, keepdims=True)
    span = min(FL, D)

    def put_bias(ref):
        for b in range(D // span):
            ref[1 + b : 2 + b, 0:span] = og_sum[:, b * span : (b + 1) * span]

    for j in range(1, N):
        owner = lax.rem(h + j, N)
        for c in range(per):
            cols = slice(c * FC, (c + 1) * FC)
            us[j - 1, :, cols] = up_part(owner, c).astype(BF)
        n_copy(0, j).start()
        for c in range(per):
            cols = slice(c * FC, (c + 1) * FC)
            ds_[j - 1, cols, :] = down_part(owner, c).astype(BF)
        n_copy(1, j).start()
        for c in range(per):
            cols = slice(c * FC, (c + 1) * FC)
            bs[j - 1, 0:1, cols] = pg_sum(owner, c)
        put_bias(bs.at[j - 1])
        b_copy(j, h).start()
    def go_copy(i, c):
        cols = pl.ds(c * FC, FC)
        if i == 0:
            return pltpu.make_async_copy(stage.at[c, :, pl.ds(0, FC)], gu_out.at[:, cols], go_sem.at[c])
        return pltpu.make_async_copy(stage.at[c, pl.ds(0, FC), :], gd_out.at[cols, :], go_sem.at[c])

    for c in range(per):
        cols = slice(c * FC, (c + 1) * FC)
        total = up_part(h, c)
        for j in range(1, N):
            if c == 0:
                n_copy(0, j).wait_recv()
            total += ur[j - 1, :, cols].astype(F32)
        stage[c, :, 0:FC] = total
        go_copy(0, c).start()
        gub_out[:, cols] = pg_sum(h, c)
    for c in range(per):
        cols = slice(c * FC, (c + 1) * FC)
        total = down_part(h, c)
        for j in range(1, N):
            if c == 0:
                n_copy(1, j).wait_recv()
            total += dr[j - 1, cols, :].astype(F32)
        go_copy(0, c).wait()
        stage[c, 0:FC, :] = total
        go_copy(1, c).start()
    put_bias(br.at[h])

    def pass_on(buffer, send, recv, i, j, src=None):
        part = buffer.at[h if src is None else src, i]
        return remote(part, part, send.at[i, j], recv.at[i, j], w, lax.rem(h + j, N) if src is None else src)

    @pl.loop(0, s.PW)
    def _(c):
        i = mix_bits(slot, c, pair_bits + 1)
        swap_r.wait_recv(i)
        for j in range(1, N):
            pass_on(rg_all, rf_send, rf_recv, i, j).start()

    @pl.loop(0, s.PW)
    def _(c):
        swap_z.start(mix_bits(slot, s.PW - 1 - c, pair_bits + 1))

    for j in range(1, N):
        src = lax.rem(h + N - j, N)
        b_copy(j, src).wait_recv()
        gub_out[...] += br[src, 0:1, :]
    for b in range(D // span):
        gdb_out[:, b * span : (b + 1) * span] = sum(br[j, 1 + b : 2 + b, 0:span] for j in range(N))

    @pl.loop(0, s.PW)
    def _(i):
        for j in range(1, N):
            pass_on(rg_all, rf_send, rf_recv, i, j, lax.rem(h + N - j, N)).wait_recv()

    def spots(c):
        rows = pl.ds(align(h * TL + c * CH, 16), CH)
        hit = jnp.logical_or(pcol[rows, 0:1] == svals[...], pcol[rows, 1:2] == svals[...])
        return jnp.where(hit, 1.0, 0.0).astype(BF)

    small[...] = jnp.zeros(small.shape, F32)
    small[0:E, :] = grt[...]

    def add_row(r, value):
        small[r : r + 1, :] += jnp.sum(value, axis=0, keepdims=True)

    load_ags.wait()

    @pl.loop(0, s.NCH)
    def _(c):
        rows = pl.ds(align(c * CH, 16), CH)
        moe_grad = dot(spots(c), rg_all[...].reshape(E * Rb, D))
        normed, inv = norm_parts(ress[rows, :])
        add_row(E + 2, moe_grad * normed)
        add_row(E + 3, moe_grad)
        total = ags[rows, :].astype(F32) + norm_pull(moe_grad, normed, inv, g2[...])
        rgrad[rows, :] = total
        ag = total.astype(BF)
        ags[rows, :] = ag
        add_row(E + 4, ag.astype(F32))
        da = dot_nt(ag, wp[...].reshape(D, D)).astype(BF)
        for m in range(s.IMG):
            image = pl.ds(align(c * CH + m * PATCHES, 16), PATCHES)
            for p in range(HP):
                cols = slice(2 * HEAD_DIM * p, 2 * HEAD_DIM * (p + 1))
                both = split_heads(da[m * PATCHES : (m + 1) * PATCHES, cols])
                low = ps[(c * s.IMG + m) * HP + p]
                probs = low.astype(F32)
                q, k, v = qs[image, cols], ks[image, cols], vs[image, cols]
                pgrad = dot_nt(both, v)
                sgrad = (probs * (pgrad - jnp.sum(pgrad * probs, axis=-1, keepdims=True))).astype(BF)
                qs[image, cols] = join_heads(dot(sgrad, k) * (HEAD_DIM ** (-0.5))).astype(BF)
                ks[image, cols] = dot_tn(sgrad, split_heads(q)).astype(BF)
                vs[image, cols] = dot_tn(low, both).astype(BF)

    def g_copy(rel, wide_place, narrow_place):
        return remote(gsend.at[rel], gnar.at[rel], n_send.at[rel], n_recv.at[rel], wide_place, narrow_place)

    for j in range(N):
        cols = slice(j * L, (j + 1) * L)
        parts = [dot_tn(ains[...], dd[:, cols]) for dd in (qs, ks, vs)]
        lower = dot_tn(atts[:, cols], ags[...])

        def put(ref, cast):
            for i in range(3):
                ref[i * D : (i + 1) * D, :] = parts[i].astype(cast)
            for b in range(N):
                ref[3 * D + b * L : 3 * D + (b + 1) * L, :] = lower[:, b * L : (b + 1) * L].astype(cast)

        @pl.when(h == j)
        def _():
            put(gown, F32)

        @pl.when(h != j)
        def _():
            rel = lax.rem(j - h + N, N) - 1
            put(gsend.at[rel], BF)
            g_copy(rel, w, j).start()

    small[E + 5 : E + 6, :] = jnp.sum(qs[...].astype(F32), axis=0, keepdims=True)
    small[E + 6 : E + 7, :] = jnp.sum(vs[...].astype(F32), axis=0, keepdims=True)

    for j in range(1, N):
        g_copy(j - 1, w, lax.rem(h + N - j, N)).wait_recv()
        gown[...] += gnar[j - 1].astype(F32)
    for j in range(1, N):
        g_copy(j - 1, w, lax.rem(h + j, N)).wait_send()
    sbuf = gsend.at[0]

    def bit_of(b):
        return lax.rem(w // (1 << b), 2)

    def segment(stream, k):
        start, size, order = s.streams[stream]
        first_row = start
        for step in range(k):
            size = size // 2
            first_row = first_row + bit_of(order[step]) * size
        return first_row, size

    def halves(stream, k):
        start, size = segment(stream, k)
        bit = s.streams[stream][2][k]
        half = size // 2
        keep = align(start + bit_of(bit) * half, 16)
        give = align(start + (1 - bit_of(bit)) * half, 16)
        return pl.ds(keep, half), pl.ds(give, half), flip(w, 1 << bit)

    def fold_copy(stream, k):
        keep, give, partner = halves(stream, k)
        return remote(
            sbuf.at[give], rbuf.at[keep], h_send.at[stream, k], h_recv.at[stream, k], partner, h
        )

    def fold_start(k):
        for t in range(len(s.streams)):
            keep, give, _p = halves(t, k)
            sbuf[give, :] = gown[give, :].astype(BF)
            fold_copy(t, k).start()

    def fold_end(k):
        for t in range(len(s.streams)):
            keep, give, partner = halves(t, k)
            remote(
                sbuf.at[give], rbuf.at[give], h_send.at[t, k], h_recv.at[t, k], partner, h
            ).wait()
            gown[keep, :] += rbuf[give, :].astype(F32)

    def grow_start(k):
        for t in range(len(s.streams)):
            keep, give, partner = halves(t, k)
            remote(gfin.at[keep], gfin.at[keep], a_send.at[t, k], a_recv.at[t, k], partner, h).start()

    def grow_end(k):
        for t in range(len(s.streams)):
            keep, give, partner = halves(t, k)
            remote(gfin.at[keep], gfin.at[give], a_send.at[t, k], a_recv.at[t, k], partner, h).wait()

    def s_copy(k):
        return remote(sacc.at[k], srec.at[k], s_send.at[k], s_recv.at[k], flip(w, 1 << k), h)

    def tok_copy(src, dst, send, recv, c, j):
        here = pl.ds(align(c * CH, 16), CH)
        there = pl.ds(align(h * TL + c * CH, 16), CH)
        return remote(src.at[here], dst.at[there], send.at[c, j], recv.at[c, j], w, lax.rem(h + j, N))

    def tok_local(src, dst, sem, c):
        here = pl.ds(align(c * CH, 16), CH)
        there = pl.ds(align(h * TL + c * CH, 16), CH)
        return pltpu.make_async_copy(src.at[here], dst.at[there], sem.at[c])

    def first_norm_back():
        @pl.loop(0, s.NCH)
        def _(c):
            rows = pl.ds(align(c * CH, 16), CH)
            back = jnp.zeros((CH, D), F32)
            for j in range(N):
                cols = slice(j * L, (j + 1) * L)
                for i, dd in enumerate((qs, ks, vs)):
                    back += dot_nt(dd[rows, cols], wq[j, i])
            normed, inv = norm_parts(tokv[rows, :].astype(F32))
            add_row(E, back * normed)
            add_row(E + 1, back)
            rgrad[rows, :] += norm_pull(back, normed, inv, g1[...])
            for j in range(1, N):
                tok_copy(rgrad, gtok, g_send, g_recv, c, j).start()
            tok_local(rgrad, gtok, g_loc, c).start()

        for b in range(D // 128):
            snar[h, b * s.RP : (b + 1) * s.RP, :] = small[:, b * 128 : (b + 1) * 128]
        for j in range(1, N):
            remote(snar.at[h], snar.at[h], sn_send.at[j], sn_recv.at[j], w, lax.rem(h + j, N)).start()

    def combine():
        @pl.loop(0, s.PW)
        def _(c):
            i = mix_bits(slot, c, pair_bits + 1)
            swap_z.wait_recv(i)
            for j in range(1, N):
                pass_on(zall, zf_send, zf_recv, i, j).start()

        @pl.loop(0, s.PW)
        def _(i):
            for j in range(1, N):
                pass_on(zall, zf_send, zf_recv, i, j, lax.rem(h + N - j, N)).wait_recv()

        @pl.loop(0, s.NCH)
        def _(c):
            rows = pl.ds(align(c * CH, 16), CH)
            mixed = dot(spots(c), zall[...].reshape(E * Rb, D))
            ains[rows, :] = (ress[rows, :] + mixed).astype(BF)
            for j in range(1, N):
                tok_copy(ains, out, o_send, o_recv, c, j).start()
            tok_local(ains, out, o_loc, c).start()

    def small_narrow():
        for j in range(1, N):
            src = lax.rem(h + N - j, N)
            remote(snar.at[h], snar.at[h], sn_send.at[j], sn_recv.at[j], w, src).wait_send()
            remote(snar.at[src], snar.at[src], sn_send.at[j], sn_recv.at[j], w, src).wait_recv()
        sacc[0] = sum(snar[j] for j in range(N))

    for k in range(s.bits):
        fold_start(k)
        if k == 0:
            first_norm_back()
        if k == 1:
            combine()
        if k == 2:
            small_narrow()
        fold_end(k)
    for t in range(len(s.streams)):
        start, size = segment(t, s.bits)
        rows = pl.ds(align(start, 16), size)
        gfin[rows, :] = gown[rows, :].astype(BF)
    for k in range(s.bits):
        s_copy(k).start()
        grow_start(s.bits - 1 - k)
        s_copy(k).wait()
        sacc[k + 1] = sacc[k] + srec[k]
        grow_end(s.bits - 1 - k)
    gsmall[...] = sacc[s.bits]
    fin = pltpu.make_async_copy(gfin, gbig, fin_sem)
    fin.start()

    for j in range(1, N):
        for i in range(2):
            n_copy(i, j).wait_send()
        b_copy(j, h).wait_send()

    @pl.loop(0, s.PW)
    def _(i):
        swap_x.wait_send(i)
        swap_r.wait_send(i)
        swap_z.wait_send(i)
        for j in range(1, N):
            pass_on(rg_all, rf_send, rf_recv, i, j).wait_send()
            pass_on(zall, zf_send, zf_recv, i, j).wait_send()

    @pl.loop(0, s.NCH)
    def _(c):
        tok_local(rgrad, gtok, g_loc, c).wait()
        tok_local(ains, out, o_loc, c).wait()
        here = pl.ds(align(c * CH, 16), CH)
        for j in range(1, N):
            src = lax.rem(h + N - j, N)
            there = pl.ds(align(src * TL + c * CH, 16), CH)
            tok_copy(rgrad, gtok, g_send, g_recv, c, j).wait_send()
            tok_copy(ains, out, o_send, o_recv, c, j).wait_send()
            remote(rgrad.at[here], gtok.at[there], g_send.at[c, j], g_recv.at[c, j], w, src).wait_recv()
            remote(ains.at[here], out.at[there], o_send.at[c, j], o_recv.at[c, j], w, src).wait_recv()

    for c in range(per):
        go_copy(1, c).wait()
    fin.wait()


VM = pl.BlockSpec(memory_space=pltpu.VMEM)
ANY = pl.BlockSpec(memory_space=pl.ANY)
DMA = pltpu.SemaphoreType.DMA
V = pltpu.VMEM


def shards(
    wide,
    narrow,
    tokens,
    attn_gain,
    attn_shift,
    qkv_weight,
    query_value_bias,
    proj_weight,
    proj_bias,
    moe_gain,
    moe_shift,
    router_weight,
    expert_up,
    expert_up_bias,
    expert_down,
    expert_down_bias,
    routes,
    slot_index,
    cotangent,
):
    s = Sizes(wide, narrow, tokens.shape[0], tokens.shape[1], router_weight.shape[1], expert_up.shape[2])
    T, D, E, N, W, L, TL = s.T, s.D, s.E, s.N, s.W, s.L, s.TL
    PW, Rb, FL, ROWS, RC, NCH = s.PW, s.Rb, s.FL, s.ROWS, s.RC, s.NCH
    slot = np.arange(E * Rb)
    half, rest = slot // (PW * Rb), slot % (PW * Rb)
    pos, inner = rest // Rb, rest % Rb
    svals = np.where(inner < s.cap, (pos * N + half) * s.cap + inner, -2).astype(np.int32)[None, :]
    row = lambda a: a.reshape(1, -1)
    blk = (PW, Rb, D)
    heads = (TL // PATCHES) * s.HP
    NS = len(s.streams)
    ins = [
        (ANY, tokens), (ANY, cotangent), (VM, row(attn_gain)), (VM, row(attn_shift)),
        (ANY, qkv_weight.transpose(1, 0, 2)), (ANY, query_value_bias), (ANY, proj_weight), (VM, row(proj_bias)),
        (VM, row(moe_gain)), (VM, row(moe_shift)), (VM, router_weight.T), (ANY, expert_up[0]),
        (ANY, expert_up_bias), (ANY, expert_down[0]), (VM, expert_down_bias), (VM, routes.T), (VM, slot_index.T),
        (VM, jnp.asarray(svals)),
    ]
    outs = [
        (ANY, (T, D), BF), (ANY, (T, D), F32), (ANY, (s.GR, L), BF), (VM, (s.RPS, 128), F32),
        (ANY, (D, FL), F32), (ANY, (FL, D), F32), (VM, (1, FL), F32), (VM, (1, D), F32),
    ]
    scratch = [
        V((TL, D), BF), V((N, 3, D, L), BF), V((N, L, D), BF), V((N, 2, L), F32), V((T, 8), jnp.int32),
        V((ROWS, T), BF), V((2 * T, D), BF), V((TL, D), BF), V((TL, D), BF), V((TL, D), BF),
        V((heads, 2 * PATCHES, PATCHES), BF), V((TL, D), BF), V((TL, D), BF), V((TL, D), F32), V(blk, BF), V(blk, BF),
        V(blk, BF), V(blk, BF), V((N, D, FL), BF), V((N, FL, D), BF), V((N, 1, FL), F32), V((ROWS, D), BF),
        V((RC, D), F32), V((RC, D), F32), V((N - 1, D, FL), BF), V((N - 1, FL, D), BF), V((N - 1, D, FL), BF),
        V((N - 1, FL, D), BF), V((N - 1, 8, FL), F32), V((N, 8, FL), F32), V((FL // s.FC, D, D), F32),
        V((E, D), F32),
        V((N,) + blk, BF), V((N,) + blk, BF), V((TL, D), BF), V((TL, D), F32), V((N - 1, s.GR, L), BF),
        V((N - 1, s.GR, L), BF), V((s.GR, L), F32), V((s.GR, L), BF), V((s.GR, L), BF),
        V((s.RP, D), F32), V((N, s.RPS, 128), F32), V((s.bits + 1, s.RPS, 128), F32), V((s.bits, s.RPS, 128), F32),
        DMA((2,)), DMA((6,)), DMA((6, N)), DMA((6, N)), DMA((NCH, N)), DMA((NCH, N)),
        DMA((PW,)), DMA((PW,)), DMA((PW,)), DMA((PW,)), DMA((PW,)), DMA((PW,)),
        DMA((PW,)), DMA((PW,)), DMA((4,)), DMA((PW, N)), DMA((PW, N)), DMA((PW, N)), DMA((PW, N)),
        DMA((3, N)), DMA((3, N)), DMA((FL // s.FC,)),
        DMA((N,)), DMA((N,)), DMA((N,)), DMA((N,)), DMA((NS, s.bits)), DMA((NS, s.bits)), DMA((NS, s.bits)),
        DMA((NS, s.bits)), DMA((s.bits,)), DMA((s.bits,)),
        DMA((NCH, N)), DMA((NCH, N)), DMA((NCH, N)), DMA((NCH, N)), DMA((NCH,)), DMA((NCH,)), DMA,
    ]
    out, gtok, gbig, gsmall, gu, gd, gub, gdb = pl.pallas_call(
        functools.partial(block_kernel, s),
        in_specs=[spec for spec, _ in ins],
        out_specs=[spec for spec, _, _ in outs],
        out_shape=[jax.ShapeDtypeStruct(shape, dtype) for _, shape, dtype in outs],
        scratch_shapes=scratch,
        compiler_params=pltpu.CompilerParams(
            collective_id=1, has_side_effects=True, vmem_limit_bytes=VMEM_MB << 20
        ),
        name="block",
    )(*[a for _, a in ins])

    big = gbig.astype(F32)
    grad_qkv = big[: 3 * D].reshape(3, D, L).transpose(1, 0, 2)
    grad_proj = big[3 * D :].reshape(N, L, L).transpose(1, 0, 2).reshape(L, D)
    flat = gsmall.reshape(D // 128, s.RP, 128).transpose(1, 0, 2).reshape(s.RP, D)
    h = lax.axis_index("narrow")
    qv = lax.dynamic_slice_in_dim(flat[E + 5 : E + 7], h * L, L, 1)
    return (
        out,
        gtok,
        flat[E],
        flat[E + 1],
        grad_qkv,
        qv,
        grad_proj,
        flat[E + 4],
        flat[E + 2],
        flat[E + 3],
        flat[:E].T,
        gu[None],
        gub,
        gd[None],
        gdb,
    )


def solution(mesh):
    in_specs = (
        P("wide", None),
        P(),
        P(),
        P(None, None, "narrow"),
        P(None, "narrow"),
        P("narrow", None),
        P(),
        P(),
        P(),
        P(),
        P("wide", None, "narrow"),
        P("wide", "narrow"),
        P("wide", "narrow", None),
        P("wide", None),
        P("wide", None),
        P("wide", None),
        P("wide", None),
    )
    out_specs = (
        P("wide", None),
        P("wide", None),
        P(),
        P(),
        P(None, None, "narrow"),
        P(None, "narrow"),
        P("narrow", None),
        P(),
        P(),
        P(),
        P(),
        P("wide", None, "narrow"),
        P("wide", "narrow"),
        P("wide", "narrow", None),
        P("wide", None),
    )
    body = functools.partial(shards, mesh.shape["wide"], mesh.shape["narrow"])
    return jax.shard_map(body, mesh=mesh, in_specs=in_specs, out_specs=out_specs, check_vma=False)
```

```python
import functools

import jax
import jax.numpy as jnp
import numpy as np
from jax import lax
from jax.experimental import pallas as pl
from jax.experimental.pallas import tpu as pltpu
from jax.sharding import PartitionSpec as P

PATCHES = 144
HEAD_DIM = 64
EPSILON = 1e-06
MESH = pl.DeviceIdType.MESH
BF = jnp.bfloat16
F32 = jnp.float32
GELU_C = 0.7978845608028654
GELU_A = 0.044715
VMEM_MB = 63
PARTS = 4


def dot(a, b):
    return jnp.dot(a, b, preferred_element_type=F32)


def dot_nt(a, b):
    return lax.dot_general(a, b, (((1,), (1,)), ((), ())), preferred_element_type=F32)


def dot_tn(a, b):
    return lax.dot_general(a, b, (((0,), (0,)), ((), ())), preferred_element_type=F32)


def norm_parts(values):
    center = values - jnp.mean(values, axis=-1, keepdims=True)
    inv_root = lax.rsqrt(jnp.mean(center * center, axis=-1, keepdims=True) + EPSILON)
    return center * inv_root, inv_root


def norm_pull(upstream, normed, inv_root, norm_gain):
    scaled = upstream * norm_gain
    bracket = (
        scaled
        - jnp.mean(scaled, axis=-1, keepdims=True)
        - normed * jnp.mean(scaled * normed, axis=-1, keepdims=True)
    )
    return inv_root * bracket


class Sizes:
    def __init__(self, wide, narrow, tokens, width, experts, local_ff):
        self.W, self.N = wide, narrow
        self.T, self.D, self.E = tokens, width, experts
        self.TL = tokens // narrow
        self.cap = tokens // experts
        self.PW = wide // narrow
        self.Rb = -(-self.cap // 16) * 16
        self.L = width // narrow
        self.FL = local_ff
        self.CH = 2 * PATCHES
        self.NCH = self.TL // self.CH
        self.IMG = self.CH // PATCHES
        self.HP = width // (2 * HEAD_DIM)
        self.ROWS = self.PW * self.Rb
        self.RC = 2 * self.Rb
        self.NR = self.PW // 2
        self.FC = min(512, local_ff)
        self.NF = narrow * local_ff // self.FC
        self.LW = min(128, self.L)
        self.halves = 2 if self.L == 256 else 1
        first = 3 * width + width // self.LW * self.L
        self.jobs = [first, 3 * width][: self.halves]
        self.RP = -(-(experts + 7) // 8) * 8
        self.RPS = self.RP * (width // 128)
        self.bits = wide.bit_length() - 1
        self.streams = [self.cut(rows, wide, j) for j, rows in enumerate(self.jobs)]

    def cut(self, rows, wide, job):
        unit = 16 * wide
        units, count = rows // unit, 3
        streams, start = [], 0
        for t in range(count):
            size = -(-(units - start) // (count - t))
            if size:
                low = list(range(min(3, self.bits)))
                order = low[t:] + low[:t] + list(range(len(low), self.bits))
                streams.append((start * unit, size * unit, order))
                start += size
        return streams


def place():
    return lax.axis_index("wide"), lax.axis_index("narrow")


def signal(sem, wide, narrow):
    pl.semaphore_signal(sem, 1, device_id=(wide, narrow), device_id_type=MESH)


def remote(src, dst, send, recv, wide, narrow):
    return pltpu.make_async_remote_copy(
        src, dst, send, recv, device_id=(wide, narrow), device_id_type=MESH
    )


class Swap:
    def __init__(self, s, src, dst, send, recv, local, half=False):
        self.s, self.src = s, src
        self.send, self.recv, self.local = send, recv, local
        w, h = place()
        self.w, self.h = w, h
        self.far = lax.rem(w, s.N)
        self.slot = w // s.N
        self.dst = dst.at[self.far] if half else dst
        self.land = dst.at[h] if half else dst

    def at(self, i):
        if len(self.src.shape) == 2:
            return self.src.at[pl.ds(align(i * self.s.Rb, 16), self.s.Rb)]
        return self.src.at[i]

    def own(self, i):
        return jnp.logical_and(self.far == self.h, i == self.slot)

    def start(self, i):
        @pl.when(jnp.logical_not(self.own(i)))
        def _():
            remote(
                self.at(i),
                self.dst.at[self.slot],
                self.send.at[i],
                self.recv.at[self.slot],
                i * self.s.N + self.h,
                self.far,
            ).start()

        @pl.when(self.own(i))
        def _():
            pltpu.make_async_copy(self.at(i), self.dst.at[self.slot], self.local).start()

    def there(self, i):
        return remote(
            self.at(i),
            self.land.at[i],
            self.send.at[i],
            self.recv.at[i],
            i * self.s.N + self.h,
            self.far,
        )

    def wait_send(self, i):
        @pl.when(jnp.logical_not(self.own(i)))
        def _():
            self.there(i).wait_send()

    def wait_recv(self, i):
        @pl.when(jnp.logical_not(self.own(i)))
        def _():
            self.there(i).wait_recv()

        @pl.when(self.own(i))
        def _():
            pltpu.make_async_copy(self.at(i), self.land.at[i], self.local).wait()


def flip(value, bit):
    return value + bit * (1 - 2 * lax.rem(value // bit, 2))


def mix_bits(value, other, count):
    total = 0
    for b in range(count):
        p, q = lax.rem(value // (1 << b), 2), lax.rem(other // (1 << b), 2)
        total = total + (p + q - 2 * p * q) * (1 << b)
    return total


def align(x, m):
    return pl.multiple_of(x, m)


def block_kernel(s, *refs):
    (
        tok, cot, g1, b1, wq_loc, qvb_loc, wp_loc, pb, g2, b2, wr, up_loc, ub_loc, dn_loc, db,
        routes, slots, svals,
        out, gtok, gsmall, gu_out, gd_out, gub_out, gdb_out, *rest,
    ) = refs
    gbigs, rest = rest[: len(s.jobs)], rest[len(s.jobs) :]
    (
        tokv, wq, wp, qvb, pcol, hot, quad, qs, ks, vs, ps, atts, ains, ress, snd_x, snd_dy,
        x, dyr, up, dn, ub, og, ysum, rsum, us, ds_, ur, dr, bs, br, stage, grt,
        rg_all, zall, ags, rgrad, small, snar, sacc, srec, *more,
    ) = rest
    NJ = len(s.jobs)
    job_refs = [more[5 * n : 5 * n + 5] for n in range(NJ)]
    (
        ld_sem, own_sem, w_send, w_recv, m_send, m_recv, x_send, x_recv, d_send, d_recv, r_send, r_recv,
        z_send, z_recv, l_sem, rf_send, rf_recv, zf_send, zf_recv, wn_send, wn_recv, go_sem,
        n_send, n_recv, sn_send, sn_recv, h_send, h_recv, a_send, a_recv, s_send, s_recv,
        o_send, o_recv, g_send, g_recv, o_loc, g_loc, fin_sem,
    ) = more[5 * NJ :]
    w, h = place()
    N, W, T, TL, CH, L, D, E = s.N, s.W, s.T, s.TL, s.CH, s.L, s.D, s.E
    RC, FC, FL, HP, Rb, NF = s.RC, s.FC, s.FL, s.HP, s.Rb, s.NF
    far = lax.rem(w, N)
    slot = w // N
    prime = slot // 2
    pair_bits = s.NR.bit_length() - 1

    barrier = pltpu.get_barrier_semaphore()

    @pl.loop(0, s.PW)
    def _(i):
        @pl.when(jnp.logical_or(far != h, i != slot))
        def _():
            signal(barrier, i * N + h, far)

    for j in range(1, N):
        signal(barrier, w, lax.rem(h + j, N))
    low_bits = [b for b in range(s.bits) if (1 << b) < N]
    for b in range(s.bits):
        if b in low_bits:
            signal(barrier, flip(w, 1 << b), h)
        else:

            @pl.when(far != h)
            def _():
                signal(barrier, flip(w, 1 << b), h)

    mine = pl.ds(align(h * TL, 16), TL)
    load_dy = pltpu.make_async_copy(cot, quad.at[pl.ds(0, T)], ld_sem.at[0])
    load_tok = pltpu.make_async_copy(tok.at[mine], tokv, ld_sem.at[1])
    load_dy.start()
    load_tok.start()
    pairs = ((wq_loc, wq), (wp_loc, wp), (qvb_loc, qvb), (up_loc, up), (dn_loc, dn), (ub_loc, ub))
    owns = [pltpu.make_async_copy(a, b.at[h], own_sem.at[i]) for i, (a, b) in enumerate(pairs)]
    for copy in owns:
        copy.start()

    slot_rows = slots[...]
    prow = jnp.where(slot_rows < s.cap, routes[...] * s.cap + slot_rows, -1)
    one_row, two_row = prow[0:1, :], prow[1:2, :]

    def build(pair):
        for k in range(2):
            i = pair * 2 + k
            row = lax.broadcasted_iota(jnp.int32, (Rb, 1), 0)
            value = jnp.where(row < s.cap, (i * N + h) * s.cap + row, -2)
            hit = jnp.logical_or(one_row == value, two_row == value)
            hot[pl.ds(align(i * Rb, 16), Rb), :] = jnp.where(hit, 1.0, 0.0).astype(BF)

    def send_pair(c):
        return mix_bits(prime, s.NR - 1 - c // 2 - (s.NR // 2) * lax.rem(c, 2), pair_bits)

    build(send_pair(0))
    pl.semaphore_wait(
        barrier,
        s.PW + N - 1 + len(low_bits)
        + jnp.where(far == h, -1, s.bits - len(low_bits)).astype(jnp.int32),
    )

    def weight_copy(i, j):
        a, b = pairs[i]
        return remote(a, b.at[h], w_send.at[i, j], w_recv.at[i, j], w, lax.rem(h + j, N))

    for i in range(len(pairs)):
        for j in range(1, N):
            weight_copy(i, j).start()

    swap_d = Swap(s, snd_dy, dyr, d_send, d_recv, l_sem.at[0])
    swap_x = Swap(s, snd_x, x, x_send, x_recv, l_sem.at[1])
    swap_r = Swap(s, snd_dy, rg_all, r_send, r_recv, l_sem.at[2], True)
    swap_z = Swap(s, dyr, zall, z_send, z_recv, l_sem.at[3], True)

    def dispatch(first_row, buffer, swap, more):
        @pl.loop(0, s.NR)
        def _(c):
            pair = send_pair(c)
            rows = pl.ds(align(pair * RC, 16), RC)
            buffer[rows, :] = dot(hot[rows, :], quad[pl.ds(first_row, T), :]).astype(BF)
            for k in range(2):
                swap.start(pair * 2 + k)
            more(c)

    def build_next(c):
        @pl.when(c + 1 < s.NR)
        def _():
            build(send_pair(c + 1))

    load_dy.wait()
    dispatch(0, snd_dy, swap_d, build_next)
    pcol[...] = jnp.transpose(jnp.concatenate([prow] * 4, axis=0))

    load_tok.wait()
    for copy in owns[:3]:
        copy.wait()
    for i in range(3):
        for j in range(1, N):
            weight_copy(i, j).wait_recv()

    def moe_copy(c, j):
        part = quad.at[pl.ds(align(T + h * TL + c * CH, 16), CH)]
        return remote(part, part, m_send.at[c, j], m_recv.at[c, j], w, lax.rem(h + j, N))

    def moe_from(c, j):
        src = lax.rem(h + N - j, N)
        part = quad.at[pl.ds(align(T + src * TL + c * CH, 16), CH)]
        return remote(part, part, m_send.at[c, j], m_recv.at[c, j], w, src)

    lane = lax.broadcasted_iota(jnp.int32, (PATCHES, 2 * HEAD_DIM), 1)
    first = lane < HEAD_DIM

    def split_heads(part):
        zero = jnp.zeros_like(part)
        return jnp.concatenate([jnp.where(first, part, zero), jnp.where(first, zero, part)], axis=0)

    def join_heads(both):
        return jnp.where(first, both[:PATCHES], both[PATCHES:])

    @pl.loop(0, s.NCH)
    def _(c):
        rows = pl.ds(align(c * CH, 16), CH)
        t = tokv[rows, :].astype(F32)
        normed, _r = norm_parts(t)
        ain = (normed * g1[...] + b1[...]).astype(BF)
        ains[rows, :] = ain
        for j in range(N):
            cols = slice(j * L, (j + 1) * L)
            q = (dot(ain, wq[j, 0]) + qvb[j, 0:1, :]).astype(BF)
            qs[rows, cols] = q * BF(HEAD_DIM ** (-0.5))
            ks[rows, cols] = dot(ain, wq[j, 1]).astype(BF)
            vs[rows, cols] = (dot(ain, wq[j, 2]) + qvb[j, 1:2, :]).astype(BF)
        for m in range(s.IMG):
            image = pl.ds(align(c * CH + m * PATCHES, 16), PATCHES)
            for p in range(HP):
                cols = slice(2 * HEAD_DIM * p, 2 * HEAD_DIM * (p + 1))
                scores = dot_nt(split_heads(qs[image, cols]), ks[image, cols])
                top = jnp.max(scores, axis=-1, keepdims=True)
                grown = jnp.exp(scores - top)
                probs = (grown * (1.0 / jnp.sum(grown, axis=-1, keepdims=True))).astype(BF)
                ps[(c * s.IMG + m) * HP + p] = probs
                atts[image, cols] = join_heads(dot(probs, vs[image, cols])).astype(BF)
        residual = t + (dot(atts[rows, :], wp[...].reshape(D, D)) + pb[...])
        ress[rows, :] = residual
        normed, _r = norm_parts(residual)
        quad[pl.ds(align(T + h * TL + c * CH, 16), CH), :] = (normed * g2[...] + b2[...]).astype(BF)
        for j in range(1, N):
            moe_copy(c, j).start()

    @pl.loop(0, s.NCH)
    def _(c):
        for j in range(1, N):
            moe_from(c, j).wait_recv()

    dispatch(T, snd_x, swap_x, lambda c: None)

    @pl.loop(0, s.NCH)
    def _(c):
        for j in range(1, N):
            moe_copy(c, j).wait_send()

    for copy in owns[3:]:
        copy.wait()
    for i in range(len(pairs)):
        for j in range(1, N):
            if i >= 3:
                weight_copy(i, j).wait_recv()
            weight_copy(i, j).wait_send()

    @pl.loop(0, s.PW)
    def _(i):
        swap_d.wait_send(i)

    load_ags = pltpu.make_async_copy(cot.at[mine], ags, ld_sem.at[0])
    load_ags.start()
    per = FL // FC
    expert_lane = lax.broadcasted_iota(jnp.int32, (RC, E), 1)
    grt[...] = jnp.zeros(grt.shape, F32)

    def pg_rows(f):
        return pl.ds(align(f * s.ROWS, 16), s.ROWS)

    @pl.loop(0, s.NR)
    def _(c):
        pair = send_pair(c)
        rows = pl.ds(align(pair * RC, 16), RC)
        both = pl.ds(pair * 2, 2)
        for k in range(2):
            swap_d.wait_recv(pair * 2 + k)
            swap_x.wait_recv(pair * 2 + k)
        xr = x[both].reshape(RC, D)
        dyf = dyr[both].reshape(RC, D).astype(F32)
        logits = dot_nt(xr, wr[...])
        top = jnp.max(logits, axis=-1, keepdims=True)
        grown = jnp.exp(logits - top)
        probs = grown * (1.0 / jnp.sum(grown, axis=-1, keepdims=True))
        gate = jnp.sum(jnp.where(expert_lane == w, probs, 0.0), axis=-1, keepdims=True)
        og[rows, :] = (gate * dyf).astype(BF)
        ysum[...] = jnp.broadcast_to(db[...], (RC, D))
        rsum[...] = jnp.zeros((RC, D), F32)

        @pl.loop(0, NF)
        def _(f):
            j = f // per
            off = pl.ds(align(lax.rem(f, per) * FC, 128), FC)
            pre = dot(x[both].reshape(RC, D), up[j, :, off]) + ub[j, :, off]
            square = pre * pre
            t = jnp.tanh(GELU_C * (pre + GELU_A * (square * pre)))
            half = 0.5 * (1.0 + t)
            hidden = (pre * half).astype(BF)
            slope = half + (0.5 * GELU_C) * pre * (1.0 - t * t) * (1.0 + (3.0 * GELU_A) * square)
            grad = (dot_nt(og[rows, :], dn[j, off, :]) * slope).astype(BF)
            hot[rows, pl.ds(align(f * FC, 128), FC)] = hidden
            quad[pl.ds(align(f * s.ROWS + pair * RC, 16), RC), 0:FC] = grad
            ysum[...] += dot(hidden, dn[j, off, :])
            rsum[...] += dot_nt(grad, up[j, :, off])

        y = ysum[...].astype(BF).astype(F32)
        gate_grad = jnp.sum(dyf * y, axis=-1, keepdims=True)
        logit = (gate_grad * probs * (jnp.where(expert_lane == w, 1.0, 0.0) - gate)).astype(BF)
        back = (rsum[...] + dot(logit, wr[...])).astype(BF)
        snd_dy[rows, :] = back
        for k in range(2):
            swap_r.start(pair * 2 + k)
        zz = (gate * y).astype(BF)
        for k in range(2):
            dyr[pair * 2 + k] = zz[k * Rb : (k + 1) * Rb]

            @pl.when(lax.rem(c, 2) == 1)
            def _():
                swap_z.start(pair * 2 + k)

        grt[...] += dot_tn(logit, xr)

    def z_far(point):
        count = s.PW // 2
        for n in range(point * count // 4, (point + 1) * count // 4):
            swap_z.start(send_pair(2 * (n // 2)) * 2 + n % 2)

    def n_copy(i, j):
        a, b = ((us, ur), (ds_, dr))[i]
        return remote(a.at[j - 1], b.at[j - 1], wn_send.at[i, j], wn_recv.at[i, j], w, lax.rem(h + j, N))

    def b_copy(j, slab):
        return remote(bs.at[j - 1], br.at[slab], wn_send.at[2, j], wn_recv.at[2, j], w, lax.rem(h + j, N))

    def hid_cols(owner, c):
        return pl.ds(align((owner * per + c) * FC, 128), FC)

    def up_part(owner, c):
        return dot_tn(x[...].reshape(s.ROWS, D), quad[pg_rows(owner * per + c), 0:FC])

    def down_part(owner, c):
        return dot_tn(hot[:, hid_cols(owner, c)], og[...])

    def pg_sum(owner, c):
        return jnp.sum(quad[pg_rows(owner * per + c), 0:FC].astype(F32), axis=0, keepdims=True)

    og_sum = jnp.sum(og[...].astype(F32), axis=0, keepdims=True)
    span = min(FL, D)

    def put_bias(ref):
        for b in range(D // span):
            ref[1 + b : 2 + b, 0:span] = og_sum[:, b * span : (b + 1) * span]

    for j in range(1, N):
        owner = lax.rem(h + j, N)
        for c in range(per):
            cols = slice(c * FC, (c + 1) * FC)
            us[j - 1, :, cols] = up_part(owner, c).astype(BF)
        n_copy(0, j).start()
        for c in range(per):
            cols = slice(c * FC, (c + 1) * FC)
            ds_[j - 1, cols, :] = down_part(owner, c).astype(BF)
        n_copy(1, j).start()
        for c in range(per):
            cols = slice(c * FC, (c + 1) * FC)
            bs[j - 1, 0:1, cols] = pg_sum(owner, c)
        put_bias(bs.at[j - 1])
        b_copy(j, h).start()
    def go_copy(i, c):
        cols = pl.ds(c * FC, FC)
        if i == 0:
            return pltpu.make_async_copy(stage.at[c, :, pl.ds(0, FC)], gu_out.at[:, cols], go_sem.at[c])
        return pltpu.make_async_copy(stage.at[c, pl.ds(0, FC), :], gd_out.at[cols, :], go_sem.at[c])

    for c in range(per):
        cols = slice(c * FC, (c + 1) * FC)
        total = up_part(h, c)
        for j in range(1, N):
            if c == 0:
                n_copy(0, j).wait_recv()
            total += ur[j - 1, :, cols].astype(F32)
        stage[c, :, 0:FC] = total.astype(BF)
        go_copy(0, c).start()
        gub_out[:, cols] = pg_sum(h, c)
    for c in range(per):
        cols = slice(c * FC, (c + 1) * FC)
        total = down_part(h, c)
        for j in range(1, N):
            if c == 0:
                n_copy(1, j).wait_recv()
            total += dr[j - 1, cols, :].astype(F32)
        go_copy(0, c).wait()
        stage[c, 0:FC, :] = total.astype(BF)
        go_copy(1, c).start()
    put_bias(br.at[h])

    z_far(0)

    def pass_on(buffer, send, recv, i, j, src=None):
        part = buffer.at[h if src is None else src, i]
        return remote(part, part, send.at[i, j], recv.at[i, j], w, lax.rem(h + j, N) if src is None else src)

    @pl.loop(0, s.PW)
    def _(c):
        i = mix_bits(slot, s.PW - 1 - c, pair_bits + 1)
        swap_r.wait_recv(i)
        for j in range(1, N):
            pass_on(rg_all, rf_send, rf_recv, i, j).start()


    for j in range(1, N):
        src = lax.rem(h + N - j, N)
        b_copy(j, src).wait_recv()
        gub_out[...] += br[src, 0:1, :]
    for b in range(D // span):
        gdb_out[:, b * span : (b + 1) * span] = sum(br[j, 1 + b : 2 + b, 0:span] for j in range(N))

    @pl.loop(0, s.PW)
    def _(i):
        for j in range(1, N):
            pass_on(rg_all, rf_send, rf_recv, i, j, lax.rem(h + N - j, N)).wait_recv()

    def spots(c):
        rows = pl.ds(align(h * TL + c * CH, 16), CH)
        hit = jnp.logical_or(pcol[rows, 0:1] == svals[...], pcol[rows, 1:2] == svals[...])
        return jnp.where(hit, 1.0, 0.0).astype(BF)

    small[...] = jnp.zeros(small.shape, F32)
    small[0:E, :] = grt[...]

    def add_row(r, value):
        small[r : r + 1, :] += jnp.sum(value, axis=0, keepdims=True)

    z_far(1)
    load_ags.wait()

    @pl.loop(0, s.PW)
    def _(i):
        swap_x.wait_send(i)

    @pl.loop(0, s.NCH)
    def _(c):
        rows = pl.ds(align(c * CH, 16), CH)
        moe_grad = dot(spots(c), rg_all[...].reshape(E * Rb, D))
        normed, inv = norm_parts(ress[rows, :])
        add_row(E + 2, moe_grad * normed)
        add_row(E + 3, moe_grad)
        total = ags[rows, :].astype(F32) + norm_pull(moe_grad, normed, inv, g2[...])
        rgrad[rows, :] = total
        ag = total.astype(BF)
        ags[rows, :] = ag
        add_row(E + 4, ag.astype(F32))
        snd_x[rows, :] = dot_nt(ag, wp[...].reshape(D, D)).astype(BF)

    def attend_back(part, start, stop):
        heads = range(part, HP, s.halves)

        @pl.loop(start, stop)
        def _(c):
            for m in range(s.IMG):
                image = pl.ds(align(c * CH + m * PATCHES, 16), PATCHES)
                for p in heads:
                    cols = slice(2 * HEAD_DIM * p, 2 * HEAD_DIM * (p + 1))
                    both = split_heads(snd_x[image, cols])
                    low = ps[(c * s.IMG + m) * HP + p]
                    probs = low.astype(F32)
                    q, k, v = qs[image, cols], ks[image, cols], vs[image, cols]
                    pgrad = dot_nt(both, v)
                    sgrad = (probs * (pgrad - jnp.sum(pgrad * probs, axis=-1, keepdims=True))).astype(BF)
                    qs[image, cols] = join_heads(dot(sgrad, k) * (HEAD_DIM ** (-0.5))).astype(BF)
                    ks[image, cols] = dot_tn(sgrad, split_heads(q)).astype(BF)
                    vs[image, cols] = dot_tn(low, both).astype(BF)

    class Job:
        def __init__(self, n):
            self.n, self.rows, self.streams = n, s.jobs[n], s.streams[n]
            self.gsend, self.gnar, self.gown, self.rbuf, self.gfin = job_refs[n]
            self.sbuf = self.gsend.at[0]

        def n_copy(self, rel, narrow_place):
            return remote(
                self.gsend.at[rel], self.gnar.at[rel], n_send.at[self.n, rel], n_recv.at[self.n, rel], w, narrow_place
            )

        def begin(self):
            LW = s.LW
            for j in range(N):
                at = j * L + self.n * LW
                cols = slice(at, at + LW)
                parts = [(i * D, dot_tn(ains[...], dd[:, cols])) for i, dd in enumerate((qs, ks, vs))]
                if self.n == 0:
                    lower = dot_tn(atts[:, j * L : (j + 1) * L], ags[...])
                    for b in range(D // LW):
                        parts.append((3 * D + b * L, lower[:, b * LW : (b + 1) * LW]))

                def put(ref, cast, parts=parts):
                    for r, value in parts:
                        ref[r : r + value.shape[0], :] = value.astype(cast)

                @pl.when(h == j)
                def _():
                    put(self.gown, F32)

                @pl.when(h != j)
                def _():
                    rel = lax.rem(j - h + N, N) - 1
                    put(self.gsend.at[rel], BF)
                    self.n_copy(rel, j).start()

        def join(self):
            for j in range(1, N):
                self.n_copy(j - 1, lax.rem(h + N - j, N)).wait_recv()
                self.gown[...] += self.gnar[j - 1].astype(F32)
            for j in range(1, N):
                self.n_copy(j - 1, lax.rem(h + j, N)).wait_send()

        def segment(self, t, k):
            start, size, order = self.streams[t]
            first_row = start
            for step in range(k):
                size = size // 2
                first_row = first_row + bit_of(order[step]) * size
            return first_row, size

        def halves(self, t, k):
            start, size = self.segment(t, k)
            bit = self.streams[t][2][k]
            half = size // 2
            keep = align(start + bit_of(bit) * half, 16)
            give = align(start + (1 - bit_of(bit)) * half, 16)
            return pl.ds(keep, half), pl.ds(give, half), flip(w, 1 << bit)

        def fold(self, t, k, land):
            keep, give, partner = self.halves(t, k)
            return remote(
                self.sbuf.at[give], self.rbuf.at[keep if land else give],
                h_send.at[self.n, t, k], h_recv.at[self.n, t, k], partner, h,
            )

        def grow(self, t, k, land):
            keep, give, partner = self.halves(t, k)
            return remote(
                self.gfin.at[keep], self.gfin.at[keep if land else give],
                a_send.at[self.n, t, k], a_recv.at[self.n, t, k], partner, h,
            )

        def start(self, q):
            for t in range(len(self.streams)):
                if q < s.bits:
                    _k, give, _p = self.halves(t, q)
                    self.sbuf[give, :] = self.gown[give, :].astype(BF)
                    self.fold(t, q, True).start()
                else:
                    if q == s.bits:
                        start, size = self.segment(t, s.bits)
                        rows = pl.ds(align(start, 16), size)
                        self.gfin[rows, :] = self.gown[rows, :].astype(BF)
                    self.grow(t, 2 * s.bits - 1 - q, True).start()

        def end(self, q):
            for t in range(len(self.streams)):
                if q < s.bits:
                    keep, give, _p = self.halves(t, q)
                    self.fold(t, q, False).wait()
                    self.gown[keep, :] += self.rbuf[give, :].astype(F32)
                else:
                    self.grow(t, 2 * s.bits - 1 - q, False).wait()

        def finish(self):
            return pltpu.make_async_copy(self.gfin, gbigs[self.n], fin_sem.at[self.n])

    def bit_of(b):
        return lax.rem(w // (1 << b), 2)

    def s_copy(k):
        return remote(sacc.at[k], srec.at[k], s_send.at[k], s_recv.at[k], flip(w, 1 << k), h)

    def tok_copy(src, dst, send, recv, c, j):
        here = pl.ds(align(c * CH, 16), CH)
        there = pl.ds(align(h * TL + c * CH, 16), CH)
        return remote(src.at[here], dst.at[there], send.at[c, j], recv.at[c, j], w, lax.rem(h + j, N))

    def tok_local(src, dst, sem, c):
        here = pl.ds(align(c * CH, 16), CH)
        there = pl.ds(align(h * TL + c * CH, 16), CH)
        return pltpu.make_async_copy(src.at[here], dst.at[there], sem.at[c])

    def first_norm_back():
        small[E + 5 : E + 6, :] = jnp.sum(qs[...].astype(F32), axis=0, keepdims=True)
        small[E + 6 : E + 7, :] = jnp.sum(vs[...].astype(F32), axis=0, keepdims=True)

        @pl.loop(0, s.NCH)
        def _(c):
            rows = pl.ds(align(c * CH, 16), CH)
            back = jnp.zeros((CH, D), F32)
            for j in range(N):
                cols = slice(j * L, (j + 1) * L)
                for i, dd in enumerate((qs, ks, vs)):
                    back += dot_nt(dd[rows, cols], wq[j, i])
            normed, inv = norm_parts(tokv[rows, :].astype(F32))
            add_row(E, back * normed)
            add_row(E + 1, back)
            ags[rows, :] = (rgrad[rows, :] + norm_pull(back, normed, inv, g1[...])).astype(BF)
            for j in range(1, N):
                tok_copy(ags, gtok, g_send, g_recv, c, j).start()
            tok_local(ags, gtok, g_loc, c).start()

        for b in range(D // 128):
            snar[h, b * s.RP : (b + 1) * s.RP, :] = small[:, b * 128 : (b + 1) * 128]
        for j in range(1, N):
            remote(snar.at[h], snar.at[h], sn_send.at[j], sn_recv.at[j], w, lax.rem(h + j, N)).start()

    def combine_pass():
        @pl.loop(0, s.PW)
        def _(c):
            i = mix_bits(slot, c, pair_bits + 1)
            swap_z.wait_recv(i)
            for j in range(1, N):
                pass_on(zall, zf_send, zf_recv, i, j).start()

    def combine_wait():
        @pl.loop(0, s.PW)
        def _(i):
            for j in range(1, N):
                pass_on(zall, zf_send, zf_recv, i, j, lax.rem(h + N - j, N)).wait_recv()

    def combine(start, stop):
        @pl.loop(start, stop)
        def _(c):
            rows = pl.ds(align(c * CH, 16), CH)
            mixed = dot(spots(c), zall[...].reshape(E * Rb, D))
            ains[rows, :] = (ress[rows, :] + mixed).astype(BF)
            for j in range(1, N):
                tok_copy(ains, out, o_send, o_recv, c, j).start()
            tok_local(ains, out, o_loc, c).start()

    def small_narrow():
        for j in range(1, N):
            src = lax.rem(h + N - j, N)
            remote(snar.at[h], snar.at[h], sn_send.at[j], sn_recv.at[j], w, src).wait_send()
            remote(snar.at[src], snar.at[src], sn_send.at[j], sn_recv.at[j], w, src).wait_recv()
        sacc[0] = sum(snar[j] for j in range(N))

    z_far(2)
    jobs = [Job(n) for n in range(NJ)]
    steps = 2 * s.bits
    attend_back(0, 0, s.NCH)
    z_far(3)
    jobs[0].begin()
    if NJ == 2:
        middle = s.NCH // 2
        attend_back(1, 0, middle)
        jobs[0].join()
        jobs[0].start(0)
        attend_back(1, middle, s.NCH)
        jobs[1].begin()
        jobs[0].end(0)
        jobs[0].start(1)
        jobs[1].join()
        jobs[1].start(0)
        at = [1, 0]
    else:
        jobs[0].join()
        jobs[0].start(0)
        at = [0]
    turn, little = 0, 0
    while min(at) < steps:
        if turn == 0:
            first_norm_back()
        if turn == 1:
            small_narrow()
        if turn == s.bits - 1:
            combine_pass()
        if turn == s.bits:
            combine_wait()
            combine(0, s.NCH // 2)
        if turn == s.bits + 1:
            combine(s.NCH // 2, s.NCH)
        if turn >= 2 and little < s.bits:
            if little:
                s_copy(little - 1).wait()
                sacc[little] = sacc[little - 1] + srec[little - 1]
            s_copy(little).start()
            little += 1
        for n in range(NJ):
            if at[n] < steps:
                jobs[n].end(at[n])
                at[n] += 1
                if at[n] < steps:
                    jobs[n].start(at[n])
                else:
                    jobs[n].finish().start()
        turn += 1
    s_copy(s.bits - 1).wait()
    gsmall[...] = sacc[s.bits - 1] + srec[s.bits - 1]

    for j in range(1, N):
        for i in range(2):
            n_copy(i, j).wait_send()
        b_copy(j, h).wait_send()

    @pl.loop(0, s.PW)
    def _(i):
        swap_r.wait_send(i)
        swap_z.wait_send(i)
        for j in range(1, N):
            pass_on(rg_all, rf_send, rf_recv, i, j).wait_send()
            pass_on(zall, zf_send, zf_recv, i, j).wait_send()

    @pl.loop(0, s.NCH)
    def _(c):
        tok_local(ags, gtok, g_loc, c).wait()
        tok_local(ains, out, o_loc, c).wait()
        here = pl.ds(align(c * CH, 16), CH)
        for j in range(1, N):
            src = lax.rem(h + N - j, N)
            there = pl.ds(align(src * TL + c * CH, 16), CH)
            tok_copy(ags, gtok, g_send, g_recv, c, j).wait_send()
            tok_copy(ains, out, o_send, o_recv, c, j).wait_send()
            remote(ags.at[here], gtok.at[there], g_send.at[c, j], g_recv.at[c, j], w, src).wait_recv()
            remote(ains.at[here], out.at[there], o_send.at[c, j], o_recv.at[c, j], w, src).wait_recv()

    for c in range(per):
        go_copy(1, c).wait()
    for job in jobs:
        job.finish().wait()


def post_kernel(s, *refs):
    (
        out_in, gtok_in, gu_in, gd_in, flat, *rest,
    ) = refs
    bigs, rest = rest[: len(s.jobs)], rest[len(s.jobs) :]
    (
        out, gtok, gu, gd, gqkv, gproj, gag, gas, gmg, gms, gpb, gqv, grouter,
        b_out, b_tok, b_gu, b_gd, f_tok, f_gu, f_gd, l_sem, s_sem,
    ) = rest
    moves = (
        (gtok_in, b_tok, f_tok, gtok), (gu_in, b_gu, f_gu, gu), (gd_in, b_gd, f_gd, gd), (out_in, b_out, b_out, out),
    )
    loads, stores, widen = [], [], []
    for i, (a, b, f, c) in enumerate(moves):
        step = a.shape[0] // PARTS
        for p in range(PARTS):
            part = pl.ds(p * step, step)
            loads.append(pltpu.make_async_copy(a.at[part], b.at[part], l_sem.at[i, p]))
            stores.append(pltpu.make_async_copy(f.at[part], c.at[part], s_sem.at[i, p]))
            widen.append((b, f, slice(p * step, (p + 1) * step)))
    for load in loads:
        load.start()
    D, L, N, E, LW = s.D, s.L, s.N, s.E, s.LW
    h = lax.axis_index("narrow")
    for load, store, (b, f, part) in zip(loads, stores, widen):
        load.wait()
        if b is not f:
            f[part, :] = b[part, :].astype(F32)
        store.start()
    for n, big in enumerate(bigs):
        for i in range(3):
            gqkv[i, :, n * LW : (n + 1) * LW] = big[i * D : (i + 1) * D, :].astype(F32)
    for b in range(D // LW):
        gproj[:, b * LW : (b + 1) * LW] = bigs[0][3 * D + b * L : 3 * D + (b + 1) * L, :].astype(F32)

    def rows(r, count):
        return jnp.concatenate([flat[b * s.RP + r : b * s.RP + r + count, :] for b in range(D // 128)], axis=1)

    grouter[...] = rows(0, E)
    for r, ref in ((E, gag), (E + 1, gas), (E + 2, gmg), (E + 3, gms), (E + 4, gpb)):
        ref[...] = rows(r, 1)
    qv = rows(E + 5, 2)
    for j in range(N):

        @pl.when(h == j)
        def _():
            gqv[...] = qv[:, j * L : (j + 1) * L]

    for store in stores:
        store.wait()


VM = pl.BlockSpec(memory_space=pltpu.VMEM)
ANY = pl.BlockSpec(memory_space=pl.ANY)
HB = pl.BlockSpec(memory_space=pltpu.HBM)
DMA = pltpu.SemaphoreType.DMA
V = pltpu.VMEM


def shards(
    wide,
    narrow,
    tokens,
    attn_gain,
    attn_shift,
    qkv_weight,
    query_value_bias,
    proj_weight,
    proj_bias,
    moe_gain,
    moe_shift,
    router_weight,
    expert_up,
    expert_up_bias,
    expert_down,
    expert_down_bias,
    routes,
    slot_index,
    cotangent,
):
    s = Sizes(wide, narrow, tokens.shape[0], tokens.shape[1], router_weight.shape[1], expert_up.shape[2])
    T, D, E, N, W, L, TL = s.T, s.D, s.E, s.N, s.W, s.L, s.TL
    PW, Rb, FL, ROWS, RC, NCH = s.PW, s.Rb, s.FL, s.ROWS, s.RC, s.NCH
    slot = np.arange(E * Rb)
    half, rest = slot // (PW * Rb), slot % (PW * Rb)
    pos, inner = rest // Rb, rest % Rb
    svals = np.where(inner < s.cap, (pos * N + half) * s.cap + inner, -2).astype(np.int32)[None, :]
    row = lambda a: a.reshape(1, -1)
    blk = (PW, Rb, D)
    heads = (TL // PATCHES) * s.HP
    NS = 3
    ins = [
        (ANY, tokens), (ANY, cotangent), (VM, row(attn_gain)), (VM, row(attn_shift)),
        (ANY, qkv_weight.transpose(1, 0, 2)), (ANY, query_value_bias), (ANY, proj_weight), (VM, row(proj_bias)),
        (VM, row(moe_gain)), (VM, row(moe_shift)), (VM, router_weight.T), (ANY, expert_up[0]),
        (ANY, expert_up_bias), (ANY, expert_down[0]), (VM, expert_down_bias), (VM, routes.T), (VM, slot_index.T),
        (VM, jnp.asarray(svals)),
    ]
    outs = [
        (ANY, (T, D), BF), (ANY, (T, D), BF), (VM, (s.RPS, 128), F32),
        (ANY, (D, FL), BF), (ANY, (FL, D), BF), (VM, (1, FL), F32), (VM, (1, D), F32),
    ] + [(ANY, (r, s.LW), BF) for r in s.jobs]
    scratch = [
        V((TL, D), BF), V((N, 3, D, L), BF), V((N, L, D), BF), V((N, 2, L), F32), V((T, 8), jnp.int32),
        V((ROWS, T), BF), V((2 * T, D), BF), V((TL, D), BF), V((TL, D), BF), V((TL, D), BF),
        V((heads, 2 * PATCHES, PATCHES), BF), V((TL, D), BF), V((TL, D), BF), V((TL, D), F32), V((ROWS, D), BF), V((ROWS, D), BF),
        V(blk, BF), V(blk, BF), V((N, D, FL), BF), V((N, FL, D), BF), V((N, 1, FL), F32), V((ROWS, D), BF),
        V((RC, D), F32), V((RC, D), F32), V((N - 1, D, FL), BF), V((N - 1, FL, D), BF), V((N - 1, D, FL), BF),
        V((N - 1, FL, D), BF), V((N - 1, 8, FL), F32), V((N, 8, FL), F32), V((FL // s.FC, D, D), BF),
        V((E, D), F32),
        V((N,) + blk, BF), V((N,) + blk, BF), V((TL, D), BF), V((TL, D), F32),
        V((s.RP, D), F32), V((N, s.RPS, 128), F32), V((s.bits, s.RPS, 128), F32), V((s.bits, s.RPS, 128), F32),
    ]
    for r in s.jobs:
        scratch += [V((N - 1, r, s.LW), BF), V((N - 1, r, s.LW), BF), V((r, s.LW), F32)]
        scratch += [V((r, s.LW), BF), V((r, s.LW), BF)]
    NJ = len(s.jobs)
    scratch += [
        DMA((2,)), DMA((6,)), DMA((6, N)), DMA((6, N)), DMA((NCH, N)), DMA((NCH, N)),
        DMA((PW,)), DMA((PW,)), DMA((PW,)), DMA((PW,)), DMA((PW,)), DMA((PW,)),
        DMA((PW,)), DMA((PW,)), DMA((4,)), DMA((PW, N)), DMA((PW, N)), DMA((PW, N)), DMA((PW, N)),
        DMA((3, N)), DMA((3, N)), DMA((FL // s.FC,)),
        DMA((NJ, N)), DMA((NJ, N)), DMA((N,)), DMA((N,)), DMA((NJ, NS, s.bits)), DMA((NJ, NS, s.bits)),
        DMA((NJ, NS, s.bits)), DMA((NJ, NS, s.bits)), DMA((s.bits,)), DMA((s.bits,)),
        DMA((NCH, N)), DMA((NCH, N)), DMA((NCH, N)), DMA((NCH, N)), DMA((NCH,)), DMA((NCH,)), DMA((NJ,)),
    ]
    out, gtok, gsmall, gu, gd, gub, gdb, *gbigs = pl.pallas_call(
        functools.partial(block_kernel, s),
        in_specs=[spec for spec, _ in ins],
        out_specs=[spec for spec, _, _ in outs],
        out_shape=[jax.ShapeDtypeStruct(shape, dtype) for _, shape, dtype in outs],
        scratch_shapes=scratch,
        compiler_params=pltpu.CompilerParams(
            collective_id=1, has_side_effects=True, vmem_limit_bytes=VMEM_MB << 20
        ),
        name="block",
    )(*[a for _, a in ins])

    post_ins = [(HB, out), (HB, gtok), (HB, gu), (HB, gd), (VM, gsmall)]
    post_ins += [(VM, a) for a in gbigs]
    post_outs = [
        (ANY, (T, D), BF), (ANY, (T, D), F32), (ANY, (D, FL), F32), (ANY, (FL, D), F32), (VM, (3, D, L), F32),
        (VM, (L, D), F32), (VM, (1, D), F32), (VM, (1, D), F32), (VM, (1, D), F32), (VM, (1, D), F32),
        (VM, (1, D), F32), (VM, (2, L), F32), (VM, (E, D), F32),
    ]
    out, gtok, gu, gd, gqkv, gproj, gag, gas, gmg, gms, gpb, gqv, grouter = pl.pallas_call(
        functools.partial(post_kernel, s),
        in_specs=[spec for spec, _ in post_ins],
        out_specs=[spec for spec, _, _ in post_outs],
        out_shape=[jax.ShapeDtypeStruct(shape, dtype) for _, shape, dtype in post_outs],
        scratch_shapes=[
            V((T, D), BF), V((T, D), BF), V((D, FL), BF), V((FL, D), BF), V((T, D), F32), V((D, FL), F32),
            V((FL, D), F32), DMA((4, PARTS)), DMA((4, PARTS)),
        ],
        compiler_params=pltpu.CompilerParams(vmem_limit_bytes=VMEM_MB << 20),
        name="post",
    )(*[a for _, a in post_ins])
    return (
        out,
        gtok,
        gag.reshape(D),
        gas.reshape(D),
        gqkv.transpose(1, 0, 2),
        gqv,
        gproj,
        gpb.reshape(D),
        gmg.reshape(D),
        gms.reshape(D),
        grouter.T,
        gu[None],
        gub,
        gd[None],
        gdb,
    )


def solution(mesh):
    in_specs = (
        P("wide", None),
        P(),
        P(),
        P(None, None, "narrow"),
        P(None, "narrow"),
        P("narrow", None),
        P(),
        P(),
        P(),
        P(),
        P("wide", None, "narrow"),
        P("wide", "narrow"),
        P("wide", "narrow", None),
        P("wide", None),
        P("wide", None),
        P("wide", None),
        P("wide", None),
    )
    out_specs = (
        P("wide", None),
        P("wide", None),
        P(),
        P(),
        P(None, None, "narrow"),
        P(None, "narrow"),
        P("narrow", None),
        P(),
        P(),
        P(),
        P(),
        P("wide", None, "narrow"),
        P("wide", "narrow"),
        P("wide", "narrow", None),
        P("wide", None),
    )
    body = functools.partial(shards, mesh.shape["wide"], mesh.shape["narrow"])
    return jax.shard_map(body, mesh=mesh, in_specs=in_specs, out_specs=out_specs, check_vma=False)
```

```python
import functools

import jax
import jax.numpy as jnp
import numpy as np
from jax import lax
from jax.experimental import pallas as pl
from jax.experimental.pallas import tpu as pltpu
from jax.sharding import PartitionSpec as P

PATCHES = 144
HEAD_DIM = 64
EPSILON = 1e-06
MESH = pl.DeviceIdType.MESH
BF = jnp.bfloat16
F32 = jnp.float32
GELU_C = 0.7978845608028654
GELU_A = 0.044715
VMEM_MB = 63
PARTS = 2
DEPTH = 4
LN_TURNS = 4
MIX_TURN = 4


def dot(a, b):
    return jnp.dot(a, b, preferred_element_type=F32)


def dot_nt(a, b):
    return lax.dot_general(a, b, (((1,), (1,)), ((), ())), preferred_element_type=F32)


def dot_tn(a, b):
    return lax.dot_general(a, b, (((0,), (0,)), ((), ())), preferred_element_type=F32)


def norm_parts(values):
    center = values - jnp.mean(values, axis=-1, keepdims=True)
    inv_root = lax.rsqrt(jnp.mean(center * center, axis=-1, keepdims=True) + EPSILON)
    return center * inv_root, inv_root


def norm_pull(upstream, normed, inv_root, norm_gain):
    scaled = upstream * norm_gain
    bracket = (
        scaled
        - jnp.mean(scaled, axis=-1, keepdims=True)
        - normed * jnp.mean(scaled * normed, axis=-1, keepdims=True)
    )
    return inv_root * bracket


class Sizes:
    def __init__(self, wide, narrow, tokens, width, experts, local_ff):
        self.W, self.N = wide, narrow
        self.T, self.D, self.E = tokens, width, experts
        self.TL = tokens // narrow
        self.cap = tokens // experts
        self.PW = wide // narrow
        self.Rb = -(-self.cap // 16) * 16
        self.L = width // narrow
        self.FL = local_ff
        self.CH = 2 * PATCHES
        self.NCH = self.TL // self.CH
        self.IMG = self.CH // PATCHES
        self.HP = width // (2 * HEAD_DIM)
        self.ROWS = self.PW * self.Rb
        self.RC = 2 * self.Rb
        self.PC = 3 if self.Rb % 48 == 0 else 1
        self.ZP = self.PW // 2 * self.PC
        self.NR = self.PW // 2
        self.FC = min(512, local_ff)
        self.NF = narrow * local_ff // self.FC
        self.LW = min(128, self.L)
        self.halves = 2 if self.L == 256 else 1
        first = 3 * width + width // self.LW * self.L
        self.jobs = [first, 3 * width][: self.halves]
        self.RP = -(-(experts + 7) // 8) * 8
        self.RPS = self.RP * (width // 128)
        self.bits = wide.bit_length() - 1
        self.streams = [self.cut(rows, wide, j) for j, rows in enumerate(self.jobs)]

    def cut(self, rows, wide, job):
        unit = 16 * wide
        units, count = rows // unit, 3
        streams, start = [], 0
        for t in range(count):
            size = -(-(units - start) // (count - t))
            if size:
                low = list(range(min(3, self.bits)))
                order = low[t:] + low[:t] + list(range(len(low), self.bits))
                streams.append((start * unit, size * unit, order))
                start += size
        return streams


def place():
    return lax.axis_index("wide"), lax.axis_index("narrow")


def signal(sem, wide, narrow):
    pl.semaphore_signal(sem, 1, device_id=(wide, narrow), device_id_type=MESH)


def remote(src, dst, send, recv, wide, narrow):
    return pltpu.make_async_remote_copy(
        src, dst, send, recv, device_id=(wide, narrow), device_id_type=MESH
    )


class Swap:
    def __init__(self, s, src, dst, send, recv, local, half=False):
        self.s, self.src = s, src
        self.send, self.recv, self.local = send, recv, local
        w, h = place()
        self.w, self.h = w, h
        self.far = lax.rem(w, s.N)
        self.slot = w // s.N
        self.dst = dst.at[self.far] if half else dst
        self.land = dst.at[h] if half else dst

    def at(self, i):
        if len(self.src.shape) == 2:
            return self.src.at[pl.ds(align(i * self.s.Rb, 16), self.s.Rb)]
        return self.src.at[i]

    def own(self, i):
        return jnp.logical_and(self.far == self.h, i == self.slot)

    def start(self, i):
        @pl.when(jnp.logical_not(self.own(i)))
        def _():
            remote(
                self.at(i),
                self.dst.at[self.slot],
                self.send.at[i],
                self.recv.at[self.slot],
                i * self.s.N + self.h,
                self.far,
            ).start()

        @pl.when(self.own(i))
        def _():
            pltpu.make_async_copy(self.at(i), self.dst.at[self.slot], self.local).start()

    def there(self, i):
        return remote(
            self.at(i),
            self.land.at[i],
            self.send.at[i],
            self.recv.at[i],
            i * self.s.N + self.h,
            self.far,
        )

    def wait_send(self, i):
        @pl.when(jnp.logical_not(self.own(i)))
        def _():
            self.there(i).wait_send()

    def wait_recv(self, i):
        @pl.when(jnp.logical_not(self.own(i)))
        def _():
            self.there(i).wait_recv()

        @pl.when(self.own(i))
        def _():
            pltpu.make_async_copy(self.at(i), self.land.at[i], self.local).wait()


def flip(value, bit):
    return value + bit * (1 - 2 * lax.rem(value // bit, 2))


def mix_bits(value, other, count):
    total = 0
    for b in range(count):
        p, q = lax.rem(value // (1 << b), 2), lax.rem(other // (1 << b), 2)
        total = total + (p + q - 2 * p * q) * (1 << b)
    return total


def align(x, m):
    return pl.multiple_of(x, m)


def block_kernel(s, *refs):
    (
        tok, cot, g1, b1, wq_loc, qvb_loc, wp_loc, pb, g2, b2, wr, up_loc, ub_loc, dn_loc, db,
        routes, slots, svals,
        out, gtok, gsmall, gu_out, gd_out, gub_out, gdb_out, *rest,
    ) = refs
    gbigs, rest = rest[: len(s.jobs)], rest[len(s.jobs) :]
    (
        tokv, wq, wp, qvb, pcol, hot, quad, qs, ks, vs, ps, atts, ains, ress, snd_x, snd_dy,
        x, dyr, up, dn, ub, og, ysum, rsum, us, ds_, ur, dr, bs, br, stage, grt,
        rg_all, zall, ags, rgrad, small, snar, sacc, srec, *more,
    ) = rest
    NJ = len(s.jobs)
    job_refs = [more[5 * n : 5 * n + 5] for n in range(NJ)]
    (
        ld_sem, own_sem, w_send, w_recv, m_send, m_recv, x_send, x_recv, d_send, d_recv, r_send, r_recv,
        z_send, z_recv, zp_send, zp_recv, l_sem, rf_send, rf_recv, zf_send, zf_recv, wn_send, wn_recv, go_sem,
        n_send, n_recv, sn_send, sn_recv, h_send, h_recv, a_send, a_recv, s_send, s_recv,
        o_send, o_recv, g_send, g_recv, o_loc, g_loc, fin_sem,
    ) = more[5 * NJ :]
    w, h = place()
    N, W, T, TL, CH, L, D, E = s.N, s.W, s.T, s.TL, s.CH, s.L, s.D, s.E
    RC, FC, FL, HP, Rb, NF = s.RC, s.FC, s.FL, s.HP, s.Rb, s.NF
    far = lax.rem(w, N)
    slot = w // N
    prime = slot // 2
    pair_bits = s.NR.bit_length() - 1

    barrier = pltpu.get_barrier_semaphore()

    @pl.loop(0, s.PW)
    def _(i):
        @pl.when(jnp.logical_or(far != h, i != slot))
        def _():
            signal(barrier, i * N + h, far)

    for j in range(1, N):
        signal(barrier, w, lax.rem(h + j, N))
    low_bits = [b for b in range(s.bits) if (1 << b) < N]
    for b in range(s.bits):
        if b in low_bits:
            signal(barrier, flip(w, 1 << b), h)
        else:

            @pl.when(far != h)
            def _():
                signal(barrier, flip(w, 1 << b), h)

    mine = pl.ds(align(h * TL, 16), TL)
    load_dy = pltpu.make_async_copy(cot, quad.at[pl.ds(0, T)], ld_sem.at[0])
    load_tok = pltpu.make_async_copy(tok.at[mine], tokv, ld_sem.at[1])
    load_dy.start()
    load_tok.start()
    pairs = ((wq_loc, wq), (wp_loc, wp), (qvb_loc, qvb), (up_loc, up), (dn_loc, dn), (ub_loc, ub))
    owns = [pltpu.make_async_copy(a, b.at[h], own_sem.at[i]) for i, (a, b) in enumerate(pairs)]
    for copy in owns:
        copy.start()

    slot_rows = slots[...]
    prow = jnp.where(slot_rows < s.cap, routes[...] * s.cap + slot_rows, -1)
    one_row, two_row = prow[0:1, :], prow[1:2, :]

    def build(pair):
        for k in range(2):
            i = pair * 2 + k
            row = lax.broadcasted_iota(jnp.int32, (Rb, 1), 0)
            value = jnp.where(row < s.cap, (i * N + h) * s.cap + row, -2)
            hit = jnp.logical_or(one_row == value, two_row == value)
            hot[pl.ds(align(i * Rb, 16), Rb), :] = jnp.where(hit, 1.0, 0.0).astype(BF)

    def send_pair(c):
        return mix_bits(prime, s.NR - 1 - c // 2 - (s.NR // 2) * lax.rem(c, 2), pair_bits)

    build(send_pair(0))
    pl.semaphore_wait(
        barrier,
        s.PW + N - 1 + len(low_bits)
        + jnp.where(far == h, -1, s.bits - len(low_bits)).astype(jnp.int32),
    )

    def weight_copy(i, j):
        a, b = pairs[i]
        return remote(a, b.at[h], w_send.at[i, j], w_recv.at[i, j], w, lax.rem(h + j, N))

    for i in range(len(pairs)):
        for j in range(1, N):
            weight_copy(i, j).start()

    swap_d = Swap(s, snd_dy, dyr, d_send, d_recv, l_sem.at[0])
    swap_x = Swap(s, snd_x, x, x_send, x_recv, l_sem.at[1])
    swap_r = Swap(s, snd_dy, rg_all, r_send, r_recv, l_sem.at[2], True)
    swap_z = Swap(s, dyr, zall, z_send, z_recv, l_sem.at[3], True)

    def dispatch(first_row, buffer, swap, more):
        @pl.loop(0, s.NR)
        def _(c):
            pair = send_pair(c)
            rows = pl.ds(align(pair * RC, 16), RC)
            buffer[rows, :] = dot(hot[rows, :], quad[pl.ds(first_row, T), :]).astype(BF)
            for k in range(2):
                swap.start(pair * 2 + k)
            more(c)

    def build_next(c):
        @pl.when(c + 1 < s.NR)
        def _():
            build(send_pair(c + 1))

    load_dy.wait()
    dispatch(0, snd_dy, swap_d, build_next)
    pcol[...] = jnp.transpose(jnp.concatenate([prow] * 4, axis=0))

    load_tok.wait()
    for copy in owns[:3]:
        copy.wait()
    for i in range(3):
        for j in range(1, N):
            weight_copy(i, j).wait_recv()

    def moe_copy(c, j):
        part = quad.at[pl.ds(align(T + h * TL + c * CH, 16), CH)]
        return remote(part, part, m_send.at[c, j], m_recv.at[c, j], w, lax.rem(h + j, N))

    def moe_from(c, j):
        src = lax.rem(h + N - j, N)
        part = quad.at[pl.ds(align(T + src * TL + c * CH, 16), CH)]
        return remote(part, part, m_send.at[c, j], m_recv.at[c, j], w, src)

    lane = lax.broadcasted_iota(jnp.int32, (PATCHES, 2 * HEAD_DIM), 1)
    first = lane < HEAD_DIM

    def split_heads(part):
        zero = jnp.zeros_like(part)
        return jnp.concatenate([jnp.where(first, part, zero), jnp.where(first, zero, part)], axis=0)

    def image_units(c, m, heads):
        image = pl.ds(align(c * CH + m * PATCHES, 16), PATCHES)
        return [
            (image, slice(2 * HEAD_DIM * p, 2 * HEAD_DIM * (p + 1)), (c * s.IMG + m) * HP + p) for p in heads
        ]

    def join_heads(both):
        return jnp.where(first, both[:PATCHES], both[PATCHES:])

    @pl.loop(0, s.NCH)
    def _(c):
        rows = pl.ds(align(c * CH, 16), CH)
        t = tokv[rows, :].astype(F32)
        normed, _r = norm_parts(t)
        ain = (normed * g1[...] + b1[...]).astype(BF)
        ains[rows, :] = ain
        for j in range(N):
            cols = slice(j * L, (j + 1) * L)
            q = (dot(ain, wq[j, 0]) + qvb[j, 0:1, :]).astype(BF)
            qs[rows, cols] = q * BF(HEAD_DIM ** (-0.5))
            ks[rows, cols] = dot(ain, wq[j, 1]).astype(BF)
            vs[rows, cols] = (dot(ain, wq[j, 2]) + qvb[j, 1:2, :]).astype(BF)
        for m in range(s.IMG):
            units = image_units(c, m, range(HP))
            inputs = [(split_heads(qs[im, cols]), ks[im, cols], vs[im, cols]) for im, cols, _u in units]
            scores = [dot_nt(k, q) for q, k, _v in inputs]
            grown = [jnp.exp(one - jnp.max(one, axis=0, keepdims=True)) for one in scores]
            probs = [(one * (1.0 / jnp.sum(one, axis=0, keepdims=True))).astype(BF) for one in grown]
            mixed = [join_heads(dot_tn(one, v)).astype(BF) for one, (_q, _k, v) in zip(probs, inputs)]
            for (im, cols, u), one, value in zip(units, probs, mixed):
                ps[u] = one
                atts[im, cols] = value
        residual = t + (dot(atts[rows, :], wp[...].reshape(D, D)) + pb[...])
        ress[rows, :] = residual
        normed, _r = norm_parts(residual)
        quad[pl.ds(align(T + h * TL + c * CH, 16), CH), :] = (normed * g2[...] + b2[...]).astype(BF)
        for j in range(1, N):
            moe_copy(c, j).start()

    @pl.loop(0, s.NCH)
    def _(c):
        for j in range(1, N):
            moe_from(c, j).wait_recv()

    dispatch(T, snd_x, swap_x, lambda c: None)

    @pl.loop(0, s.NCH)
    def _(c):
        for j in range(1, N):
            moe_copy(c, j).wait_send()

    for copy in owns[3:]:
        copy.wait()
    for i in range(len(pairs)):
        for j in range(1, N):
            if i >= 3:
                weight_copy(i, j).wait_recv()
            weight_copy(i, j).wait_send()

    @pl.loop(0, s.PW)
    def _(i):
        swap_d.wait_send(i)

    load_ags = pltpu.make_async_copy(cot.at[mine], ags, ld_sem.at[0])
    load_ags.start()
    per = FL // FC
    expert_lane = lax.broadcasted_iota(jnp.int32, (RC, E), 1)
    grt[...] = jnp.zeros(grt.shape, F32)

    def pg_rows(f):
        return pl.ds(align(f * s.ROWS, 16), s.ROWS)

    @pl.loop(0, s.NR)
    def _(c):
        pair = send_pair(c)
        rows = pl.ds(align(pair * RC, 16), RC)
        both = pl.ds(pair * 2, 2)
        for k in range(2):
            swap_d.wait_recv(pair * 2 + k)
            swap_x.wait_recv(pair * 2 + k)
        xr = x[both].reshape(RC, D)
        dyf = dyr[both].reshape(RC, D).astype(F32)
        logits = dot_nt(xr, wr[...])
        top = jnp.max(logits, axis=-1, keepdims=True)
        grown = jnp.exp(logits - top)
        probs = grown * (1.0 / jnp.sum(grown, axis=-1, keepdims=True))
        gate = jnp.sum(jnp.where(expert_lane == w, probs, 0.0), axis=-1, keepdims=True)
        og[rows, :] = (gate * dyf).astype(BF)
        ysum[...] = jnp.broadcast_to(db[...], (RC, D))
        rsum[...] = jnp.zeros((RC, D), F32)

        @pl.loop(0, NF)
        def _(f):
            j = f // per
            off = pl.ds(align(lax.rem(f, per) * FC, 128), FC)
            pre = dot(x[both].reshape(RC, D), up[j, :, off]) + ub[j, :, off]
            square = pre * pre
            t = jnp.tanh(GELU_C * (pre + GELU_A * (square * pre)))
            half = 0.5 * (1.0 + t)
            hidden = (pre * half).astype(BF)
            slope = half + (0.5 * GELU_C) * pre * (1.0 - t * t) * (1.0 + (3.0 * GELU_A) * square)
            grad = (dot_nt(og[rows, :], dn[j, off, :]) * slope).astype(BF)
            hot[rows, pl.ds(align(f * FC, 128), FC)] = hidden
            quad[pl.ds(align(f * s.ROWS + pair * RC, 16), RC), 0:FC] = grad
            ysum[...] += dot(hidden, dn[j, off, :])
            rsum[...] += dot_nt(grad, up[j, :, off])

        y = ysum[...].astype(BF).astype(F32)
        gate_grad = jnp.sum(dyf * y, axis=-1, keepdims=True)
        logit = (gate_grad * probs * (jnp.where(expert_lane == w, 1.0, 0.0) - gate)).astype(BF)
        back = (rsum[...] + dot(logit, wr[...])).astype(BF)
        snd_dy[rows, :] = back
        for k in range(2):
            swap_r.start(pair * 2 + k)
        zz = (gate * y).astype(BF)
        for k in range(2):
            dyr[pair * 2 + k] = zz[k * Rb : (k + 1) * Rb]

            @pl.when(lax.rem(c, 2) == 1)
            def _():
                swap_z.start(pair * 2 + k)

        grt[...] += dot_tn(logit, xr)

    piece_rows = Rb // s.PC

    def z_piece(n):
        block, part = n // s.PC, lax.rem(n, s.PC)
        i = send_pair(2 * (block // 2)) * 2 + lax.rem(block, 2)
        rows = pl.ds(align(part * piece_rows, 16), piece_rows)
        return remote(
            dyr.at[i, rows], zall.at[far, slot, rows], zp_send.at[n], zp_recv.at[slot * s.PC + part], i * N + h, far
        )

    def z_landed(i):
        for part in range(s.PC):
            rows = pl.ds(part * piece_rows, piece_rows)
            remote(
                dyr.at[i, rows], zall.at[h, i, rows], zp_send.at[0], zp_recv.at[i * s.PC + part], i * N + h, far
            ).wait_recv()

    def z_go(n):
        if isinstance(n, int):
            if n < s.ZP:
                if n >= DEPTH:
                    z_piece(n - DEPTH).wait_send()
                z_piece(n).start()
        else:

            @pl.when(n < s.ZP)
            def _():
                z_piece(n - DEPTH).wait_send()
                z_piece(n).start()

    def n_copy(i, j):
        a, b = ((us, ur), (ds_, dr))[i]
        return remote(a.at[j - 1], b.at[j - 1], wn_send.at[i, j], wn_recv.at[i, j], w, lax.rem(h + j, N))

    def b_copy(j, slab):
        return remote(bs.at[j - 1], br.at[slab], wn_send.at[2, j], wn_recv.at[2, j], w, lax.rem(h + j, N))

    def hid_cols(owner, c):
        return pl.ds(align((owner * per + c) * FC, 128), FC)

    def up_part(owner, c):
        return dot_tn(x[...].reshape(s.ROWS, D), quad[pg_rows(owner * per + c), 0:FC])

    def down_part(owner, c):
        return dot_tn(hot[:, hid_cols(owner, c)], og[...])

    def pg_sum(owner, c):
        return jnp.sum(quad[pg_rows(owner * per + c), 0:FC].astype(F32), axis=0, keepdims=True)

    og_sum = jnp.sum(og[...].astype(F32), axis=0, keepdims=True)
    span = min(FL, D)

    def put_bias(ref):
        for b in range(D // span):
            ref[1 + b : 2 + b, 0:span] = og_sum[:, b * span : (b + 1) * span]

    for j in range(1, N):
        owner = lax.rem(h + j, N)
        for c in range(per):
            cols = slice(c * FC, (c + 1) * FC)
            us[j - 1, :, cols] = up_part(owner, c).astype(BF)
        n_copy(0, j).start()
        for c in range(per):
            cols = slice(c * FC, (c + 1) * FC)
            ds_[j - 1, cols, :] = down_part(owner, c).astype(BF)
        n_copy(1, j).start()
        for c in range(per):
            cols = slice(c * FC, (c + 1) * FC)
            bs[j - 1, 0:1, cols] = pg_sum(owner, c)
        put_bias(bs.at[j - 1])
        b_copy(j, h).start()
    def go_copy(i, c):
        cols = pl.ds(c * FC, FC)
        if i == 0:
            return pltpu.make_async_copy(stage.at[c, :, pl.ds(0, FC)], gu_out.at[:, cols], go_sem.at[c])
        return pltpu.make_async_copy(stage.at[c, pl.ds(0, FC), :], gd_out.at[cols, :], go_sem.at[c])

    for c in range(per):
        cols = slice(c * FC, (c + 1) * FC)
        total = up_part(h, c)
        for j in range(1, N):
            if c == 0:
                n_copy(0, j).wait_recv()
            total += ur[j - 1, :, cols].astype(F32)
        stage[c, :, 0:FC] = total.astype(BF)
        go_copy(0, c).start()
        gub_out[:, cols] = pg_sum(h, c)
    for c in range(per):
        cols = slice(c * FC, (c + 1) * FC)
        total = down_part(h, c)
        for j in range(1, N):
            if c == 0:
                n_copy(1, j).wait_recv()
            total += dr[j - 1, cols, :].astype(F32)
        go_copy(0, c).wait()
        stage[c, 0:FC, :] = total.astype(BF)
        go_copy(1, c).start()
    put_bias(br.at[h])

    for n in range(DEPTH):
        z_go(n)

    def pass_on(buffer, send, recv, i, j, src=None):
        part = buffer.at[h if src is None else src, i]
        return remote(part, part, send.at[i, j], recv.at[i, j], w, lax.rem(h + j, N) if src is None else src)

    @pl.loop(0, s.NR)
    def _(c):
        for k in range(2):
            i = send_pair(c) * 2 + k
            swap_r.wait_recv(i)
            for j in range(1, N):
                pass_on(rg_all, rf_send, rf_recv, i, j).start()


    for j in range(1, N):
        src = lax.rem(h + N - j, N)
        b_copy(j, src).wait_recv()
        gub_out[...] += br[src, 0:1, :]
    for b in range(D // span):
        gdb_out[:, b * span : (b + 1) * span] = sum(br[j, 1 + b : 2 + b, 0:span] for j in range(N))

    @pl.loop(0, s.PW)
    def _(i):
        for j in range(1, N):
            pass_on(rg_all, rf_send, rf_recv, i, j, lax.rem(h + N - j, N)).wait_recv()

    def spots(c):
        rows = pl.ds(align(h * TL + c * CH, 16), CH)
        hit = jnp.logical_or(pcol[rows, 0:1] == svals[...], pcol[rows, 1:2] == svals[...])
        return jnp.where(hit, 1.0, 0.0).astype(BF)

    small[...] = jnp.zeros(small.shape, F32)
    small[0:E, :] = grt[...]

    def add_row(r, value):
        small[r : r + 1, :] += jnp.sum(value, axis=0, keepdims=True)

    load_ags.wait()

    @pl.loop(0, s.PW)
    def _(i):
        swap_x.wait_send(i)

    @pl.loop(0, s.NCH)
    def _(c):
        rows = pl.ds(align(c * CH, 16), CH)
        z_go(c + DEPTH)
        moe_grad = dot(spots(c), rg_all[...].reshape(E * Rb, D))
        normed, inv = norm_parts(ress[rows, :])
        add_row(E + 2, moe_grad * normed)
        add_row(E + 3, moe_grad)
        total = ags[rows, :].astype(F32) + norm_pull(moe_grad, normed, inv, g2[...])
        rgrad[rows, :] = total
        ag = total.astype(BF)
        ags[rows, :] = ag
        add_row(E + 4, ag.astype(F32))
        snd_x[rows, :] = dot_nt(ag, wp[...].reshape(D, D)).astype(BF)

    def attend_back(part, start, stop):
        heads = range(part, HP, s.halves)

        @pl.loop(start, stop)
        def _(c):
            units = [u for m in range(s.IMG) for u in image_units(c, m, heads)]
            inputs = [
                (split_heads(snd_x[im, cols]), qs[im, cols], ks[im, cols], vs[im, cols], ps[u])
                for im, cols, u in units
            ]
            pgrads = [dot_nt(v, both) for both, _q, _k, v, _p in inputs]
            vgrads = [dot(low, both) for both, _q, _k, _v, low in inputs]
            sgrads = []
            for pgrad, (_b, _q, _k, _v, low) in zip(pgrads, inputs):
                probs = low.astype(F32)
                sgrads.append((probs * (pgrad - jnp.sum(pgrad * probs, axis=0, keepdims=True))).astype(BF))
            qgrads = [dot_tn(sg, one[2]) for sg, one in zip(sgrads, inputs)]
            kgrads = [dot(sg, split_heads(one[1])) for sg, one in zip(sgrads, inputs)]
            for (im, cols, _u), qg, kg, vg in zip(units, qgrads, kgrads, vgrads):
                qs[im, cols] = join_heads(qg * (HEAD_DIM ** (-0.5))).astype(BF)
                ks[im, cols] = kg.astype(BF)
                vs[im, cols] = vg.astype(BF)

    class Job:
        def __init__(self, n):
            self.n, self.rows, self.streams = n, s.jobs[n], s.streams[n]
            self.gsend, self.gnar, self.gown, self.rbuf, self.gfin = job_refs[n]
            self.sbuf = self.gsend.at[0]

        def n_copy(self, rel, narrow_place):
            return remote(
                self.gsend.at[rel], self.gnar.at[rel], n_send.at[self.n, rel], n_recv.at[self.n, rel], w, narrow_place
            )

        def begin(self):
            LW = s.LW
            first_cols = [j * L + self.n * LW for j in range(N)]
            right = jnp.concatenate([dd[:, a : a + LW] for dd in (qs, ks, vs) for a in first_cols], axis=1)
            upper = dot_tn(ains[...], right)
            if self.n == 0:
                lower = dot_tn(atts[...], ags[...])
            for j in range(N):
                parts = [(i * D, upper[:, (i * N + j) * LW : (i * N + j + 1) * LW]) for i in range(3)]
                if self.n == 0:
                    for b in range(D // LW):
                        parts.append((3 * D + b * L, lower[j * L : (j + 1) * L, b * LW : (b + 1) * LW]))

                def put(ref, cast, parts=parts):
                    for r, value in parts:
                        ref[r : r + value.shape[0], :] = value.astype(cast)

                @pl.when(h == j)
                def _():
                    put(self.gown, F32)

                @pl.when(h != j)
                def _():
                    rel = lax.rem(j - h + N, N) - 1
                    put(self.gsend.at[rel], BF)
                    self.n_copy(rel, j).start()

        def join(self):
            for j in range(1, N):
                self.n_copy(j - 1, lax.rem(h + N - j, N)).wait_recv()
                self.gown[...] += self.gnar[j - 1].astype(F32)
            for j in range(1, N):
                self.n_copy(j - 1, lax.rem(h + j, N)).wait_send()

        def segment(self, t, k):
            start, size, order = self.streams[t]
            first_row = start
            for step in range(k):
                size = size // 2
                first_row = first_row + bit_of(order[step]) * size
            return first_row, size

        def halves(self, t, k):
            start, size = self.segment(t, k)
            bit = self.streams[t][2][k]
            half = size // 2
            keep = align(start + bit_of(bit) * half, 16)
            give = align(start + (1 - bit_of(bit)) * half, 16)
            return pl.ds(keep, half), pl.ds(give, half), flip(w, 1 << bit)

        def fold(self, t, k, land):
            keep, give, partner = self.halves(t, k)
            return remote(
                self.sbuf.at[give], self.rbuf.at[keep if land else give],
                h_send.at[self.n, t, k], h_recv.at[self.n, t, k], partner, h,
            )

        def grow(self, t, k, land):
            keep, give, partner = self.halves(t, k)
            return remote(
                self.gfin.at[keep], self.gfin.at[keep if land else give],
                a_send.at[self.n, t, k], a_recv.at[self.n, t, k], partner, h,
            )

        def start(self, q):
            for t in range(len(self.streams)):
                if q < s.bits:
                    _k, give, _p = self.halves(t, q)
                    self.sbuf[give, :] = self.gown[give, :].astype(BF)
                    self.fold(t, q, True).start()
                else:
                    if q == s.bits:
                        start, size = self.segment(t, s.bits)
                        rows = pl.ds(align(start, 16), size)
                        self.gfin[rows, :] = self.gown[rows, :].astype(BF)
                    self.grow(t, 2 * s.bits - 1 - q, True).start()

        def end(self, q):
            for t in range(len(self.streams)):
                if q < s.bits:
                    keep, give, _p = self.halves(t, q)
                    self.fold(t, q, False).wait()
                    self.gown[keep, :] += self.rbuf[give, :].astype(F32)
                else:
                    self.grow(t, 2 * s.bits - 1 - q, False).wait()

        def finish(self):
            return pltpu.make_async_copy(self.gfin, gbigs[self.n], fin_sem.at[self.n])

    def bit_of(b):
        return lax.rem(w // (1 << b), 2)

    def s_copy(k):
        return remote(sacc.at[k], srec.at[k], s_send.at[k], s_recv.at[k], flip(w, 1 << k), h)

    def tok_copy(src, dst, send, recv, c, j):
        here = pl.ds(align(c * CH, 16), CH)
        there = pl.ds(align(h * TL + c * CH, 16), CH)
        return remote(src.at[here], dst.at[there], send.at[c, j], recv.at[c, j], w, lax.rem(h + j, N))

    def tok_local(src, dst, sem, c):
        here = pl.ds(align(c * CH, 16), CH)
        there = pl.ds(align(h * TL + c * CH, 16), CH)
        return pltpu.make_async_copy(src.at[here], dst.at[there], sem.at[c])

    def bias_sums():
        small[E + 5 : E + 6, :] = jnp.sum(qs[...].astype(F32), axis=0, keepdims=True)
        small[E + 6 : E + 7, :] = jnp.sum(vs[...].astype(F32), axis=0, keepdims=True)

    def first_norm_part(start, stop):
        @pl.loop(start, stop)
        def _(c):
            rows = pl.ds(align(c * CH, 16), CH)
            back = jnp.zeros((CH, D), F32)
            for j in range(N):
                cols = slice(j * L, (j + 1) * L)
                for i, dd in enumerate((qs, ks, vs)):
                    back += dot_nt(dd[rows, cols], wq[j, i])
            normed, inv = norm_parts(tokv[rows, :].astype(F32))
            add_row(E, back * normed)
            add_row(E + 1, back)
            ags[rows, :] = (rgrad[rows, :] + norm_pull(back, normed, inv, g1[...])).astype(BF)
            for j in range(1, N):
                tok_copy(ags, gtok, g_send, g_recv, c, j).start()
            tok_local(ags, gtok, g_loc, c).start()

    def small_send():
        for b in range(D // 128):
            snar[h, b * s.RP : (b + 1) * s.RP, :] = small[:, b * 128 : (b + 1) * 128]
        for j in range(1, N):
            remote(snar.at[h], snar.at[h], sn_send.at[j], sn_recv.at[j], w, lax.rem(h + j, N)).start()

    def combine_pass():
        for n in range(z_next + 1, s.ZP):
            z_go(n)

        @pl.loop(0, s.NR // 2)
        def _(c):
            for k in range(4):
                i = send_pair(2 * c + 1 - k // 2) * 2 + k % 2
                if k < 2:
                    swap_z.wait_recv(i)
                else:
                    z_landed(i)
                for j in range(1, N):
                    pass_on(zall, zf_send, zf_recv, i, j).start()

    def combine_wait():
        @pl.loop(0, s.PW)
        def _(i):
            for j in range(1, N):
                pass_on(zall, zf_send, zf_recv, i, j, lax.rem(h + N - j, N)).wait_recv()

    def combine(start, stop):
        @pl.loop(start, stop)
        def _(c):
            rows = pl.ds(align(c * CH, 16), CH)
            mixed = dot(spots(c), zall[...].reshape(E * Rb, D))
            ains[rows, :] = (ress[rows, :] + mixed).astype(BF)
            for j in range(1, N):
                tok_copy(ains, out, o_send, o_recv, c, j).start()
            tok_local(ains, out, o_loc, c).start()

    def small_narrow():
        for j in range(1, N):
            src = lax.rem(h + N - j, N)
            remote(snar.at[h], snar.at[h], sn_send.at[j], sn_recv.at[j], w, src).wait_send()
            remote(snar.at[src], snar.at[src], sn_send.at[j], sn_recv.at[j], w, src).wait_recv()
        sacc[0] = sum(snar[j] for j in range(N))

    jobs = [Job(n) for n in range(NJ)]
    steps = 2 * s.bits
    attend_back(0, 0, s.NCH)
    z_next = DEPTH + s.NCH
    z_go(z_next)
    jobs[0].begin()
    if NJ == 2:
        middle = s.NCH // 2
        attend_back(1, 0, middle)
        z_next += 1
        z_go(z_next)
        jobs[0].join()
        jobs[0].start(0)
        attend_back(1, middle, s.NCH)
        z_next += 1
        z_go(z_next)
        jobs[1].begin()
        jobs[0].end(0)
        jobs[0].start(1)
        jobs[1].join()
        jobs[1].start(0)
        at = [1, 0]
    else:
        jobs[0].join()
        jobs[0].start(0)
        at = [0]
    turn, little = 0, 0
    while min(at) < steps:
        z_next += 1
        z_go(z_next)
        if turn == 0:
            bias_sums()
        if turn < LN_TURNS:
            first_norm_part(turn * s.NCH // LN_TURNS, (turn + 1) * s.NCH // LN_TURNS)
        if turn == LN_TURNS - 1:
            small_send()
        if turn == LN_TURNS:
            small_narrow()
        if turn == MIX_TURN:
            combine_pass()
        if turn == MIX_TURN + 1:
            combine_wait()
            combine(0, s.NCH // 2)
        if turn == MIX_TURN + 2:
            combine(s.NCH // 2, s.NCH)
        if turn >= LN_TURNS and little < s.bits:
            if little:
                s_copy(little - 1).wait()
                sacc[little] = sacc[little - 1] + srec[little - 1]
            s_copy(little).start()
            little += 1
        for n in range(NJ):
            if at[n] < steps:
                jobs[n].end(at[n])
                at[n] += 1
                if at[n] < steps:
                    jobs[n].start(at[n])
                else:
                    jobs[n].finish().start()
        turn += 1
    while little < s.bits:
        s_copy(little - 1).wait()
        sacc[little] = sacc[little - 1] + srec[little - 1]
        s_copy(little).start()
        little += 1
    s_copy(s.bits - 1).wait()
    gsmall[...] = sacc[s.bits - 1] + srec[s.bits - 1]

    for j in range(1, N):
        for i in range(2):
            n_copy(i, j).wait_send()
        b_copy(j, h).wait_send()

    @pl.loop(0, s.PW)
    def _(i):
        swap_r.wait_send(i)
        for j in range(1, N):
            pass_on(rg_all, rf_send, rf_recv, i, j).wait_send()
            pass_on(zall, zf_send, zf_recv, i, j).wait_send()

    @pl.loop(0, s.NCH)
    def _(c):
        tok_local(ags, gtok, g_loc, c).wait()
        tok_local(ains, out, o_loc, c).wait()
        here = pl.ds(align(c * CH, 16), CH)
        for j in range(1, N):
            src = lax.rem(h + N - j, N)
            there = pl.ds(align(src * TL + c * CH, 16), CH)
            tok_copy(ags, gtok, g_send, g_recv, c, j).wait_send()
            tok_copy(ains, out, o_send, o_recv, c, j).wait_send()
            remote(ags.at[here], gtok.at[there], g_send.at[c, j], g_recv.at[c, j], w, src).wait_recv()
            remote(ains.at[here], out.at[there], o_send.at[c, j], o_recv.at[c, j], w, src).wait_recv()

    for c in range(per):
        go_copy(1, c).wait()
    @pl.loop(0, s.NR // 2)
    def _(c):
        for k in range(2):
            swap_z.wait_send(send_pair(2 * c + 1) * 2 + k)

    for n in range(max(0, s.ZP - DEPTH), s.ZP):
        z_piece(n).wait_send()
    for job in jobs:
        job.finish().wait()


def post_kernel(s, *refs):
    (
        out_in, gtok_in, gu_in, gd_in, flat, *rest,
    ) = refs
    bigs, rest = rest[: len(s.jobs)], rest[len(s.jobs) :]
    (
        out, gtok, gu, gd, gqkv, gproj, gag, gas, gmg, gms, gpb, gqv, grouter,
        b_out, b_tok, b_gu, b_gd, f_tok, f_gu, f_gd, l_sem, s_sem,
    ) = rest
    moves = (
        (gtok_in, b_tok, f_tok, gtok), (gu_in, b_gu, f_gu, gu), (gd_in, b_gd, f_gd, gd), (out_in, b_out, b_out, out),
    )
    loads, stores, widen = [], [], []
    for i, (a, b, f, c) in enumerate(moves):
        step = a.shape[0] // PARTS
        for p in range(PARTS):
            part = pl.ds(p * step, step)
            loads.append(pltpu.make_async_copy(a.at[part], b.at[part], l_sem.at[i, p]))
            stores.append(pltpu.make_async_copy(f.at[part], c.at[part], s_sem.at[i, p]))
            widen.append((b, f, slice(p * step, (p + 1) * step)))
    for load in loads:
        load.start()
    D, L, N, E, LW = s.D, s.L, s.N, s.E, s.LW
    h = lax.axis_index("narrow")
    for load, store, (b, f, part) in zip(loads, stores, widen):
        load.wait()
        if b is not f:
            f[part, :] = b[part, :].astype(F32)
        store.start()
    for n, big in enumerate(bigs):
        for i in range(3):
            gqkv[i, :, n * LW : (n + 1) * LW] = big[i * D : (i + 1) * D, :].astype(F32)
    for b in range(D // LW):
        gproj[:, b * LW : (b + 1) * LW] = bigs[0][3 * D + b * L : 3 * D + (b + 1) * L, :].astype(F32)

    def rows(r, count):
        return jnp.concatenate([flat[b * s.RP + r : b * s.RP + r + count, :] for b in range(D // 128)], axis=1)

    grouter[...] = rows(0, E)
    for r, ref in ((E, gag), (E + 1, gas), (E + 2, gmg), (E + 3, gms), (E + 4, gpb)):
        ref[...] = rows(r, 1)
    qv = rows(E + 5, 2)
    for j in range(N):

        @pl.when(h == j)
        def _():
            gqv[...] = qv[:, j * L : (j + 1) * L]

    for store in stores:
        store.wait()


VM = pl.BlockSpec(memory_space=pltpu.VMEM)
ANY = pl.BlockSpec(memory_space=pl.ANY)
HB = pl.BlockSpec(memory_space=pltpu.HBM)
DMA = pltpu.SemaphoreType.DMA
V = pltpu.VMEM


def shards(
    wide,
    narrow,
    tokens,
    attn_gain,
    attn_shift,
    qkv_weight,
    query_value_bias,
    proj_weight,
    proj_bias,
    moe_gain,
    moe_shift,
    router_weight,
    expert_up,
    expert_up_bias,
    expert_down,
    expert_down_bias,
    routes,
    slot_index,
    cotangent,
):
    s = Sizes(wide, narrow, tokens.shape[0], tokens.shape[1], router_weight.shape[1], expert_up.shape[2])
    T, D, E, N, W, L, TL = s.T, s.D, s.E, s.N, s.W, s.L, s.TL
    PW, Rb, FL, ROWS, RC, NCH = s.PW, s.Rb, s.FL, s.ROWS, s.RC, s.NCH
    slot = np.arange(E * Rb)
    half, rest = slot // (PW * Rb), slot % (PW * Rb)
    pos, inner = rest // Rb, rest % Rb
    svals = np.where(inner < s.cap, (pos * N + half) * s.cap + inner, -2).astype(np.int32)[None, :]
    row = lambda a: a.reshape(1, -1)
    blk = (PW, Rb, D)
    heads = (TL // PATCHES) * s.HP
    NS = 3
    ins = [
        (ANY, tokens), (ANY, cotangent), (VM, row(attn_gain)), (VM, row(attn_shift)),
        (ANY, qkv_weight.transpose(1, 0, 2)), (ANY, query_value_bias), (ANY, proj_weight), (VM, row(proj_bias)),
        (VM, row(moe_gain)), (VM, row(moe_shift)), (VM, router_weight.T), (ANY, expert_up[0]),
        (ANY, expert_up_bias), (ANY, expert_down[0]), (VM, expert_down_bias), (VM, routes.T), (VM, slot_index.T),
        (VM, jnp.asarray(svals)),
    ]
    outs = [
        (ANY, (T, D), BF), (ANY, (T, D), BF), (VM, (s.RPS, 128), F32),
        (ANY, (D, FL), BF), (ANY, (FL, D), BF), (VM, (1, FL), F32), (VM, (1, D), F32),
    ] + [(ANY, (r, s.LW), BF) for r in s.jobs]
    scratch = [
        V((TL, D), BF), V((N, 3, D, L), BF), V((N, L, D), BF), V((N, 2, L), F32), V((T, 8), jnp.int32),
        V((ROWS, T), BF), V((2 * T, D), BF), V((TL, D), BF), V((TL, D), BF), V((TL, D), BF),
        V((heads, PATCHES, 2 * PATCHES), BF), V((TL, D), BF), V((TL, D), BF), V((TL, D), F32), V((ROWS, D), BF), V((ROWS, D), BF),
        V(blk, BF), V(blk, BF), V((N, D, FL), BF), V((N, FL, D), BF), V((N, 1, FL), F32), V((ROWS, D), BF),
        V((RC, D), F32), V((RC, D), F32), V((N - 1, D, FL), BF), V((N - 1, FL, D), BF), V((N - 1, D, FL), BF),
        V((N - 1, FL, D), BF), V((N - 1, 8, FL), F32), V((N, 8, FL), F32), V((FL // s.FC, D, D), BF),
        V((E, D), F32),
        V((N,) + blk, BF), V((N,) + blk, BF), V((TL, D), BF), V((TL, D), F32),
        V((s.RP, D), F32), V((N, s.RPS, 128), F32), V((s.bits, s.RPS, 128), F32), V((s.bits, s.RPS, 128), F32),
    ]
    for r in s.jobs:
        scratch += [V((N - 1, r, s.LW), BF), V((N - 1, r, s.LW), BF), V((r, s.LW), F32)]
        scratch += [V((r, s.LW), BF), V((r, s.LW), BF)]
    NJ = len(s.jobs)
    scratch += [
        DMA((2,)), DMA((6,)), DMA((6, N)), DMA((6, N)), DMA((NCH, N)), DMA((NCH, N)),
        DMA((PW,)), DMA((PW,)), DMA((PW,)), DMA((PW,)), DMA((PW,)), DMA((PW,)),
        DMA((PW,)), DMA((PW,)), DMA((s.ZP,)), DMA((PW * s.PC,)), DMA((4,)), DMA((PW, N)), DMA((PW, N)), DMA((PW, N)), DMA((PW, N)),
        DMA((3, N)), DMA((3, N)), DMA((FL // s.FC,)),
        DMA((NJ, N)), DMA((NJ, N)), DMA((N,)), DMA((N,)), DMA((NJ, NS, s.bits)), DMA((NJ, NS, s.bits)),
        DMA((NJ, NS, s.bits)), DMA((NJ, NS, s.bits)), DMA((s.bits,)), DMA((s.bits,)),
        DMA((NCH, N)), DMA((NCH, N)), DMA((NCH, N)), DMA((NCH, N)), DMA((NCH,)), DMA((NCH,)), DMA((NJ,)),
    ]
    out, gtok, gsmall, gu, gd, gub, gdb, *gbigs = pl.pallas_call(
        functools.partial(block_kernel, s),
        in_specs=[spec for spec, _ in ins],
        out_specs=[spec for spec, _, _ in outs],
        out_shape=[jax.ShapeDtypeStruct(shape, dtype) for _, shape, dtype in outs],
        scratch_shapes=scratch,
        compiler_params=pltpu.CompilerParams(
            collective_id=1, has_side_effects=True, vmem_limit_bytes=VMEM_MB << 20
        ),
        name="block",
    )(*[a for _, a in ins])

    post_ins = [(HB, out), (HB, gtok), (HB, gu), (HB, gd), (VM, gsmall)]
    post_ins += [(VM, a) for a in gbigs]
    post_outs = [
        (ANY, (T, D), BF), (ANY, (T, D), F32), (ANY, (D, FL), F32), (ANY, (FL, D), F32), (VM, (3, D, L), F32),
        (VM, (L, D), F32), (VM, (1, D), F32), (VM, (1, D), F32), (VM, (1, D), F32), (VM, (1, D), F32),
        (VM, (1, D), F32), (VM, (2, L), F32), (VM, (E, D), F32),
    ]
    out, gtok, gu, gd, gqkv, gproj, gag, gas, gmg, gms, gpb, gqv, grouter = pl.pallas_call(
        functools.partial(post_kernel, s),
        in_specs=[spec for spec, _ in post_ins],
        out_specs=[spec for spec, _, _ in post_outs],
        out_shape=[jax.ShapeDtypeStruct(shape, dtype) for _, shape, dtype in post_outs],
        scratch_shapes=[
            V((T, D), BF), V((T, D), BF), V((D, FL), BF), V((FL, D), BF), V((T, D), F32), V((D, FL), F32),
            V((FL, D), F32), DMA((4, PARTS)), DMA((4, PARTS)),
        ],
        compiler_params=pltpu.CompilerParams(vmem_limit_bytes=VMEM_MB << 20),
        name="post",
    )(*[a for _, a in post_ins])
    return (
        out,
        gtok,
        gag.reshape(D),
        gas.reshape(D),
        gqkv.transpose(1, 0, 2),
        gqv,
        gproj,
        gpb.reshape(D),
        gmg.reshape(D),
        gms.reshape(D),
        grouter.T,
        gu[None],
        gub,
        gd[None],
        gdb,
    )


def solution(mesh):
    in_specs = (
        P("wide", None),
        P(),
        P(),
        P(None, None, "narrow"),
        P(None, "narrow"),
        P("narrow", None),
        P(),
        P(),
        P(),
        P(),
        P("wide", None, "narrow"),
        P("wide", "narrow"),
        P("wide", "narrow", None),
        P("wide", None),
        P("wide", None),
        P("wide", None),
        P("wide", None),
    )
    out_specs = (
        P("wide", None),
        P("wide", None),
        P(),
        P(),
        P(None, None, "narrow"),
        P(None, "narrow"),
        P("narrow", None),
        P(),
        P(),
        P(),
        P(),
        P("wide", None, "narrow"),
        P("wide", "narrow"),
        P("wide", "narrow", None),
        P("wide", None),
    )
    body = functools.partial(shards, mesh.shape["wide"], mesh.shape["narrow"])
    return jax.shard_map(body, mesh=mesh, in_specs=in_specs, out_specs=out_specs, check_vma=False)
```

```python
import functools

import jax
import jax.numpy as jnp
import numpy as np
from jax import lax
from jax.experimental import pallas as pl
from jax.experimental.pallas import tpu as pltpu
from jax.sharding import PartitionSpec as P

PATCHES = 144
HEAD_DIM = 64
EPSILON = 1e-06
MESH = pl.DeviceIdType.MESH
BF = jnp.bfloat16
F32 = jnp.float32
GELU_C = 0.7978845608028654
GELU_A = 0.044715
VMEM_MB = 63
PARTS = 2
DEPTH = 4
LN_TURNS = 1
MIX_TURN = 2


def dot(a, b):
    return jnp.dot(a, b, preferred_element_type=F32)


def dot_nt(a, b):
    return lax.dot_general(a, b, (((1,), (1,)), ((), ())), preferred_element_type=F32)


def dot_tn(a, b):
    return lax.dot_general(a, b, (((0,), (0,)), ((), ())), preferred_element_type=F32)


def norm_parts(values):
    center = values - jnp.mean(values, axis=-1, keepdims=True)
    inv_root = lax.rsqrt(jnp.mean(center * center, axis=-1, keepdims=True) + EPSILON)
    return center * inv_root, inv_root


def norm_pull(upstream, normed, inv_root, norm_gain):
    scaled = upstream * norm_gain
    bracket = (
        scaled
        - jnp.mean(scaled, axis=-1, keepdims=True)
        - normed * jnp.mean(scaled * normed, axis=-1, keepdims=True)
    )
    return inv_root * bracket


class Sizes:
    def __init__(self, wide, narrow, tokens, width, experts, local_ff):
        self.W, self.N = wide, narrow
        self.T, self.D, self.E = tokens, width, experts
        self.TL = tokens // narrow
        self.cap = tokens // experts
        self.PW = wide // narrow
        self.Rb = -(-self.cap // 16) * 16
        self.L = width // narrow
        self.FL = local_ff
        self.CH = 2 * PATCHES
        self.NCH = self.TL // self.CH
        self.IMG = self.CH // PATCHES
        self.HP = width // (2 * HEAD_DIM)
        self.ROWS = self.PW * self.Rb
        self.RC = 2 * self.Rb
        self.PC = 3 if self.Rb % 48 == 0 else 1
        self.ZP = self.PW // 2 * self.PC
        self.NR = self.PW // 2
        self.FC = min(512, local_ff)
        self.NF = narrow * local_ff // self.FC
        self.LW = min(128, self.L)
        self.halves = 2 if self.L == 256 else 1
        self.jobs = [width // self.LW * self.L] + [3 * width] * self.halves
        self.RP = -(-(experts + 7) // 8) * 8
        self.RPS = self.RP * (width // 128)
        self.near = min(4, wide)
        self.teams = (self.near, wide // self.near)


def place():
    return lax.axis_index("wide"), lax.axis_index("narrow")


def signal(sem, wide, narrow):
    pl.semaphore_signal(sem, 1, device_id=(wide, narrow), device_id_type=MESH)


def remote(src, dst, send, recv, wide, narrow):
    return pltpu.make_async_remote_copy(
        src, dst, send, recv, device_id=(wide, narrow), device_id_type=MESH
    )


class Swap:
    def __init__(self, s, src, dst, send, recv, local, half=False):
        self.s, self.src = s, src
        self.send, self.recv, self.local = send, recv, local
        w, h = place()
        self.w, self.h = w, h
        self.far = lax.rem(w, s.N)
        self.slot = w // s.N
        self.dst = dst.at[self.far] if half else dst
        self.land = dst.at[h] if half else dst

    def at(self, i):
        if len(self.src.shape) == 2:
            return self.src.at[pl.ds(align(i * self.s.Rb, 16), self.s.Rb)]
        return self.src.at[i]

    def own(self, i):
        return jnp.logical_and(self.far == self.h, i == self.slot)

    def start(self, i):
        @pl.when(jnp.logical_not(self.own(i)))
        def _():
            remote(
                self.at(i),
                self.dst.at[self.slot],
                self.send.at[i],
                self.recv.at[self.slot],
                i * self.s.N + self.h,
                self.far,
            ).start()

        @pl.when(self.own(i))
        def _():
            pltpu.make_async_copy(self.at(i), self.dst.at[self.slot], self.local).start()

    def there(self, i):
        return remote(
            self.at(i),
            self.land.at[i],
            self.send.at[i],
            self.recv.at[i],
            i * self.s.N + self.h,
            self.far,
        )

    def wait_send(self, i):
        @pl.when(jnp.logical_not(self.own(i)))
        def _():
            self.there(i).wait_send()

    def wait_recv(self, i):
        @pl.when(jnp.logical_not(self.own(i)))
        def _():
            self.there(i).wait_recv()

        @pl.when(self.own(i))
        def _():
            pltpu.make_async_copy(self.at(i), self.land.at[i], self.local).wait()


def mix_bits(value, other, count):
    total = 0
    for b in range(count):
        p, q = lax.rem(value // (1 << b), 2), lax.rem(other // (1 << b), 2)
        total = total + (p + q - 2 * p * q) * (1 << b)
    return total


def align(x, m):
    return pl.multiple_of(x, m)


def block_kernel(s, *refs):
    (
        tok, cot, g1, b1, wq_loc, qvb_loc, wp_loc, pb, g2, b2, wr, up_loc, ub_loc, dn_loc, db,
        routes, slots, svals,
        out, gtok, gsmall, gu_out, gd_out, gub_out, gdb_out, *rest,
    ) = refs
    gbigs, rest = rest[: len(s.jobs)], rest[len(s.jobs) :]
    (
        tokv, wq, wp, qvb, pcol, hot, quad, qs, ks, vs, ps, atts, ains, ress, snd_x, snd_dy,
        x, dyr, up, dn, ub, og, ysum, rsum, us, ds_, ur, dr, bs, br, stage, grt,
        rg_all, zall, ags, rgrad, small, snar, sacc, srec, *more,
    ) = rest
    NJ = len(s.jobs)
    job_refs = [more[5 * n : 5 * n + 5] for n in range(NJ)]
    (
        ld_sem, own_sem, w_send, w_recv, m_send, m_recv, x_send, x_recv, d_send, d_recv, r_send, r_recv,
        z_send, z_recv, zp_send, zp_recv, l_sem, rf_send, rf_recv, zf_send, zf_recv, wn_send, wn_recv, go_sem,
        n_send, n_recv, sn_send, sn_recv, h_send, h_recv, a_send, a_recv, s_send, s_recv,
        o_send, o_recv, g_send, g_recv, o_loc, g_loc, fin_sem,
    ) = more[5 * NJ :]
    w, h = place()
    N, W, T, TL, CH, L, D, E = s.N, s.W, s.T, s.TL, s.CH, s.L, s.D, s.E
    RC, FC, FL, HP, Rb, NF = s.RC, s.FC, s.FL, s.HP, s.Rb, s.NF
    far = lax.rem(w, N)
    slot = w // N
    prime = slot // 2
    pair_bits = s.NR.bit_length() - 1

    barrier = pltpu.get_barrier_semaphore()

    @pl.loop(0, s.PW)
    def _(i):
        @pl.when(jnp.logical_or(far != h, i != slot))
        def _():
            signal(barrier, i * N + h, far)

    for j in range(1, N):
        signal(barrier, w, lax.rem(h + j, N))
    spot = (lax.rem(w, s.near), w // s.near)

    def mate(team, place_in_team):
        return w + (place_in_team - spot[team]) * (1, s.near)[team]

    mates = [mate(f, lax.rem(spot[f] + r, s.teams[f])) for f in range(2) for r in range(1, s.teams[f])]
    extra = 0
    for other in mates:
        fresh = jnp.logical_or(far != h, lax.rem(other, N) != far)
        extra = extra + fresh.astype(jnp.int32)

        @pl.when(fresh)
        def _():
            signal(barrier, other, h)

    mine = pl.ds(align(h * TL, 16), TL)
    load_dy = pltpu.make_async_copy(cot, quad.at[pl.ds(0, T)], ld_sem.at[0])
    load_tok = pltpu.make_async_copy(tok.at[mine], tokv, ld_sem.at[1])
    load_dy.start()
    load_tok.start()
    pairs = ((wq_loc, wq), (wp_loc, wp), (qvb_loc, qvb), (up_loc, up), (dn_loc, dn), (ub_loc, ub))
    owns = [pltpu.make_async_copy(a, b.at[h], own_sem.at[i]) for i, (a, b) in enumerate(pairs)]
    for copy in owns:
        copy.start()

    slot_rows = slots[...]
    prow = jnp.where(slot_rows < s.cap, routes[...] * s.cap + slot_rows, -1)
    one_row, two_row = prow[0:1, :], prow[1:2, :]

    def build(pair):
        for k in range(2):
            i = pair * 2 + k
            row = lax.broadcasted_iota(jnp.int32, (Rb, 1), 0)
            value = jnp.where(row < s.cap, (i * N + h) * s.cap + row, -2)
            hit = jnp.logical_or(one_row == value, two_row == value)
            hot[pl.ds(align(i * Rb, 16), Rb), 0:T] = jnp.where(hit, 1.0, 0.0).astype(BF)

    def send_pair(c):
        return mix_bits(prime, s.NR - 1 - c // 2 - (s.NR // 2) * lax.rem(c, 2), pair_bits)

    build(send_pair(0))
    pl.semaphore_wait(
        barrier,
        s.PW + N - 1 + extra - (far == h).astype(jnp.int32),
    )

    def weight_copy(i, j):
        a, b = pairs[i]
        return remote(a, b.at[h], w_send.at[i, j], w_recv.at[i, j], w, lax.rem(h + j, N))

    for i in range(len(pairs)):
        for j in range(1, N):
            weight_copy(i, j).start()

    swap_d = Swap(s, snd_dy, dyr, d_send, d_recv, l_sem.at[0])
    swap_x = Swap(s, snd_x, x, x_send, x_recv, l_sem.at[1])
    swap_r = Swap(s, snd_dy, rg_all, r_send, r_recv, l_sem.at[2], True)
    swap_z = Swap(s, dyr, zall, z_send, z_recv, l_sem.at[3], True)

    def dispatch(first_row, buffer, swap, more):
        @pl.loop(0, s.NR)
        def _(c):
            pair = send_pair(c)
            rows = pl.ds(align(pair * RC, 16), RC)
            buffer[rows, :] = dot(hot[rows, 0:T], quad[pl.ds(first_row, T), :]).astype(BF)
            for k in range(2):
                swap.start(pair * 2 + k)
            more(c)

    def build_next(c):
        @pl.when(c + 1 < s.NR)
        def _():
            build(send_pair(c + 1))

    load_dy.wait()
    dispatch(0, snd_dy, swap_d, build_next)
    pcol[...] = jnp.transpose(jnp.concatenate([prow] * 4, axis=0))

    load_tok.wait()
    for copy in owns[:3]:
        copy.wait()
    for i in range(3):
        for j in range(1, N):
            weight_copy(i, j).wait_recv()

    def moe_copy(c, j):
        part = quad.at[pl.ds(align(T + h * TL + c * CH, 16), CH)]
        return remote(part, part, m_send.at[c, j], m_recv.at[c, j], w, lax.rem(h + j, N))

    def moe_from(c, j):
        src = lax.rem(h + N - j, N)
        part = quad.at[pl.ds(align(T + src * TL + c * CH, 16), CH)]
        return remote(part, part, m_send.at[c, j], m_recv.at[c, j], w, src)

    lane = lax.broadcasted_iota(jnp.int32, (PATCHES, 2 * HEAD_DIM), 1)
    first = lane < HEAD_DIM

    def split_heads(part):
        zero = jnp.zeros_like(part)
        return jnp.concatenate([jnp.where(first, part, zero), jnp.where(first, zero, part)], axis=0)

    def image_units(c, m, heads):
        image = pl.ds(align(c * CH + m * PATCHES, 16), PATCHES)
        return [
            (image, slice(2 * HEAD_DIM * p, 2 * HEAD_DIM * (p + 1)), (c * s.IMG + m) * HP + p) for p in heads
        ]

    def join_heads(both):
        return jnp.where(first, both[:PATCHES], both[PATCHES:])

    @pl.loop(0, s.NCH)
    def _(c):
        rows = pl.ds(align(c * CH, 16), CH)
        t = tokv[rows, :].astype(F32)
        normed, _r = norm_parts(t)
        ain = (normed * g1[...] + b1[...]).astype(BF)
        ains[rows, :] = ain
        for j in range(N):
            cols = slice(j * L, (j + 1) * L)
            q = (dot(ain, wq[j, 0]) + qvb[j, 0:1, :]).astype(BF)
            qs[rows, cols] = q * BF(HEAD_DIM ** (-0.5))
            ks[rows, cols] = dot(ain, wq[j, 1]).astype(BF)
            vs[rows, cols] = (dot(ain, wq[j, 2]) + qvb[j, 1:2, :]).astype(BF)
        for m in range(s.IMG):
            units = image_units(c, m, range(HP))
            inputs = [(split_heads(qs[im, cols]), ks[im, cols], vs[im, cols]) for im, cols, _u in units]
            scores = [dot_nt(k, q) for q, k, _v in inputs]
            grown = [jnp.exp(one - jnp.max(one, axis=0, keepdims=True)) for one in scores]
            probs = [(one * (1.0 / jnp.sum(one, axis=0, keepdims=True))).astype(BF) for one in grown]
            mixed = [join_heads(dot_tn(one, v)).astype(BF) for one, (_q, _k, v) in zip(probs, inputs)]
            for (im, cols, u), one, value in zip(units, probs, mixed):
                ps[u] = one
                atts[im, cols] = value
        residual = t + (dot(atts[rows, :], wp[...].reshape(D, D)) + pb[...])
        ress[rows, :] = residual
        normed, _r = norm_parts(residual)
        quad[pl.ds(align(T + h * TL + c * CH, 16), CH), :] = (normed * g2[...] + b2[...]).astype(BF)
        for j in range(1, N):
            moe_copy(c, j).start()

    @pl.loop(0, s.NCH)
    def _(c):
        for j in range(1, N):
            moe_from(c, j).wait_recv()

    dispatch(T, snd_x, swap_x, lambda c: None)

    @pl.loop(0, s.NCH)
    def _(c):
        for j in range(1, N):
            moe_copy(c, j).wait_send()

    for copy in owns[3:]:
        copy.wait()
    for i in range(len(pairs)):
        for j in range(1, N):
            if i >= 3:
                weight_copy(i, j).wait_recv()
            weight_copy(i, j).wait_send()

    @pl.loop(0, s.PW)
    def _(i):
        swap_d.wait_send(i)

    load_ags = pltpu.make_async_copy(cot.at[mine], ags, ld_sem.at[0])
    load_ags.start()
    per = FL // FC
    expert_lane = lax.broadcasted_iota(jnp.int32, (RC, E), 1)
    grt[...] = jnp.zeros(grt.shape, F32)

    def pg_rows(f):
        return pl.ds(align(f * s.ROWS, 16), s.ROWS)

    @pl.loop(0, s.NR)
    def _(c):
        pair = send_pair(c)
        rows = pl.ds(align(pair * RC, 16), RC)
        both = pl.ds(pair * 2, 2)
        for k in range(2):
            swap_d.wait_recv(pair * 2 + k)
            swap_x.wait_recv(pair * 2 + k)
        xr = x[both].reshape(RC, D)
        dyf = dyr[both].reshape(RC, D).astype(F32)
        logits = dot_nt(xr, wr[...])
        top = jnp.max(logits, axis=-1, keepdims=True)
        grown = jnp.exp(logits - top)
        probs = grown * (1.0 / jnp.sum(grown, axis=-1, keepdims=True))
        gate = jnp.sum(jnp.where(expert_lane == w, probs, 0.0), axis=-1, keepdims=True)
        og[rows, :] = (gate * dyf).astype(BF)
        ysum[...] = jnp.broadcast_to(db[...], (RC, D))
        rsum[...] = jnp.zeros((RC, D), F32)

        @pl.loop(0, NF)
        def _(f):
            j = f // per
            off = pl.ds(align(lax.rem(f, per) * FC, 128), FC)
            pre = dot(x[both].reshape(RC, D), up[j, :, off]) + ub[j, :, off]
            square = pre * pre
            t = jnp.tanh(GELU_C * (pre + GELU_A * (square * pre)))
            half = 0.5 * (1.0 + t)
            hidden = (pre * half).astype(BF)
            slope = half + (0.5 * GELU_C) * pre * (1.0 - t * t) * (1.0 + (3.0 * GELU_A) * square)
            grad = (dot_nt(og[rows, :], dn[j, off, :]) * slope).astype(BF)
            hot[rows, pl.ds(align(f * FC, 128), FC)] = hidden
            quad[pl.ds(align(f * s.ROWS + pair * RC, 16), RC), 0:FC] = grad
            ysum[...] += dot(hidden, dn[j, off, :])
            rsum[...] += dot_nt(grad, up[j, :, off])

        y = ysum[...].astype(BF).astype(F32)
        gate_grad = jnp.sum(dyf * y, axis=-1, keepdims=True)
        logit = (gate_grad * probs * (jnp.where(expert_lane == w, 1.0, 0.0) - gate)).astype(BF)
        back = (rsum[...] + dot(logit, wr[...])).astype(BF)
        snd_dy[rows, :] = back
        for k in range(2):
            swap_r.start(pair * 2 + k)
        zz = (gate * y).astype(BF)
        for k in range(2):
            dyr[pair * 2 + k] = zz[k * Rb : (k + 1) * Rb]

            @pl.when(lax.rem(c, 2) == 1)
            def _():
                swap_z.start(pair * 2 + k)

        grt[...] += dot_tn(logit, xr)

    piece_rows = Rb // s.PC

    def z_piece(n):
        block, part = n // s.PC, lax.rem(n, s.PC)
        i = send_pair(2 * (block // 2)) * 2 + lax.rem(block, 2)
        rows = pl.ds(align(part * piece_rows, 16), piece_rows)
        return remote(
            dyr.at[i, rows], zall.at[far, slot, rows], zp_send.at[n], zp_recv.at[slot * s.PC + part], i * N + h, far
        )

    def z_landed(i):
        for part in range(s.PC):
            rows = pl.ds(part * piece_rows, piece_rows)
            remote(
                dyr.at[i, rows], zall.at[h, i, rows], zp_send.at[0], zp_recv.at[i * s.PC + part], i * N + h, far
            ).wait_recv()

    def z_go(n):
        if isinstance(n, int):
            if n < s.ZP:
                if n >= DEPTH:
                    z_piece(n - DEPTH).wait_send()
                z_piece(n).start()
        else:

            @pl.when(n < s.ZP)
            def _():
                z_piece(n - DEPTH).wait_send()
                z_piece(n).start()

    def n_copy(i, j):
        a, b = ((us, ur), (ds_, dr))[i]
        return remote(a.at[j - 1], b.at[j - 1], wn_send.at[i, j], wn_recv.at[i, j], w, lax.rem(h + j, N))

    def b_copy(j, slab):
        return remote(bs.at[j - 1], br.at[slab], wn_send.at[2, j], wn_recv.at[2, j], w, lax.rem(h + j, N))

    def hid_cols(owner, c):
        return pl.ds(align((owner * per + c) * FC, 128), FC)

    def up_part(owner, c):
        return dot_tn(x[...].reshape(s.ROWS, D), quad[pg_rows(owner * per + c), 0:FC])

    def down_part(owner, c):
        return dot_tn(hot[:, hid_cols(owner, c)], og[...])

    def pg_sum(owner, c):
        return jnp.sum(quad[pg_rows(owner * per + c), 0:FC].astype(F32), axis=0, keepdims=True)

    og_sum = jnp.sum(og[...].astype(F32), axis=0, keepdims=True)
    span = min(FL, D)

    def put_bias(ref):
        for b in range(D // span):
            ref[1 + b : 2 + b, 0:span] = og_sum[:, b * span : (b + 1) * span]

    for j in range(1, N):
        owner = lax.rem(h + j, N)
        for c in range(per):
            cols = slice(c * FC, (c + 1) * FC)
            us[j - 1, :, cols] = up_part(owner, c).astype(BF)
        n_copy(0, j).start()
        for c in range(per):
            cols = slice(c * FC, (c + 1) * FC)
            ds_[j - 1, cols, :] = down_part(owner, c).astype(BF)
        n_copy(1, j).start()
        for c in range(per):
            cols = slice(c * FC, (c + 1) * FC)
            bs[j - 1, 0:1, cols] = pg_sum(owner, c)
        put_bias(bs.at[j - 1])
        b_copy(j, h).start()
    def go_copy(i, c):
        cols = pl.ds(c * FC, FC)
        if i == 0:
            return pltpu.make_async_copy(stage.at[c, :, pl.ds(0, FC)], gu_out.at[:, cols], go_sem.at[c])
        return pltpu.make_async_copy(stage.at[c, pl.ds(0, FC), :], gd_out.at[cols, :], go_sem.at[c])

    for c in range(per):
        cols = slice(c * FC, (c + 1) * FC)
        total = up_part(h, c)
        for j in range(1, N):
            if c == 0:
                n_copy(0, j).wait_recv()
            total += ur[j - 1, :, cols].astype(F32)
        stage[c, :, 0:FC] = total.astype(BF)
        go_copy(0, c).start()
        gub_out[:, cols] = pg_sum(h, c)
    for c in range(per):
        cols = slice(c * FC, (c + 1) * FC)
        total = down_part(h, c)
        for j in range(1, N):
            if c == 0:
                n_copy(1, j).wait_recv()
            total += dr[j - 1, cols, :].astype(F32)
        go_copy(0, c).wait()
        stage[c, 0:FC, :] = total.astype(BF)
        go_copy(1, c).start()
    put_bias(br.at[h])

    for n in range(DEPTH):
        z_go(n)

    @pl.loop(0, s.NCH)
    def _(c):
        rows = pl.ds(align(h * TL + c * CH, 16), CH)
        hit = jnp.logical_or(pcol[rows, 0:1] == svals[...], pcol[rows, 1:2] == svals[...])
        hot[pl.ds(align(c * CH, 16), CH), 0 : E * Rb] = jnp.where(hit, 1.0, 0.0).astype(BF)

    def pass_on(buffer, send, recv, i, j, src=None):
        part = buffer.at[h if src is None else src, i]
        return remote(part, part, send.at[i, j], recv.at[i, j], w, lax.rem(h + j, N) if src is None else src)

    @pl.loop(0, s.NR)
    def _(c):
        for k in range(2):
            i = send_pair(c) * 2 + k
            swap_r.wait_recv(i)
            for j in range(1, N):
                pass_on(rg_all, rf_send, rf_recv, i, j).start()


    for j in range(1, N):
        src = lax.rem(h + N - j, N)
        b_copy(j, src).wait_recv()
        gub_out[...] += br[src, 0:1, :]
    for b in range(D // span):
        gdb_out[:, b * span : (b + 1) * span] = sum(br[j, 1 + b : 2 + b, 0:span] for j in range(N))

    @pl.loop(0, s.PW)
    def _(i):
        for j in range(1, N):
            pass_on(rg_all, rf_send, rf_recv, i, j, lax.rem(h + N - j, N)).wait_recv()

    small[...] = jnp.zeros(small.shape, F32)
    small[0:E, :] = grt[...]

    def add_row(r, value):
        small[r : r + 1, :] += jnp.sum(value, axis=0, keepdims=True)

    load_ags.wait()

    @pl.loop(0, s.PW)
    def _(i):
        swap_x.wait_send(i)

    @pl.loop(0, s.NCH)
    def _(c):
        rows = pl.ds(align(c * CH, 16), CH)
        z_go(c + DEPTH)
        moe_grad = dot(hot[rows, 0 : E * Rb], rg_all[...].reshape(E * Rb, D))
        normed, inv = norm_parts(ress[rows, :])
        add_row(E + 2, moe_grad * normed)
        add_row(E + 3, moe_grad)
        total = ags[rows, :].astype(F32) + norm_pull(moe_grad, normed, inv, g2[...])
        rgrad[rows, :] = total
        ag = total.astype(BF)
        ags[rows, :] = ag
        add_row(E + 4, ag.astype(F32))
        snd_x[rows, :] = dot_nt(ag, wp[...].reshape(D, D)).astype(BF)

    def attend_back(part, start, stop):
        heads = range(part, HP, s.halves)

        @pl.loop(start, stop)
        def _(c):
            units = [u for m in range(s.IMG) for u in image_units(c, m, heads)]
            inputs = [
                (split_heads(snd_x[im, cols]), qs[im, cols], ks[im, cols], vs[im, cols], ps[u])
                for im, cols, u in units
            ]
            pgrads = [dot_nt(v, both) for both, _q, _k, v, _p in inputs]
            vgrads = [dot(low, both) for both, _q, _k, _v, low in inputs]
            sgrads = []
            for pgrad, (_b, _q, _k, _v, low) in zip(pgrads, inputs):
                probs = low.astype(F32)
                sgrads.append((probs * (pgrad - jnp.sum(pgrad * probs, axis=0, keepdims=True))).astype(BF))
            qgrads = [dot_tn(sg, one[2]) for sg, one in zip(sgrads, inputs)]
            kgrads = [dot(sg, split_heads(one[1])) for sg, one in zip(sgrads, inputs)]
            for (im, cols, _u), qg, kg, vg in zip(units, qgrads, kgrads, vgrads):
                qs[im, cols] = join_heads(qg * (HEAD_DIM ** (-0.5))).astype(BF)
                ks[im, cols] = kg.astype(BF)
                vs[im, cols] = vg.astype(BF)

    class Job:
        def __init__(self, n):
            self.n, self.rows = n, s.jobs[n]
            self.gsend, self.gnar, self.gown, self.rbuf, self.gfin = job_refs[n]
            self.sbuf = self.gsend.at[0]

        def n_copy(self, rel, narrow_place):
            return remote(
                self.gsend.at[rel], self.gnar.at[rel], n_send.at[self.n, rel], n_recv.at[self.n, rel], w, narrow_place
            )

        def begin(self):
            LW = s.LW
            if self.n == 0:
                lower = dot_tn(atts[...], ags[...])
            else:
                first_cols = [j * L + (self.n - 1) * LW for j in range(N)]
                right = jnp.concatenate([dd[:, a : a + LW] for dd in (qs, ks, vs) for a in first_cols], axis=1)
                upper = dot_tn(ains[...], right)
            for j in range(N):
                if self.n == 0:
                    parts = [(b * L, lower[j * L : (j + 1) * L, b * LW : (b + 1) * LW]) for b in range(D // LW)]
                else:
                    parts = [(i * D, upper[:, (i * N + j) * LW : (i * N + j + 1) * LW]) for i in range(3)]

                def put(ref, cast, parts=parts):
                    for r, value in parts:
                        ref[r : r + value.shape[0], :] = value.astype(cast)

                @pl.when(h == j)
                def _():
                    put(self.gown, F32)

                @pl.when(h != j)
                def _():
                    rel = lax.rem(j - h + N, N) - 1
                    put(self.gsend.at[rel], BF)
                    self.n_copy(rel, j).start()

        def join(self):
            for j in range(1, N):
                self.n_copy(j - 1, lax.rem(h + N - j, N)).wait_recv()
                self.gown[...] += self.gnar[j - 1].astype(F32)
            for j in range(1, N):
                self.n_copy(j - 1, lax.rem(h + j, N)).wait_send()

        def part(self, f, place_in_team):
            size = self.rows // s.near
            if f == 0:
                return pl.ds(align(place_in_team * size, 16), size)
            piece = size // s.teams[1]
            return pl.ds(align(spot[0] * size + place_in_team * piece, 16), piece)

        def others(self, f):
            return [lax.rem(spot[f] + r, s.teams[f]) for r in range(1, s.teams[f])]

        def fold(self, f, other, land):
            return remote(
                self.sbuf.at[self.part(f, other)], self.rbuf.at[self.part(f, land)],
                h_send.at[self.n, f, other], h_recv.at[self.n, f, land], mate(f, other), h,
            )

        def grow(self, f, other, land):
            return remote(
                self.gfin.at[self.part(f, spot[f])], self.gfin.at[self.part(f, land)],
                a_send.at[self.n, f, other], a_recv.at[self.n, f, land], mate(f, other), h,
            )

        def start(self, q):
            f = min(q, 3 - q)
            for other in self.others(f):
                if q < 2:
                    rows = self.part(f, other)
                    self.sbuf[rows, :] = self.gown[rows, :].astype(BF)
                    self.fold(f, other, spot[f]).start()
                else:
                    self.grow(f, other, spot[f]).start()

        def end(self, q):
            f = min(q, 3 - q)
            own = self.part(f, spot[f])
            if q < 2:
                total = self.gown[own, :]
                for other in self.others(f):
                    self.fold(f, other, other).wait()
                    total += self.rbuf[self.part(f, other), :].astype(F32)
                if q == 0:
                    self.gown[own, :] = total
                else:
                    self.gfin[own, :] = total.astype(BF)
            else:
                for other in self.others(f):
                    self.grow(f, other, other).wait()

        def turn(self, q):
            self.end(q)
            if q < 3:
                self.start(q + 1)

        def finish(self):
            return pltpu.make_async_copy(self.gfin, gbigs[self.n], fin_sem.at[self.n])

    def s_copy(f, other, land):
        return remote(
            sacc.at[f], srec.at[f, land], s_send.at[f, other], s_recv.at[f, land], mate(f, other), h
        )

    def s_others(f):
        return [lax.rem(spot[f] + r, s.teams[f]) for r in range(1, s.teams[f])]

    def s_start(f):
        srec[f, spot[f]] = sacc[f]
        for other in s_others(f):
            s_copy(f, other, spot[f]).start()

    def s_end(f):
        for other in s_others(f):
            s_copy(f, other, other).wait()
        return sum(srec[f, i] for i in range(s.teams[f]))

    def tok_copy(src, dst, send, recv, c, j):
        here = pl.ds(align(c * CH, 16), CH)
        there = pl.ds(align(h * TL + c * CH, 16), CH)
        return remote(src.at[here], dst.at[there], send.at[c, j], recv.at[c, j], w, lax.rem(h + j, N))

    def tok_local(src, dst, sem, c):
        here = pl.ds(align(c * CH, 16), CH)
        there = pl.ds(align(h * TL + c * CH, 16), CH)
        return pltpu.make_async_copy(src.at[here], dst.at[there], sem.at[c])

    def bias_sums():
        small[E + 5 : E + 6, :] = jnp.sum(qs[...].astype(F32), axis=0, keepdims=True)
        small[E + 6 : E + 7, :] = jnp.sum(vs[...].astype(F32), axis=0, keepdims=True)

    def first_norm_part(start, stop):
        @pl.loop(start, stop)
        def _(c):
            rows = pl.ds(align(c * CH, 16), CH)
            back = jnp.zeros((CH, D), F32)
            for j in range(N):
                cols = slice(j * L, (j + 1) * L)
                for i, dd in enumerate((qs, ks, vs)):
                    back += dot_nt(dd[rows, cols], wq[j, i])
            normed, inv = norm_parts(tokv[rows, :].astype(F32))
            add_row(E, back * normed)
            add_row(E + 1, back)
            ags[rows, :] = (rgrad[rows, :] + norm_pull(back, normed, inv, g1[...])).astype(BF)
            for j in range(1, N):
                tok_copy(ags, gtok, g_send, g_recv, c, j).start()
            tok_local(ags, gtok, g_loc, c).start()

    def small_send():
        for b in range(D // 128):
            snar[h, b * s.RP : (b + 1) * s.RP, :] = small[:, b * 128 : (b + 1) * 128]
        for j in range(1, N):
            remote(snar.at[h], snar.at[h], sn_send.at[j], sn_recv.at[j], w, lax.rem(h + j, N)).start()

    def combine_pass():
        for n in range(z_next + 1, s.ZP):
            z_go(n)

        @pl.loop(0, s.NR // 2)
        def _(c):
            for k in range(4):
                i = send_pair(2 * c + 1 - k // 2) * 2 + k % 2
                if k < 2:
                    swap_z.wait_recv(i)
                else:
                    z_landed(i)
                for j in range(1, N):
                    pass_on(zall, zf_send, zf_recv, i, j).start()

    def combine_wait():
        @pl.loop(0, s.PW)
        def _(i):
            for j in range(1, N):
                pass_on(zall, zf_send, zf_recv, i, j, lax.rem(h + N - j, N)).wait_recv()

    def combine(start, stop):
        @pl.loop(start, stop)
        def _(c):
            rows = pl.ds(align(c * CH, 16), CH)
            mixed = dot(hot[rows, 0 : E * Rb], zall[...].reshape(E * Rb, D))
            ains[rows, :] = (ress[rows, :] + mixed).astype(BF)
            for j in range(1, N):
                tok_copy(ains, out, o_send, o_recv, c, j).start()
            tok_local(ains, out, o_loc, c).start()

    def small_narrow():
        for j in range(1, N):
            src = lax.rem(h + N - j, N)
            remote(snar.at[h], snar.at[h], sn_send.at[j], sn_recv.at[j], w, src).wait_send()
            remote(snar.at[src], snar.at[src], sn_send.at[j], sn_recv.at[j], w, src).wait_recv()
        sacc[0] = sum(snar[j] for j in range(N))

    jobs = [Job(n) for n in range(NJ)]
    steps = 4
    middle = s.NCH // 2
    z_next = DEPTH + s.NCH
    jobs[0].begin()
    attend_back(0, 0, middle)
    jobs[0].join()
    jobs[0].start(0)
    attend_back(0, middle, s.NCH)
    z_go(z_next)
    jobs[1].begin()
    at = [0] * NJ
    if NJ == 3:
        jobs[0].turn(0)
        attend_back(1, 0, middle)
        z_next += 1
        z_go(z_next)
        jobs[1].join()
        jobs[1].start(0)
        attend_back(1, middle, s.NCH)
        z_next += 1
        z_go(z_next)
        jobs[0].turn(1)
        jobs[2].begin()
        jobs[1].turn(0)
        jobs[2].join()
        jobs[2].start(0)
        at = [2, 1, 0]
    else:
        jobs[1].join()
        jobs[1].start(0)
    turn = 0
    while min(at) < steps:
        z_next += 1
        z_go(z_next)
        if turn == 0:
            bias_sums()
        if turn < LN_TURNS:
            first_norm_part(turn * s.NCH // LN_TURNS, (turn + 1) * s.NCH // LN_TURNS)
        if turn == LN_TURNS - 1:
            small_send()
        if turn == LN_TURNS:
            small_narrow()
            s_start(0)
        if turn == LN_TURNS + 1:
            sacc[1] = s_end(0)
            s_start(1)
        if turn == MIX_TURN:
            combine_pass()
        if turn == MIX_TURN + 1:
            combine_wait()
            combine(0, s.NCH)
        for n in range(NJ):
            if at[n] < steps:
                jobs[n].turn(at[n])
                at[n] += 1
                if at[n] == steps:
                    jobs[n].finish().start()
        turn += 1
    gsmall[...] = s_end(1)

    for j in range(1, N):
        for i in range(2):
            n_copy(i, j).wait_send()
        b_copy(j, h).wait_send()

    @pl.loop(0, s.PW)
    def _(i):
        swap_r.wait_send(i)
        for j in range(1, N):
            pass_on(rg_all, rf_send, rf_recv, i, j).wait_send()
            pass_on(zall, zf_send, zf_recv, i, j).wait_send()

    @pl.loop(0, s.NCH)
    def _(c):
        tok_local(ags, gtok, g_loc, c).wait()
        tok_local(ains, out, o_loc, c).wait()
        here = pl.ds(align(c * CH, 16), CH)
        for j in range(1, N):
            src = lax.rem(h + N - j, N)
            there = pl.ds(align(src * TL + c * CH, 16), CH)
            tok_copy(ags, gtok, g_send, g_recv, c, j).wait_send()
            tok_copy(ains, out, o_send, o_recv, c, j).wait_send()
            remote(ags.at[here], gtok.at[there], g_send.at[c, j], g_recv.at[c, j], w, src).wait_recv()
            remote(ains.at[here], out.at[there], o_send.at[c, j], o_recv.at[c, j], w, src).wait_recv()

    for c in range(per):
        go_copy(1, c).wait()
    @pl.loop(0, s.NR // 2)
    def _(c):
        for k in range(2):
            swap_z.wait_send(send_pair(2 * c + 1) * 2 + k)

    for n in range(max(0, s.ZP - DEPTH), s.ZP):
        z_piece(n).wait_send()
    for job in jobs:
        job.finish().wait()


def post_kernel(s, *refs):
    (
        out_in, gtok_in, gu_in, gd_in, flat, gub_in, gdb_in, *rest,
    ) = refs
    bigs, rest = rest[: len(s.jobs)], rest[len(s.jobs) :]
    (
        out, gtok, gu, gd, gqkv, gproj, gag, gas, gmg, gms, gpb, gqv, grouter, gub, gdb,
        b_out, b_tok, b_gu, b_gd, f_tok, f_gu, f_gd, l_sem, s_sem,
    ) = rest
    moves = (
        (gtok_in, b_tok, f_tok, gtok), (gu_in, b_gu, f_gu, gu), (gd_in, b_gd, f_gd, gd), (out_in, b_out, b_out, out),
    )
    loads, stores, widen = [], [], []
    for i, (a, b, f, c) in enumerate(moves):
        step = a.shape[0] // PARTS
        for p in range(PARTS):
            part = pl.ds(p * step, step)
            loads.append(pltpu.make_async_copy(a.at[part], b.at[part], l_sem.at[i, p]))
            stores.append(pltpu.make_async_copy(f.at[part], c.at[part], s_sem.at[i, p]))
            widen.append((b, f, slice(p * step, (p + 1) * step)))
    for load in loads:
        load.start()
    D, L, N, E, LW = s.D, s.L, s.N, s.E, s.LW
    h = lax.axis_index("narrow")
    for load, store, (b, f, part) in zip(loads, stores, widen):
        load.wait()
        if b is not f:
            f[part, :] = b[part, :].astype(F32)
        store.start()
    for n, big in enumerate(bigs[1:]):
        for i in range(3):
            gqkv[i, :, n * LW : (n + 1) * LW] = big[i * D : (i + 1) * D, :].astype(F32)
    for b in range(D // LW):
        gproj[:, b * LW : (b + 1) * LW] = bigs[0][b * L : (b + 1) * L, :].astype(F32)

    def rows(r, count):
        return jnp.concatenate([flat[b * s.RP + r : b * s.RP + r + count, :] for b in range(D // 128)], axis=1)

    gub[...] = gub_in[...]
    gdb[...] = gdb_in[...]
    grouter[...] = rows(0, E)
    for r, ref in ((E, gag), (E + 1, gas), (E + 2, gmg), (E + 3, gms), (E + 4, gpb)):
        ref[...] = rows(r, 1)
    qv = rows(E + 5, 2)
    for j in range(N):

        @pl.when(h == j)
        def _():
            gqv[...] = qv[:, j * L : (j + 1) * L]

    for store in stores:
        store.wait()


VM = pl.BlockSpec(memory_space=pltpu.VMEM)
ANY = pl.BlockSpec(memory_space=pl.ANY)
HB = pl.BlockSpec(memory_space=pltpu.HBM)
DMA = pltpu.SemaphoreType.DMA
V = pltpu.VMEM


def shards(
    wide,
    narrow,
    tokens,
    attn_gain,
    attn_shift,
    qkv_weight,
    query_value_bias,
    proj_weight,
    proj_bias,
    moe_gain,
    moe_shift,
    router_weight,
    expert_up,
    expert_up_bias,
    expert_down,
    expert_down_bias,
    routes,
    slot_index,
    cotangent,
):
    s = Sizes(wide, narrow, tokens.shape[0], tokens.shape[1], router_weight.shape[1], expert_up.shape[2])
    T, D, E, N, W, L, TL = s.T, s.D, s.E, s.N, s.W, s.L, s.TL
    PW, Rb, FL, ROWS, RC, NCH = s.PW, s.Rb, s.FL, s.ROWS, s.RC, s.NCH
    slot = np.arange(E * Rb)
    half, rest = slot // (PW * Rb), slot % (PW * Rb)
    pos, inner = rest // Rb, rest % Rb
    svals = np.where(inner < s.cap, (pos * N + half) * s.cap + inner, -2).astype(np.int32)[None, :]
    row = lambda a: a.reshape(1, -1)
    blk = (PW, Rb, D)
    heads = (TL // PATCHES) * s.HP
    TM = max(s.teams)
    ins = [
        (ANY, tokens), (ANY, cotangent), (VM, row(attn_gain)), (VM, row(attn_shift)),
        (ANY, qkv_weight.transpose(1, 0, 2)), (ANY, query_value_bias), (ANY, proj_weight), (VM, row(proj_bias)),
        (VM, row(moe_gain)), (VM, row(moe_shift)), (VM, router_weight.T), (ANY, expert_up[0]),
        (ANY, expert_up_bias), (ANY, expert_down[0]), (VM, expert_down_bias), (VM, routes.T), (VM, slot_index.T),
        (VM, jnp.asarray(svals)),
    ]
    outs = [
        (ANY, (T, D), BF), (ANY, (T, D), BF), (VM, (s.RPS, 128), F32),
        (ANY, (D, FL), BF), (ANY, (FL, D), BF), (VM, (1, FL), F32), (VM, (1, D), F32),
    ] + [(ANY, (r, s.LW), BF) for r in s.jobs]
    scratch = [
        V((TL, D), BF), V((N, 3, D, L), BF), V((N, L, D), BF), V((N, 2, L), F32), V((T, 8), jnp.int32),
        V((ROWS, max(T, E * Rb)), BF), V((2 * T, D), BF), V((TL, D), BF), V((TL, D), BF), V((TL, D), BF),
        V((heads, PATCHES, 2 * PATCHES), BF), V((TL, D), BF), V((TL, D), BF), V((TL, D), F32), V((ROWS, D), BF), V((ROWS, D), BF),
        V(blk, BF), V(blk, BF), V((N, D, FL), BF), V((N, FL, D), BF), V((N, 1, FL), F32), V((ROWS, D), BF),
        V((RC, D), F32), V((RC, D), F32), V((N - 1, D, FL), BF), V((N - 1, FL, D), BF), V((N - 1, D, FL), BF),
        V((N - 1, FL, D), BF), V((N - 1, 8, FL), F32), V((N, 8, FL), F32), V((FL // s.FC, D, D), BF),
        V((E, D), F32),
        V((N,) + blk, BF), V((N,) + blk, BF), V((TL, D), BF), V((TL, D), F32),
        V((s.RP, D), F32), V((N, s.RPS, 128), F32), V((2, s.RPS, 128), F32),
        V((2, max(s.teams), s.RPS, 128), F32),
    ]
    for r in s.jobs:
        scratch += [V((N - 1, r, s.LW), BF), V((N - 1, r, s.LW), BF), V((r, s.LW), F32)]
        scratch += [V((r, s.LW), BF), V((r, s.LW), BF)]
    NJ = len(s.jobs)
    scratch += [
        DMA((2,)), DMA((6,)), DMA((6, N)), DMA((6, N)), DMA((NCH, N)), DMA((NCH, N)),
        DMA((PW,)), DMA((PW,)), DMA((PW,)), DMA((PW,)), DMA((PW,)), DMA((PW,)),
        DMA((PW,)), DMA((PW,)), DMA((s.ZP,)), DMA((PW * s.PC,)), DMA((4,)), DMA((PW, N)), DMA((PW, N)), DMA((PW, N)), DMA((PW, N)),
        DMA((3, N)), DMA((3, N)), DMA((FL // s.FC,)),
        DMA((NJ, N)), DMA((NJ, N)), DMA((N,)), DMA((N,)), DMA((NJ, 2, TM)), DMA((NJ, 2, TM)),
        DMA((NJ, 2, TM)), DMA((NJ, 2, TM)), DMA((2, TM)), DMA((2, TM)),
        DMA((NCH, N)), DMA((NCH, N)), DMA((NCH, N)), DMA((NCH, N)), DMA((NCH,)), DMA((NCH,)), DMA((NJ,)),
    ]
    out, gtok, gsmall, gu, gd, gub, gdb, *gbigs = pl.pallas_call(
        functools.partial(block_kernel, s),
        in_specs=[spec for spec, _ in ins],
        out_specs=[spec for spec, _, _ in outs],
        out_shape=[jax.ShapeDtypeStruct(shape, dtype) for _, shape, dtype in outs],
        scratch_shapes=scratch,
        compiler_params=pltpu.CompilerParams(
            collective_id=1, has_side_effects=True, vmem_limit_bytes=VMEM_MB << 20
        ),
        name="block",
    )(*[a for _, a in ins])

    post_ins = [(HB, out), (HB, gtok), (HB, gu), (HB, gd), (VM, gsmall), (VM, gub), (VM, gdb)]
    post_ins += [(VM, a) for a in gbigs]
    post_outs = [
        (ANY, (T, D), BF), (ANY, (T, D), F32), (ANY, (D, FL), F32), (ANY, (FL, D), F32), (VM, (3, D, L), F32),
        (VM, (L, D), F32), (VM, (1, D), F32), (VM, (1, D), F32), (VM, (1, D), F32), (VM, (1, D), F32),
        (VM, (1, D), F32), (VM, (2, L), F32), (VM, (E, D), F32), (VM, (1, FL), F32), (VM, (1, D), F32),
    ]
    out, gtok, gu, gd, gqkv, gproj, gag, gas, gmg, gms, gpb, gqv, grouter, gub, gdb = pl.pallas_call(
        functools.partial(post_kernel, s),
        in_specs=[spec for spec, _ in post_ins],
        out_specs=[spec for spec, _, _ in post_outs],
        out_shape=[jax.ShapeDtypeStruct(shape, dtype) for _, shape, dtype in post_outs],
        scratch_shapes=[
            V((T, D), BF), V((T, D), BF), V((D, FL), BF), V((FL, D), BF), V((T, D), F32), V((D, FL), F32),
            V((FL, D), F32), DMA((4, PARTS)), DMA((4, PARTS)),
        ],
        compiler_params=pltpu.CompilerParams(vmem_limit_bytes=VMEM_MB << 20),
        name="post",
    )(*[a for _, a in post_ins])
    return (
        out,
        gtok,
        gag.reshape(D),
        gas.reshape(D),
        gqkv.transpose(1, 0, 2),
        gqv,
        gproj,
        gpb.reshape(D),
        gmg.reshape(D),
        gms.reshape(D),
        grouter.T,
        gu[None],
        gub,
        gd[None],
        gdb,
    )


def solution(mesh):
    in_specs = (
        P("wide", None),
        P(),
        P(),
        P(None, None, "narrow"),
        P(None, "narrow"),
        P("narrow", None),
        P(),
        P(),
        P(),
        P(),
        P("wide", None, "narrow"),
        P("wide", "narrow"),
        P("wide", "narrow", None),
        P("wide", None),
        P("wide", None),
        P("wide", None),
        P("wide", None),
    )
    out_specs = (
        P("wide", None),
        P("wide", None),
        P(),
        P(),
        P(None, None, "narrow"),
        P(None, "narrow"),
        P("narrow", None),
        P(),
        P(),
        P(),
        P(),
        P("wide", None, "narrow"),
        P("wide", "narrow"),
        P("wide", "narrow", None),
        P("wide", None),
    )
    body = functools.partial(shards, mesh.shape["wide"], mesh.shape["narrow"])
    return jax.shard_map(body, mesh=mesh, in_specs=in_specs, out_specs=out_specs, check_vma=False)
```

```python
import functools

import jax
import jax.numpy as jnp
import numpy as np
from jax import lax
from jax.experimental import pallas as pl
from jax.experimental.pallas import tpu as pltpu
from jax.sharding import PartitionSpec as P

PATCHES = 144
HEAD_DIM = 64
EPSILON = 1e-06
MESH = pl.DeviceIdType.MESH
BF = jnp.bfloat16
F32 = jnp.float32
GELU_C = 0.7978845608028654
GELU_A = 0.044715
VMEM_MB = 63
PARTS = 2
DEPTH = 5
LN_TURNS = 1
MIX_TURN = 2


def dot(a, b):
    return jnp.dot(a, b, preferred_element_type=F32)


def dot_nt(a, b):
    return lax.dot_general(a, b, (((1,), (1,)), ((), ())), preferred_element_type=F32)


def dot_tn(a, b):
    return lax.dot_general(a, b, (((0,), (0,)), ((), ())), preferred_element_type=F32)


def norm_parts(values):
    center = values - jnp.mean(values, axis=-1, keepdims=True)
    inv_root = lax.rsqrt(jnp.mean(center * center, axis=-1, keepdims=True) + EPSILON)
    return center * inv_root, inv_root


def norm_pull(upstream, normed, inv_root, norm_gain):
    scaled = upstream * norm_gain
    bracket = (
        scaled
        - jnp.mean(scaled, axis=-1, keepdims=True)
        - normed * jnp.mean(scaled * normed, axis=-1, keepdims=True)
    )
    return inv_root * bracket


class Sizes:
    def __init__(self, wide, narrow, tokens, width, experts, local_ff):
        self.W, self.N = wide, narrow
        self.T, self.D, self.E = tokens, width, experts
        self.TL = tokens // narrow
        self.cap = tokens // experts
        self.PW = wide // narrow
        self.Rb = -(-self.cap // 16) * 16
        self.L = width // narrow
        self.FL = local_ff
        self.CH = 2 * PATCHES
        self.NCH = self.TL // self.CH
        self.IMG = self.CH // PATCHES
        self.HP = width // (2 * HEAD_DIM)
        self.ROWS = self.PW * self.Rb
        self.RC = 2 * self.Rb
        self.PC = 3 if self.Rb % 48 == 0 else 1
        self.ZP = self.PW // 2 * self.PC
        self.NR = self.PW // 2
        self.FC = min(512, local_ff)
        self.NF = narrow * local_ff // self.FC
        self.LW = min(128, self.L)
        self.halves = 2 if self.L == 256 else 1
        self.jobs = [width // self.LW * self.L] + [3 * width] * self.halves
        self.RP = -(-(experts + 7) // 8) * 8
        self.RPS = self.RP * (width // 128)
        self.near = min(4, wide)
        self.teams = (self.near, wide // self.near)


def place():
    return lax.axis_index("wide"), lax.axis_index("narrow")


def signal(sem, wide, narrow):
    pl.semaphore_signal(sem, 1, device_id=(wide, narrow), device_id_type=MESH)


def remote(src, dst, send, recv, wide, narrow):
    return pltpu.make_async_remote_copy(
        src, dst, send, recv, device_id=(wide, narrow), device_id_type=MESH
    )


class Swap:
    def __init__(self, s, src, dst, send, recv, local, half=False):
        self.s, self.src = s, src
        self.send, self.recv, self.local = send, recv, local
        w, h = place()
        self.w, self.h = w, h
        self.far = lax.rem(w, s.N)
        self.slot = w // s.N
        self.dst = dst.at[self.far] if half else dst
        self.land = dst.at[h] if half else dst

    def at(self, i):
        if len(self.src.shape) == 2:
            return self.src.at[pl.ds(align(i * self.s.Rb, 16), self.s.Rb)]
        return self.src.at[i]

    def own(self, i):
        return jnp.logical_and(self.far == self.h, i == self.slot)

    def start(self, i):
        @pl.when(jnp.logical_not(self.own(i)))
        def _():
            remote(
                self.at(i),
                self.dst.at[self.slot],
                self.send.at[i],
                self.recv.at[self.slot],
                i * self.s.N + self.h,
                self.far,
            ).start()

        @pl.when(self.own(i))
        def _():
            pltpu.make_async_copy(self.at(i), self.dst.at[self.slot], self.local).start()

    def there(self, i):
        return remote(
            self.at(i),
            self.land.at[i],
            self.send.at[i],
            self.recv.at[i],
            i * self.s.N + self.h,
            self.far,
        )

    def wait_send(self, i):
        @pl.when(jnp.logical_not(self.own(i)))
        def _():
            self.there(i).wait_send()

    def wait_recv(self, i):
        @pl.when(jnp.logical_not(self.own(i)))
        def _():
            self.there(i).wait_recv()

        @pl.when(self.own(i))
        def _():
            pltpu.make_async_copy(self.at(i), self.land.at[i], self.local).wait()


def mix_bits(value, other, count):
    total = 0
    for b in range(count):
        p, q = lax.rem(value // (1 << b), 2), lax.rem(other // (1 << b), 2)
        total = total + (p + q - 2 * p * q) * (1 << b)
    return total


def align(x, m):
    return pl.multiple_of(x, m)


def block_kernel(s, *refs):
    (
        tok, cot, g1, b1, wq_loc, qvb_loc, wp_loc, pb, g2, b2, wr, up_loc, ub_loc, dn_loc, db,
        routes, slots, svals,
        out, gtok, gsmall, gu_out, gd_out, gub_out, gdb_out, *rest,
    ) = refs
    gbigs, rest = rest[: len(s.jobs)], rest[len(s.jobs) :]
    (
        tokv, wq, wp, qvb, pcol, hot, quad, qs, ks, vs, ps, atts, ains, ress, snd_x, snd_dy,
        x, dyr, up, dn, ub, og, ysum, rsum, us, ds_, ur, dr, bs, br, stage, grt,
        rg_all, zall, ags, rgrad, small, snar, sacc, srec, *more,
    ) = rest
    NJ = len(s.jobs)
    job_refs = [more[5 * n : 5 * n + 5] for n in range(NJ)]
    (
        ld_sem, own_sem, w_send, w_recv, m_send, m_recv, x_send, x_recv, d_send, d_recv, r_send, r_recv,
        z_send, z_recv, zp_send, zp_recv, l_sem, rf_send, rf_recv, zf_send, zf_recv, wn_send, wn_recv, go_sem,
        n_send, n_recv, sn_send, sn_recv, h_send, h_recv, a_send, a_recv, s_send, s_recv,
        o_send, o_recv, g_send, g_recv, o_loc, g_loc, fin_sem,
    ) = more[5 * NJ :]
    w, h = place()
    N, W, T, TL, CH, L, D, E = s.N, s.W, s.T, s.TL, s.CH, s.L, s.D, s.E
    RC, FC, FL, HP, Rb, NF = s.RC, s.FC, s.FL, s.HP, s.Rb, s.NF
    far = lax.rem(w, N)
    slot = w // N
    prime = slot // 2
    pair_bits = s.NR.bit_length() - 1

    barrier = pltpu.get_barrier_semaphore()

    @pl.loop(0, s.PW)
    def _(i):
        @pl.when(jnp.logical_or(far != h, i != slot))
        def _():
            signal(barrier, i * N + h, far)

    for j in range(1, N):
        signal(barrier, w, lax.rem(h + j, N))
    spot = (lax.rem(w, s.near), w // s.near)

    def mate(team, place_in_team):
        return w + (place_in_team - spot[team]) * (1, s.near)[team]

    mates = [mate(f, lax.rem(spot[f] + r, s.teams[f])) for f in range(2) for r in range(1, s.teams[f])]
    extra = 0
    for other in mates:
        fresh = jnp.logical_or(far != h, lax.rem(other, N) != far)
        extra = extra + fresh.astype(jnp.int32)

        @pl.when(fresh)
        def _():
            signal(barrier, other, h)

    mine = pl.ds(align(h * TL, 16), TL)
    load_dy = pltpu.make_async_copy(cot, quad.at[pl.ds(0, T)], ld_sem.at[0])
    load_tok = pltpu.make_async_copy(tok.at[mine], tokv, ld_sem.at[1])
    load_dy.start()
    load_tok.start()
    pairs = ((wq_loc, wq), (wp_loc, wp), (qvb_loc, qvb), (up_loc, up), (dn_loc, dn), (ub_loc, ub))
    owns = [pltpu.make_async_copy(a, b.at[h], own_sem.at[i]) for i, (a, b) in enumerate(pairs)]
    for copy in owns:
        copy.start()

    slot_rows = slots[...]
    prow = jnp.where(slot_rows < s.cap, routes[...] * s.cap + slot_rows, -1)
    one_row, two_row = prow[0:1, :], prow[1:2, :]

    def build(pair):
        for k in range(2):
            i = pair * 2 + k
            row = lax.broadcasted_iota(jnp.int32, (Rb, 1), 0)
            value = jnp.where(row < s.cap, (i * N + h) * s.cap + row, -2)
            hit = jnp.logical_or(one_row == value, two_row == value)
            hot[pl.ds(align(i * Rb, 16), Rb), 0:T] = jnp.where(hit, 1.0, 0.0).astype(BF)

    def send_pair(c):
        return mix_bits(prime, s.NR - 1 - c // 2 - (s.NR // 2) * lax.rem(c, 2), pair_bits)

    build(send_pair(0))
    pl.semaphore_wait(
        barrier,
        s.PW + N - 1 + extra - (far == h).astype(jnp.int32),
    )

    def weight_copy(i, j):
        a, b = pairs[i]
        return remote(a, b.at[h], w_send.at[i, j], w_recv.at[i, j], w, lax.rem(h + j, N))

    for i in range(len(pairs)):
        for j in range(1, N):
            weight_copy(i, j).start()

    swap_d = Swap(s, snd_dy, dyr, d_send, d_recv, l_sem.at[0])
    swap_x = Swap(s, snd_x, x, x_send, x_recv, l_sem.at[1])
    swap_r = Swap(s, snd_dy, rg_all, r_send, r_recv, l_sem.at[2], True)
    swap_z = Swap(s, dyr, zall, z_send, z_recv, l_sem.at[3], True)

    def dispatch(first_row, buffer, swap, more):
        @pl.loop(0, s.NR)
        def _(c):
            pair = send_pair(c)
            rows = pl.ds(align(pair * RC, 16), RC)
            buffer[rows, :] = dot(hot[rows, 0:T], quad[pl.ds(first_row, T), :]).astype(BF)
            for k in range(2):
                swap.start(pair * 2 + k)
            more(c)

    def build_next(c):
        @pl.when(c + 1 < s.NR)
        def _():
            build(send_pair(c + 1))

    load_dy.wait()
    dispatch(0, snd_dy, swap_d, build_next)
    pcol[...] = jnp.transpose(jnp.concatenate([prow] * 4, axis=0))

    load_tok.wait()
    for copy in owns[:3]:
        copy.wait()
    for i in range(3):
        for j in range(1, N):
            weight_copy(i, j).wait_recv()

    def moe_copy(c, j):
        part = quad.at[pl.ds(align(T + h * TL + c * CH, 16), CH)]
        return remote(part, part, m_send.at[c, j], m_recv.at[c, j], w, lax.rem(h + j, N))

    def moe_from(c, j):
        src = lax.rem(h + N - j, N)
        part = quad.at[pl.ds(align(T + src * TL + c * CH, 16), CH)]
        return remote(part, part, m_send.at[c, j], m_recv.at[c, j], w, src)

    lane = lax.broadcasted_iota(jnp.int32, (PATCHES, 2 * HEAD_DIM), 1)
    first = lane < HEAD_DIM

    def split_heads(part):
        zero = jnp.zeros_like(part)
        return jnp.concatenate([jnp.where(first, part, zero), jnp.where(first, zero, part)], axis=0)

    def image_units(c, m, heads):
        image = pl.ds(align(c * CH + m * PATCHES, 16), PATCHES)
        return [
            (image, slice(2 * HEAD_DIM * p, 2 * HEAD_DIM * (p + 1)), (c * s.IMG + m) * HP + p) for p in heads
        ]

    def join_heads(both):
        return jnp.where(first, both[:PATCHES], both[PATCHES:])

    @pl.loop(0, s.NCH)
    def _(c):
        rows = pl.ds(align(c * CH, 16), CH)
        t = tokv[rows, :].astype(F32)
        normed, _r = norm_parts(t)
        ain = (normed * g1[...] + b1[...]).astype(BF)
        ains[rows, :] = ain
        for j in range(N):
            cols = slice(j * L, (j + 1) * L)
            q = (dot(ain, wq[j, 0]) + qvb[j, 0:1, :]).astype(BF)
            qs[rows, cols] = q * BF(HEAD_DIM ** (-0.5))
            ks[rows, cols] = dot(ain, wq[j, 1]).astype(BF)
            vs[rows, cols] = (dot(ain, wq[j, 2]) + qvb[j, 1:2, :]).astype(BF)
        for m in range(s.IMG):
            units = image_units(c, m, range(HP))
            inputs = [(split_heads(qs[im, cols]), ks[im, cols], vs[im, cols]) for im, cols, _u in units]
            scores = [dot_nt(k, q) for q, k, _v in inputs]
            grown = [jnp.exp(one - jnp.max(one, axis=0, keepdims=True)) for one in scores]
            probs = [(one * (1.0 / jnp.sum(one, axis=0, keepdims=True))).astype(BF) for one in grown]
            mixed = [join_heads(dot_tn(one, v)).astype(BF) for one, (_q, _k, v) in zip(probs, inputs)]
            for (im, cols, u), one, value in zip(units, probs, mixed):
                ps[u] = one
                atts[im, cols] = value
        residual = t + (dot(atts[rows, :], wp[...].reshape(D, D)) + pb[...])
        ress[rows, :] = residual
        normed, _r = norm_parts(residual)
        quad[pl.ds(align(T + h * TL + c * CH, 16), CH), :] = (normed * g2[...] + b2[...]).astype(BF)
        for j in range(1, N):
            moe_copy(c, j).start()

    @pl.loop(0, s.NCH)
    def _(c):
        for j in range(1, N):
            moe_from(c, j).wait_recv()

    dispatch(T, snd_x, swap_x, lambda c: None)

    @pl.loop(0, s.NCH)
    def _(c):
        for j in range(1, N):
            moe_copy(c, j).wait_send()

    for copy in owns[3:]:
        copy.wait()
    for i in range(len(pairs)):
        for j in range(1, N):
            if i >= 3:
                weight_copy(i, j).wait_recv()
            weight_copy(i, j).wait_send()

    @pl.loop(0, s.PW)
    def _(i):
        swap_d.wait_send(i)

    load_ags = pltpu.make_async_copy(cot.at[mine], ags, ld_sem.at[0])
    load_ags.start()
    per = FL // FC
    expert_lane = lax.broadcasted_iota(jnp.int32, (RC, E), 1)
    grt[...] = jnp.zeros(grt.shape, F32)

    def pg_rows(f):
        return pl.ds(align(f * s.ROWS, 16), s.ROWS)

    @pl.loop(0, s.NR)
    def _(c):
        pair = send_pair(c)
        rows = pl.ds(align(pair * RC, 16), RC)
        both = pl.ds(pair * 2, 2)
        for k in range(2):
            swap_d.wait_recv(pair * 2 + k)
            swap_x.wait_recv(pair * 2 + k)
        xr = x[both].reshape(RC, D)
        dyf = dyr[both].reshape(RC, D).astype(F32)
        logits = dot_nt(xr, wr[...])
        top = jnp.max(logits, axis=-1, keepdims=True)
        grown = jnp.exp(logits - top)
        probs = grown * (1.0 / jnp.sum(grown, axis=-1, keepdims=True))
        gate = jnp.sum(jnp.where(expert_lane == w, probs, 0.0), axis=-1, keepdims=True)
        og[rows, :] = (gate * dyf).astype(BF)
        ysum[...] = jnp.broadcast_to(db[...], (RC, D))
        rsum[...] = jnp.zeros((RC, D), F32)

        @pl.loop(0, NF)
        def _(f):
            j = f // per
            off = pl.ds(align(lax.rem(f, per) * FC, 128), FC)
            pre = dot(x[both].reshape(RC, D), up[j, :, off]) + ub[j, :, off]
            square = pre * pre
            t = jnp.tanh(GELU_C * (pre + GELU_A * (square * pre)))
            half = 0.5 * (1.0 + t)
            hidden = (pre * half).astype(BF)
            slope = half + (0.5 * GELU_C) * pre * (1.0 - t * t) * (1.0 + (3.0 * GELU_A) * square)
            grad = (dot_nt(og[rows, :], dn[j, off, :]) * slope).astype(BF)
            hot[rows, pl.ds(align(f * FC, 128), FC)] = hidden
            quad[pl.ds(align(f * s.ROWS + pair * RC, 16), RC), 0:FC] = grad
            ysum[...] += dot(hidden, dn[j, off, :])
            rsum[...] += dot_nt(grad, up[j, :, off])

        y = ysum[...].astype(BF).astype(F32)
        gate_grad = jnp.sum(dyf * y, axis=-1, keepdims=True)
        logit = (gate_grad * probs * (jnp.where(expert_lane == w, 1.0, 0.0) - gate)).astype(BF)
        back = (rsum[...] + dot(logit, wr[...])).astype(BF)
        snd_dy[rows, :] = back
        for k in range(2):
            swap_r.start(pair * 2 + k)
        zz = (gate * y).astype(BF)
        for k in range(2):
            dyr[pair * 2 + k] = zz[k * Rb : (k + 1) * Rb]

            @pl.when(lax.rem(c, 2) == 1)
            def _():
                swap_z.start(pair * 2 + k)

        grt[...] += dot_tn(logit, xr)

    piece_rows = Rb // s.PC

    def z_piece(n):
        block, part = n // s.PC, lax.rem(n, s.PC)
        i = send_pair(2 * (block // 2)) * 2 + lax.rem(block, 2)
        rows = pl.ds(align(part * piece_rows, 16), piece_rows)
        return remote(
            dyr.at[i, rows], zall.at[far, slot, rows], zp_send.at[n], zp_recv.at[slot * s.PC + part], i * N + h, far
        )

    def z_landed(i):
        for part in range(s.PC):
            rows = pl.ds(part * piece_rows, piece_rows)
            remote(
                dyr.at[i, rows], zall.at[h, i, rows], zp_send.at[0], zp_recv.at[i * s.PC + part], i * N + h, far
            ).wait_recv()

    def z_go(n):
        if isinstance(n, int):
            if n < s.ZP:
                if n >= DEPTH:
                    z_piece(n - DEPTH).wait_send()
                z_piece(n).start()
        else:

            @pl.when(n < s.ZP)
            def _():
                z_piece(n - DEPTH).wait_send()
                z_piece(n).start()

    def n_copy(i, j):
        a, b = ((us, ur), (ds_, dr))[i]
        return remote(a.at[j - 1], b.at[j - 1], wn_send.at[i, j], wn_recv.at[i, j], w, lax.rem(h + j, N))

    def b_copy(j, slab):
        return remote(bs.at[j - 1], br.at[slab], wn_send.at[2, j], wn_recv.at[2, j], w, lax.rem(h + j, N))

    def hid_cols(owner, c):
        return pl.ds(align((owner * per + c) * FC, 128), FC)

    def up_part(owner, c):
        return dot_tn(x[...].reshape(s.ROWS, D), quad[pg_rows(owner * per + c), 0:FC])

    def down_part(owner, c):
        return dot_tn(hot[:, hid_cols(owner, c)], og[...])

    def pg_sum(owner, c):
        return jnp.sum(quad[pg_rows(owner * per + c), 0:FC].astype(F32), axis=0, keepdims=True)

    og_sum = jnp.sum(og[...].astype(F32), axis=0, keepdims=True)
    span = min(FL, D)

    def put_bias(ref):
        for b in range(D // span):
            ref[1 + b : 2 + b, 0:span] = og_sum[:, b * span : (b + 1) * span]

    for j in range(1, N):
        owner = lax.rem(h + j, N)
        for c in range(per):
            cols = slice(c * FC, (c + 1) * FC)
            us[j - 1, :, cols] = up_part(owner, c).astype(BF)
        n_copy(0, j).start()
        for c in range(per):
            cols = slice(c * FC, (c + 1) * FC)
            ds_[j - 1, cols, :] = down_part(owner, c).astype(BF)
        n_copy(1, j).start()
        for c in range(per):
            cols = slice(c * FC, (c + 1) * FC)
            bs[j - 1, 0:1, cols] = pg_sum(owner, c)
        put_bias(bs.at[j - 1])
        b_copy(j, h).start()
    def go_copy(i, c):
        cols = pl.ds(c * FC, FC)
        if i == 0:
            return pltpu.make_async_copy(stage.at[c, :, pl.ds(0, FC)], gu_out.at[:, cols], go_sem.at[c])
        return pltpu.make_async_copy(stage.at[c, pl.ds(0, FC), :], gd_out.at[cols, :], go_sem.at[c])

    for c in range(per):
        cols = slice(c * FC, (c + 1) * FC)
        total = up_part(h, c)
        for j in range(1, N):
            if c == 0:
                n_copy(0, j).wait_recv()
            total += ur[j - 1, :, cols].astype(F32)
        stage[c, :, 0:FC] = total.astype(BF)
        go_copy(0, c).start()
        gub_out[:, cols] = pg_sum(h, c)
    for c in range(per):
        cols = slice(c * FC, (c + 1) * FC)
        total = down_part(h, c)
        for j in range(1, N):
            if c == 0:
                n_copy(1, j).wait_recv()
            total += dr[j - 1, cols, :].astype(F32)
        go_copy(0, c).wait()
        stage[c, 0:FC, :] = total.astype(BF)
        go_copy(1, c).start()
    put_bias(br.at[h])

    for n in range(DEPTH):
        z_go(n)

    @pl.loop(0, s.NCH)
    def _(c):
        rows = pl.ds(align(h * TL + c * CH, 16), CH)
        hit = jnp.logical_or(pcol[rows, 0:1] == svals[...], pcol[rows, 1:2] == svals[...])
        hot[pl.ds(align(c * CH, 16), CH), 0 : E * Rb] = jnp.where(hit, 1.0, 0.0).astype(BF)

    def pass_on(buffer, send, recv, i, j, src=None):
        part = buffer.at[h if src is None else src, i]
        return remote(part, part, send.at[i, j], recv.at[i, j], w, lax.rem(h + j, N) if src is None else src)

    @pl.loop(0, s.NR)
    def _(c):
        for k in range(2):
            i = send_pair(c) * 2 + k
            swap_r.wait_recv(i)
            for j in range(1, N):
                pass_on(rg_all, rf_send, rf_recv, i, j).start()


    for j in range(1, N):
        src = lax.rem(h + N - j, N)
        b_copy(j, src).wait_recv()
        gub_out[...] += br[src, 0:1, :]
    for b in range(D // span):
        gdb_out[:, b * span : (b + 1) * span] = sum(br[j, 1 + b : 2 + b, 0:span] for j in range(N))

    @pl.loop(0, s.PW)
    def _(i):
        for j in range(1, N):
            pass_on(rg_all, rf_send, rf_recv, i, j, lax.rem(h + N - j, N)).wait_recv()

    small[...] = jnp.zeros(small.shape, F32)
    small[0:E, :] = grt[...]

    def add_row(r, value):
        small[r : r + 1, :] += jnp.sum(value, axis=0, keepdims=True)

    load_ags.wait()

    @pl.loop(0, s.PW)
    def _(i):
        swap_x.wait_send(i)

    @pl.loop(0, s.NCH)
    def _(c):
        rows = pl.ds(align(c * CH, 16), CH)
        z_go(c + DEPTH)
        moe_grad = dot(hot[rows, 0 : E * Rb], rg_all[...].reshape(E * Rb, D))
        normed, inv = norm_parts(ress[rows, :])
        add_row(E + 2, moe_grad * normed)
        add_row(E + 3, moe_grad)
        total = ags[rows, :].astype(F32) + norm_pull(moe_grad, normed, inv, g2[...])
        rgrad[rows, :] = total
        ag = total.astype(BF)
        ags[rows, :] = ag
        add_row(E + 4, ag.astype(F32))
        snd_x[rows, :] = dot_nt(ag, wp[...].reshape(D, D)).astype(BF)

    def attend_back(part, start, stop):
        heads = range(part, HP, s.halves)

        @pl.loop(start, stop)
        def _(c):
            units = [u for m in range(s.IMG) for u in image_units(c, m, heads)]
            inputs = [
                (split_heads(snd_x[im, cols]), qs[im, cols], ks[im, cols], vs[im, cols], ps[u])
                for im, cols, u in units
            ]
            pgrads = [dot_nt(v, both) for both, _q, _k, v, _p in inputs]
            vgrads = [dot(low, both) for both, _q, _k, _v, low in inputs]
            sgrads = []
            for pgrad, (_b, _q, _k, _v, low) in zip(pgrads, inputs):
                probs = low.astype(F32)
                sgrads.append((probs * (pgrad - jnp.sum(pgrad * probs, axis=0, keepdims=True))).astype(BF))
            qgrads = [dot_tn(sg, one[2]) for sg, one in zip(sgrads, inputs)]
            kgrads = [dot(sg, split_heads(one[1])) for sg, one in zip(sgrads, inputs)]
            for (im, cols, _u), qg, kg, vg in zip(units, qgrads, kgrads, vgrads):
                qs[im, cols] = join_heads(qg * (HEAD_DIM ** (-0.5))).astype(BF)
                ks[im, cols] = kg.astype(BF)
                vs[im, cols] = vg.astype(BF)

    class Job:
        def __init__(self, n):
            self.n, self.rows = n, s.jobs[n]
            self.gsend, self.gnar, self.gown, self.rbuf, self.gfin = job_refs[n]
            self.sbuf = self.gsend.at[0]

        def n_copy(self, rel, narrow_place):
            return remote(
                self.gsend.at[rel], self.gnar.at[rel], n_send.at[self.n, rel], n_recv.at[self.n, rel], w, narrow_place
            )

        def begin(self):
            LW = s.LW
            if self.n == 0:
                lower = dot_tn(atts[...], ags[...])
            else:
                first_cols = [j * L + (self.n - 1) * LW for j in range(N)]
                right = jnp.concatenate([dd[:, a : a + LW] for dd in (qs, ks, vs) for a in first_cols], axis=1)
                upper = dot_tn(ains[...], right)
            for j in range(N):
                if self.n == 0:
                    parts = [(b * L, lower[j * L : (j + 1) * L, b * LW : (b + 1) * LW]) for b in range(D // LW)]
                else:
                    parts = [(i * D, upper[:, (i * N + j) * LW : (i * N + j + 1) * LW]) for i in range(3)]

                def put(ref, cast, parts=parts):
                    for r, value in parts:
                        ref[r : r + value.shape[0], :] = value.astype(cast)

                @pl.when(h == j)
                def _():
                    put(self.gown, F32)

                @pl.when(h != j)
                def _():
                    rel = lax.rem(j - h + N, N) - 1
                    put(self.gsend.at[rel], BF)
                    self.n_copy(rel, j).start()

        def join(self):
            for j in range(1, N):
                self.n_copy(j - 1, lax.rem(h + N - j, N)).wait_recv()
                self.gown[...] += self.gnar[j - 1].astype(F32)
            for j in range(1, N):
                self.n_copy(j - 1, lax.rem(h + j, N)).wait_send()

        def part(self, f, place_in_team):
            size = self.rows // s.near
            if f == 0:
                return pl.ds(align(place_in_team * size, 16), size)
            piece = size // s.teams[1]
            return pl.ds(align(spot[0] * size + place_in_team * piece, 16), piece)

        def others(self, f):
            return [lax.rem(spot[f] + r, s.teams[f]) for r in range(1, s.teams[f])]

        def fold(self, f, other, land):
            return remote(
                self.sbuf.at[self.part(f, other)], self.rbuf.at[self.part(f, land)],
                h_send.at[self.n, f, other], h_recv.at[self.n, f, land], mate(f, other), h,
            )

        def grow(self, f, other, land):
            return remote(
                self.gfin.at[self.part(f, spot[f])], self.gfin.at[self.part(f, land)],
                a_send.at[self.n, f, other], a_recv.at[self.n, f, land], mate(f, other), h,
            )

        def start(self, q):
            f = min(q, 3 - q)
            for other in self.others(f):
                if q < 2:
                    rows = self.part(f, other)
                    self.sbuf[rows, :] = self.gown[rows, :].astype(BF)
                    self.fold(f, other, spot[f]).start()
                else:
                    self.grow(f, other, spot[f]).start()

        def end(self, q):
            f = min(q, 3 - q)
            own = self.part(f, spot[f])
            if q < 2:
                total = self.gown[own, :]
                for other in self.others(f):
                    self.fold(f, other, other).wait()
                    total += self.rbuf[self.part(f, other), :].astype(F32)
                if q == 0:
                    self.gown[own, :] = total
                else:
                    self.gfin[own, :] = total.astype(BF)
            else:
                for other in self.others(f):
                    self.grow(f, other, other).wait()

        def turn(self, q):
            self.end(q)
            if q < 3:
                self.start(q + 1)

        def finish(self):
            return pltpu.make_async_copy(self.gfin, gbigs[self.n], fin_sem.at[self.n])

    def s_copy(f, other, land):
        return remote(
            sacc.at[f], srec.at[f, land], s_send.at[f, other], s_recv.at[f, land], mate(f, other), h
        )

    def s_others(f):
        return [lax.rem(spot[f] + r, s.teams[f]) for r in range(1, s.teams[f])]

    def s_start(f):
        srec[f, spot[f]] = sacc[f]
        for other in s_others(f):
            s_copy(f, other, spot[f]).start()

    def s_end(f):
        for other in s_others(f):
            s_copy(f, other, other).wait()
        return sum(srec[f, i] for i in range(s.teams[f]))

    def tok_copy(src, dst, send, recv, c, j):
        here = pl.ds(align(c * CH, 16), CH)
        there = pl.ds(align(h * TL + c * CH, 16), CH)
        return remote(src.at[here], dst.at[there], send.at[c, j], recv.at[c, j], w, lax.rem(h + j, N))

    def tok_local(src, dst, sem, c):
        here = pl.ds(align(c * CH, 16), CH)
        there = pl.ds(align(h * TL + c * CH, 16), CH)
        return pltpu.make_async_copy(src.at[here], dst.at[there], sem.at[c])

    def bias_sums():
        small[E + 5 : E + 6, :] = jnp.sum(qs[...].astype(F32), axis=0, keepdims=True)
        small[E + 6 : E + 7, :] = jnp.sum(vs[...].astype(F32), axis=0, keepdims=True)

    def first_norm_part(start, stop):
        @pl.loop(start, stop)
        def _(c):
            rows = pl.ds(align(c * CH, 16), CH)
            back = jnp.zeros((CH, D), F32)
            for j in range(N):
                cols = slice(j * L, (j + 1) * L)
                for i, dd in enumerate((qs, ks, vs)):
                    back += dot_nt(dd[rows, cols], wq[j, i])
            normed, inv = norm_parts(tokv[rows, :].astype(F32))
            add_row(E, back * normed)
            add_row(E + 1, back)
            ags[rows, :] = (rgrad[rows, :] + norm_pull(back, normed, inv, g1[...])).astype(BF)
            for j in range(1, N):
                tok_copy(ags, gtok, g_send, g_recv, c, j).start()
            tok_local(ags, gtok, g_loc, c).start()

    def small_send():
        for b in range(D // 128):
            snar[h, b * s.RP : (b + 1) * s.RP, :] = small[:, b * 128 : (b + 1) * 128]
        for j in range(1, N):
            remote(snar.at[h], snar.at[h], sn_send.at[j], sn_recv.at[j], w, lax.rem(h + j, N)).start()

    def combine_pass():
        for n in range(z_next + 1, s.ZP):
            z_go(n)

        @pl.loop(0, s.NR // 2)
        def _(c):
            for k in range(4):
                i = send_pair(2 * c + 1 - k // 2) * 2 + k % 2
                if k < 2:
                    swap_z.wait_recv(i)
                else:
                    z_landed(i)
                for j in range(1, N):
                    pass_on(zall, zf_send, zf_recv, i, j).start()

    def combine_wait():
        @pl.loop(0, s.PW)
        def _(i):
            for j in range(1, N):
                pass_on(zall, zf_send, zf_recv, i, j, lax.rem(h + N - j, N)).wait_recv()

    def combine(start, stop):
        @pl.loop(start, stop)
        def _(c):
            rows = pl.ds(align(c * CH, 16), CH)
            mixed = dot(hot[rows, 0 : E * Rb], zall[...].reshape(E * Rb, D))
            ains[rows, :] = (ress[rows, :] + mixed).astype(BF)
            for j in range(1, N):
                tok_copy(ains, out, o_send, o_recv, c, j).start()
            tok_local(ains, out, o_loc, c).start()

    def small_narrow():
        for j in range(1, N):
            src = lax.rem(h + N - j, N)
            remote(snar.at[h], snar.at[h], sn_send.at[j], sn_recv.at[j], w, src).wait_send()
            remote(snar.at[src], snar.at[src], sn_send.at[j], sn_recv.at[j], w, src).wait_recv()
        sacc[0] = sum(snar[j] for j in range(N))

    jobs = [Job(n) for n in range(NJ)]
    steps = 4
    middle = s.NCH // 2
    z_next = DEPTH + s.NCH
    jobs[0].begin()
    attend_back(0, 0, middle)
    jobs[0].join()
    jobs[0].start(0)
    attend_back(0, middle, s.NCH)
    z_go(z_next)
    jobs[1].begin()
    at = [0] * NJ
    if NJ == 3:
        jobs[0].turn(0)
        attend_back(1, 0, middle)
        z_next += 1
        z_go(z_next)
        jobs[1].join()
        jobs[1].start(0)
        attend_back(1, middle, s.NCH)
        z_next += 1
        z_go(z_next)
        jobs[0].turn(1)
        jobs[2].begin()
        jobs[1].turn(0)
        jobs[2].join()
        jobs[2].start(0)
        at = [2, 1, 0]
    else:
        jobs[1].join()
        jobs[1].start(0)
    turn = 0
    while min(at) < steps:
        z_next += 1
        z_go(z_next)
        if turn == 0:
            bias_sums()
        if turn < LN_TURNS:
            first_norm_part(turn * s.NCH // LN_TURNS, (turn + 1) * s.NCH // LN_TURNS)
        if turn == LN_TURNS - 1:
            small_send()
        if turn == LN_TURNS:
            small_narrow()
            s_start(0)
        if turn == LN_TURNS + 1:
            sacc[1] = s_end(0)
            s_start(1)
        if turn == MIX_TURN:
            combine_pass()
        if turn == MIX_TURN + 1:
            combine_wait()
            combine(0, s.NCH)
        for n in range(NJ):
            if at[n] < steps:
                jobs[n].turn(at[n])
                at[n] += 1
                if at[n] == steps:
                    jobs[n].finish().start()
        turn += 1
    gsmall[...] = s_end(1)

    for j in range(1, N):
        for i in range(2):
            n_copy(i, j).wait_send()
        b_copy(j, h).wait_send()

    @pl.loop(0, s.PW)
    def _(i):
        swap_r.wait_send(i)
        for j in range(1, N):
            pass_on(rg_all, rf_send, rf_recv, i, j).wait_send()
            pass_on(zall, zf_send, zf_recv, i, j).wait_send()

    @pl.loop(0, s.NCH)
    def _(c):
        tok_local(ags, gtok, g_loc, c).wait()
        tok_local(ains, out, o_loc, c).wait()
        here = pl.ds(align(c * CH, 16), CH)
        for j in range(1, N):
            src = lax.rem(h + N - j, N)
            there = pl.ds(align(src * TL + c * CH, 16), CH)
            tok_copy(ags, gtok, g_send, g_recv, c, j).wait_send()
            tok_copy(ains, out, o_send, o_recv, c, j).wait_send()
            remote(ags.at[here], gtok.at[there], g_send.at[c, j], g_recv.at[c, j], w, src).wait_recv()
            remote(ains.at[here], out.at[there], o_send.at[c, j], o_recv.at[c, j], w, src).wait_recv()

    for c in range(per):
        go_copy(1, c).wait()
    @pl.loop(0, s.NR // 2)
    def _(c):
        for k in range(2):
            swap_z.wait_send(send_pair(2 * c + 1) * 2 + k)

    for n in range(max(0, s.ZP - DEPTH), s.ZP):
        z_piece(n).wait_send()
    for job in jobs:
        job.finish().wait()


def post_kernel(s, *refs):
    (
        out_in, gtok_in, gu_in, gd_in, flat, gub_in, gdb_in, *rest,
    ) = refs
    bigs, rest = rest[: len(s.jobs)], rest[len(s.jobs) :]
    (
        out, gtok, gu, gd, gqkv, gproj, gag, gas, gmg, gms, gpb, gqv, grouter, gub, gdb,
        b_out, b_tok, b_gu, b_gd, f_tok, f_gu, f_gd, l_sem, s_sem,
    ) = rest
    moves = (
        (gtok_in, b_tok, f_tok, gtok), (gu_in, b_gu, f_gu, gu), (gd_in, b_gd, f_gd, gd), (out_in, b_out, b_out, out),
    )
    loads, stores, widen = [], [], []
    for i, (a, b, f, c) in enumerate(moves):
        step = a.shape[0] // PARTS
        for p in range(PARTS):
            part = pl.ds(p * step, step)
            loads.append(pltpu.make_async_copy(a.at[part], b.at[part], l_sem.at[i, p]))
            stores.append(pltpu.make_async_copy(f.at[part], c.at[part], s_sem.at[i, p]))
            widen.append((b, f, slice(p * step, (p + 1) * step)))
    for load in loads:
        load.start()
    D, L, N, E, LW = s.D, s.L, s.N, s.E, s.LW
    h = lax.axis_index("narrow")
    for load, store, (b, f, part) in zip(loads, stores, widen):
        load.wait()
        if b is not f:
            f[part, :] = b[part, :].astype(F32)
        store.start()
    for n, big in enumerate(bigs[1:]):
        for i in range(3):
            gqkv[i, :, n * LW : (n + 1) * LW] = big[i * D : (i + 1) * D, :].astype(F32)
    for b in range(D // LW):
        gproj[:, b * LW : (b + 1) * LW] = bigs[0][b * L : (b + 1) * L, :].astype(F32)

    def rows(r, count):
        return jnp.concatenate([flat[b * s.RP + r : b * s.RP + r + count, :] for b in range(D // 128)], axis=1)

    gub[...] = gub_in[...]
    gdb[...] = gdb_in[...]
    grouter[...] = rows(0, E)
    for r, ref in ((E, gag), (E + 1, gas), (E + 2, gmg), (E + 3, gms), (E + 4, gpb)):
        ref[...] = rows(r, 1)
    qv = rows(E + 5, 2)
    for j in range(N):

        @pl.when(h == j)
        def _():
            gqv[...] = qv[:, j * L : (j + 1) * L]

    for store in stores:
        store.wait()


VM = pl.BlockSpec(memory_space=pltpu.VMEM)
ANY = pl.BlockSpec(memory_space=pl.ANY)
HB = pl.BlockSpec(memory_space=pltpu.HBM)
DMA = pltpu.SemaphoreType.DMA
V = pltpu.VMEM


def shards(
    wide,
    narrow,
    tokens,
    attn_gain,
    attn_shift,
    qkv_weight,
    query_value_bias,
    proj_weight,
    proj_bias,
    moe_gain,
    moe_shift,
    router_weight,
    expert_up,
    expert_up_bias,
    expert_down,
    expert_down_bias,
    routes,
    slot_index,
    cotangent,
):
    s = Sizes(wide, narrow, tokens.shape[0], tokens.shape[1], router_weight.shape[1], expert_up.shape[2])
    T, D, E, N, W, L, TL = s.T, s.D, s.E, s.N, s.W, s.L, s.TL
    PW, Rb, FL, ROWS, RC, NCH = s.PW, s.Rb, s.FL, s.ROWS, s.RC, s.NCH
    slot = np.arange(E * Rb)
    half, rest = slot // (PW * Rb), slot % (PW * Rb)
    pos, inner = rest // Rb, rest % Rb
    svals = np.where(inner < s.cap, (pos * N + half) * s.cap + inner, -2).astype(np.int32)[None, :]
    row = lambda a: a.reshape(1, -1)
    blk = (PW, Rb, D)
    heads = (TL // PATCHES) * s.HP
    TM = max(s.teams)
    ins = [
        (ANY, tokens), (ANY, cotangent), (VM, row(attn_gain)), (VM, row(attn_shift)),
        (ANY, qkv_weight.transpose(1, 0, 2)), (ANY, query_value_bias), (ANY, proj_weight), (VM, row(proj_bias)),
        (VM, row(moe_gain)), (VM, row(moe_shift)), (VM, router_weight.T), (ANY, expert_up[0]),
        (ANY, expert_up_bias), (ANY, expert_down[0]), (VM, expert_down_bias), (VM, routes.T), (VM, slot_index.T),
        (VM, jnp.asarray(svals)),
    ]
    outs = [
        (ANY, (T, D), BF), (ANY, (T, D), BF), (VM, (s.RPS, 128), F32),
        (ANY, (D, FL), BF), (ANY, (FL, D), BF), (VM, (1, FL), F32), (VM, (1, D), F32),
    ] + [(ANY, (r, s.LW), BF) for r in s.jobs]
    scratch = [
        V((TL, D), BF), V((N, 3, D, L), BF), V((N, L, D), BF), V((N, 2, L), F32), V((T, 8), jnp.int32),
        V((ROWS, max(T, E * Rb)), BF), V((2 * T, D), BF), V((TL, D), BF), V((TL, D), BF), V((TL, D), BF),
        V((heads, PATCHES, 2 * PATCHES), BF), V((TL, D), BF), V((TL, D), BF), V((TL, D), F32), V((ROWS, D), BF), V((ROWS, D), BF),
        V(blk, BF), V(blk, BF), V((N, D, FL), BF), V((N, FL, D), BF), V((N, 1, FL), F32), V((ROWS, D), BF),
        V((RC, D), F32), V((RC, D), F32), V((N - 1, D, FL), BF), V((N - 1, FL, D), BF), V((N - 1, D, FL), BF),
        V((N - 1, FL, D), BF), V((N - 1, 8, FL), F32), V((N, 8, FL), F32), V((FL // s.FC, D, D), BF),
        V((E, D), F32),
        V((N,) + blk, BF), V((N,) + blk, BF), V((TL, D), BF), V((TL, D), F32),
        V((s.RP, D), F32), V((N, s.RPS, 128), F32), V((2, s.RPS, 128), F32),
        V((2, max(s.teams), s.RPS, 128), F32),
    ]
    for r in s.jobs:
        scratch += [V((N - 1, r, s.LW), BF), V((N - 1, r, s.LW), BF), V((r, s.LW), F32)]
        scratch += [V((r, s.LW), BF), V((r, s.LW), BF)]
    NJ = len(s.jobs)
    scratch += [
        DMA((2,)), DMA((6,)), DMA((6, N)), DMA((6, N)), DMA((NCH, N)), DMA((NCH, N)),
        DMA((PW,)), DMA((PW,)), DMA((PW,)), DMA((PW,)), DMA((PW,)), DMA((PW,)),
        DMA((PW,)), DMA((PW,)), DMA((s.ZP,)), DMA((PW * s.PC,)), DMA((4,)), DMA((PW, N)), DMA((PW, N)), DMA((PW, N)), DMA((PW, N)),
        DMA((3, N)), DMA((3, N)), DMA((FL // s.FC,)),
        DMA((NJ, N)), DMA((NJ, N)), DMA((N,)), DMA((N,)), DMA((NJ, 2, TM)), DMA((NJ, 2, TM)),
        DMA((NJ, 2, TM)), DMA((NJ, 2, TM)), DMA((2, TM)), DMA((2, TM)),
        DMA((NCH, N)), DMA((NCH, N)), DMA((NCH, N)), DMA((NCH, N)), DMA((NCH,)), DMA((NCH,)), DMA((NJ,)),
    ]
    out, gtok, gsmall, gu, gd, gub, gdb, *gbigs = pl.pallas_call(
        functools.partial(block_kernel, s),
        in_specs=[spec for spec, _ in ins],
        out_specs=[spec for spec, _, _ in outs],
        out_shape=[jax.ShapeDtypeStruct(shape, dtype) for _, shape, dtype in outs],
        scratch_shapes=scratch,
        compiler_params=pltpu.CompilerParams(
            collective_id=1, has_side_effects=True, vmem_limit_bytes=VMEM_MB << 20
        ),
        name="block",
    )(*[a for _, a in ins])

    post_ins = [(HB, out), (HB, gtok), (HB, gu), (HB, gd), (VM, gsmall), (VM, gub), (VM, gdb)]
    post_ins += [(VM, a) for a in gbigs]
    post_outs = [
        (ANY, (T, D), BF), (ANY, (T, D), F32), (ANY, (D, FL), F32), (ANY, (FL, D), F32), (VM, (3, D, L), F32),
        (VM, (L, D), F32), (VM, (1, D), F32), (VM, (1, D), F32), (VM, (1, D), F32), (VM, (1, D), F32),
        (VM, (1, D), F32), (VM, (2, L), F32), (VM, (E, D), F32), (VM, (1, FL), F32), (VM, (1, D), F32),
    ]
    out, gtok, gu, gd, gqkv, gproj, gag, gas, gmg, gms, gpb, gqv, grouter, gub, gdb = pl.pallas_call(
        functools.partial(post_kernel, s),
        in_specs=[spec for spec, _ in post_ins],
        out_specs=[spec for spec, _, _ in post_outs],
        out_shape=[jax.ShapeDtypeStruct(shape, dtype) for _, shape, dtype in post_outs],
        scratch_shapes=[
            V((T, D), BF), V((T, D), BF), V((D, FL), BF), V((FL, D), BF), V((T, D), F32), V((D, FL), F32),
            V((FL, D), F32), DMA((4, PARTS)), DMA((4, PARTS)),
        ],
        compiler_params=pltpu.CompilerParams(vmem_limit_bytes=VMEM_MB << 20),
        name="post",
    )(*[a for _, a in post_ins])
    return (
        out,
        gtok,
        gag.reshape(D),
        gas.reshape(D),
        gqkv.transpose(1, 0, 2),
        gqv,
        gproj,
        gpb.reshape(D),
        gmg.reshape(D),
        gms.reshape(D),
        grouter.T,
        gu[None],
        gub,
        gd[None],
        gdb,
    )


def solution(mesh):
    in_specs = (
        P("wide", None),
        P(),
        P(),
        P(None, None, "narrow"),
        P(None, "narrow"),
        P("narrow", None),
        P(),
        P(),
        P(),
        P(),
        P("wide", None, "narrow"),
        P("wide", "narrow"),
        P("wide", "narrow", None),
        P("wide", None),
        P("wide", None),
        P("wide", None),
        P("wide", None),
    )
    out_specs = (
        P("wide", None),
        P("wide", None),
        P(),
        P(),
        P(None, None, "narrow"),
        P(None, "narrow"),
        P("narrow", None),
        P(),
        P(),
        P(),
        P(),
        P("wide", None, "narrow"),
        P("wide", "narrow"),
        P("wide", "narrow", None),
        P("wide", None),
    )
    body = functools.partial(shards, mesh.shape["wide"], mesh.shape["narrow"])
    return jax.shard_map(body, mesh=mesh, in_specs=in_specs, out_specs=out_specs, check_vma=False)
```
